256 devices in a mesh: row: 16 (over x, y_hi, core), col: 16 (over z, y_lo).
Axes of the slice: x: 4, y: 4 (y_hi: 2, y_lo: 2; y = y_hi * 2 + y_lo), z: 8, core: 2. Of those that a mesh axis runs over, the one named last changes fastest.
Arguments:
- positions: float32 [3, 16384], P(None, ('row', 'col')), may hold values from -0.2 to 63.2, as said below
- radii: float32 [16384], P(('row', 'col')), may hold values from 0.1 to 0.28
- basis: float32 [32, 3, 16384], P(None, None, ('row', 'col')), may hold values from -0.0112763724 to 0.0112763724, as said below
- rhs: float32 [3, 16384], P(None, ('row', 'col')), may hold values from -6 to 6
Outputs:
- solution: float32 [3, 16384], P(None, ('row', 'col'))
- residual: float32 [3, 16384], P(None, ('row', 'col'))
The draws below stay inside these ranges and needn't reach their ends.
Inputs may be any that keep to these rules, and one draw needn't show every extreme that they name: `positions`: every coordinate lies within 0.2 of a whole number and any two centres are 0.6 or more apart, more than the sum of any two radii. `basis`: the 32 vectors are linearly independent.
All inputs are finite; a program needn't handle non-finite values.
Results may differ from the reference program's by a relative error of at most 0.0003.
Values sent between devices are 32-bit elements; how exact they have to be, the bound alone decides.
A program may use at most 64 MiB of HBM per device.

```python
import math
import jax
import jax.numpy as jnp
from jax import lax

SPHERES_DEV = 64
BASIS = 32
ITERS = 2
TARGETS = 1024
SOURCES = 1024
SPHERES = 16384
ORDER = 49152


def lattice_points():
    sphere_index = jnp.arange(SPHERES, dtype=jnp.int32)
    piece = sphere_index // SPHERES_DEV
    columns = SOURCES // SPHERES_DEV
    coords = jnp.stack([piece // columns, piece % columns, sphere_index % SPHERES_DEV])
    return coords.astype(jnp.float32)


def lattice_extent():
    return jnp.array([TARGETS // SPHERES_DEV, SOURCES // SPHERES_DEV, SPHERES_DEV], jnp.float32)[:, None]


def draw_positions(key, part):
    points = lattice_points()
    jitter = jax.random.uniform(key, (3, SPHERES), jnp.float32, -0.2, 0.2)
    return points + jitter


def draw_basis(key, part):
    streams = jax.random.split(jax.random.fold_in(key, 11), 3)
    scaled_points = lattice_points() / lattice_extent()
    freqs = jax.random.randint(streams[0], (BASIS, 3, 3), 0, 3).astype(jnp.float32)
    phase = jax.random.uniform(streams[1], (BASIS, 3, 1), jnp.float32, 0.0, 2.0 * math.pi)
    wave = jnp.cos(2.0 * math.pi * jnp.einsum('kcd,dp->kcp', freqs, scaled_points) + phase)
    rough = jax.random.normal(streams[2], (BASIS, 3, SPHERES), jnp.float32)
    return jnp.clip(wave + 0.5 * rough, -2.5, 2.5) / math.sqrt(ORDER)


def draw_rhs(key, part):
    streams = jax.random.split(jax.random.fold_in(key, 23), 3)
    scaled_points = lattice_points() / lattice_extent()
    order_float = jnp.arange(SPHERES, dtype=jnp.int32).astype(jnp.float32)
    rising = jnp.exp(math.log(3.0) * order_float / SPHERES)
    phase = jax.random.uniform(streams[0], (3, 1), jnp.float32, 0.0, 2.0 * math.pi)
    freqs = jax.random.randint(streams[1], (3, 3), 1, 3).astype(jnp.float32)
    wave = jnp.cos(2.0 * math.pi * jnp.einsum('cd,dp->cp', freqs, scaled_points) + phase)
    rough = jnp.clip(jax.random.normal(streams[2], (3, SPHERES), jnp.float32), -4.0, 4.0)
    value = 0.5 * rising * (rough + wave)
    return jnp.clip(value, -6.0, 6.0)


def steps_of(rng, shape, cuts, low, top_value):
    def one(axis_at, parts):
        heights = jax.random.uniform(jax.random.fold_in(jax.random.fold_in(rng, 6), axis_at), (parts,), jnp.float32, low / len(cuts), top_value / len(cuts))
        return jnp.repeat(jnp.exp(heights), shape[axis_at] // parts).reshape((-1,) + (1,) * (len(shape) - axis_at - 1))

    level = one(*cuts[0])
    for cut in cuts[1:]:
        level = level * one(*cut)
    return level


def setup_inputs(seed: int = 0) -> dict:
    streams_of = jax.random.split(jax.random.key(seed), 5)
    return {
        "positions": draw_positions(jax.random.fold_in(streams_of[4], 71), 0),
        "radii": jnp.clip(jnp.exp(math.log(0.28) - 1.0296194 * jax.random.uniform(streams_of[1], (SPHERES,), jnp.float32) ** steps_of(streams_of[1], (SPHERES,), ((0, 256),), -0.2, 0.2)), 0.1, 0.28),
        "basis": draw_basis(jax.random.fold_in(streams_of[4], 71), 0),
        "rhs": draw_rhs(jax.random.fold_in(streams_of[4], 71), 0),
    }


far_scale = 1.0 / (8.0 * math.pi)
self_scale = 1.0 / (6.0 * math.pi)
highest = lax.Precision.HIGHEST

def contract(left, right):
    return lax.dot_general(left.astype(jnp.float32), right.astype(jnp.float32), (((1,), (1,)), ((), ())), precision=highest, preferred_element_type=jnp.float32)

def block_apply(out_pos, out_rad, out_index, in_pos, in_rad, in_index, fields):
    deltas = [out_pos[axis_id][:, None] - in_pos[axis_id][None, :] for axis_id in range(3)]
    coincide = out_index[:, None] == in_index[None, :]
    dist_sq = deltas[0] * deltas[0] + deltas[1] * deltas[1] + deltas[2] * deltas[2]
    safe_sq = jnp.where(coincide, jnp.ones_like(dist_sq), dist_sq)
    inv_sq = 1.0 / safe_sq
    inv_dist = jnp.sqrt(inv_sq)
    radius_sum = (out_rad * out_rad)[:, None] + (in_rad * in_rad)[None, :]
    scaled = far_scale * inv_dist
    isotropic = scaled * (1.0 + radius_sum * inv_sq / 3.0)
    own_term = jnp.broadcast_to((self_scale / out_rad)[:, None], isotropic.shape)
    isotropic = jnp.where(coincide, own_term, isotropic)
    along = jnp.where(coincide, jnp.zeros_like(dist_sq), scaled * (1.0 - radius_sum * inv_sq) * inv_sq)
    tensors = {}
    for first in range(3):
        for second in range(first, 3):
            entry = along * deltas[first] * deltas[second]
            if first == second:
                entry = entry + isotropic
            tensors[first, second] = entry
    results = []
    for first in range(3):
        total = None
        for second in range(3):
            term = contract(fields[:, second, :], tensors[min(first, second), max(first, second)])
            total = term if total is None else total + term
        results.append(total)
    return jnp.stack(results, axis=1)

def field_apply(out_pos, out_rad, out_index, in_pos, in_rad, in_index, fields, width):
    count = out_rad.shape[0] // width
    pos_blocks = out_pos.reshape(3, count, width).transpose(1, 0, 2)
    rad_blocks = out_rad.reshape(count, width)
    index_blocks = out_index.reshape(count, width)

    def one_block(packed):
        return block_apply(packed[0], packed[1], packed[2], in_pos, in_rad, in_index, fields)
    stacked = lax.map(one_block, (pos_blocks, rad_blocks, index_blocks))
    return stacked.transpose(1, 2, 0, 3).reshape(fields.shape[0], 3, count * width)

def reference(positions, radii, basis, rhs):
    sphere_index = jnp.arange(SPHERES, dtype=jnp.int32)

    def mobility(fields):
        return field_apply(positions, radii, sphere_index, positions, radii, sphere_index, fields, SPHERES_DEV)
    basis_image = mobility(basis)
    gram = jnp.einsum('kcp,lcp->kl', basis, basis_image, precision=highest)
    load = jnp.einsum('kcp,cp->k', basis, rhs, precision=highest)
    factor = jnp.linalg.cholesky(gram)

    def coarse_solve(vector):
        return jax.scipy.linalg.cho_solve((factor, True), vector)
    coarse = coarse_solve(load)
    solution = jnp.einsum('k,kcp->cp', coarse, basis, precision=highest)
    residual = rhs - jnp.einsum('k,kcp->cp', coarse, basis_image, precision=highest)
    norm_now = jnp.sum(residual * residual)
    projection = coarse_solve(jnp.einsum('kcp,cp->k', basis_image, residual, precision=highest))
    direction = residual - jnp.einsum('k,kcp->cp', projection, basis, precision=highest)
    for iteration in range(ITERS):
        image = mobility(direction[None])[0]
        step_size = norm_now / jnp.sum(direction * image)
        solution = solution + step_size * direction
        residual = residual - step_size * image
        if iteration + 1 < ITERS:
            norm_next = jnp.sum(residual * residual)
            projection = coarse_solve(jnp.einsum('kcp,cp->k', basis_image, residual, precision=highest))
            direction = residual + norm_next / norm_now * direction - jnp.einsum('k,kcp->cp', projection, basis, precision=highest)
            norm_now = norm_next
    return (solution, residual)
```

```python
import functools
import math

import jax
import jax.numpy as jnp
from jax import lax
from jax.experimental import pallas as pl
from jax.experimental.pallas import tpu as pltpu
from jax.sharding import PartitionSpec as P

MESH = pl.DeviceIdType.MESH
F32 = jnp.float32
BF16 = jnp.bfloat16

far_scale = 1.0 / (8.0 * math.pi)
self_scale = 1.0 / (6.0 * math.pi)

LANES = 128
HALF = 64
PAIRS = ((0, 0), (1, 1), (2, 2), (0, 1), (1, 2), (2, 0))
SLOT = {}
for _slot, (_a, _b) in enumerate(PAIRS):
    SLOT[_a, _b] = _slot
    SLOT[_b, _a] = _slot


def kernel(
    n, vectors,
    geo_ref, wp_ref,
    sol_ref, res_ref,
    grow, gcol, wcol, src_b, tgt, mob, fields, aw_send, aw_recv, aw,
    gram_a, gram_row, gram_b, gram_col,
    vec_a, vec_col_a, stat_a, stat_row_a, part_a, part_row_a, stat_b, stat_col_b,
    vec_c, vec_col_c, stat_c, stat_row_c, part_c, part_row_c, stat_d, stat_col_d,
    stat_e, stat_row_e, stat_f, stat_col_f,
    send_sems, recv_sems,
):
    r = lax.axis_index("row")
    c = lax.axis_index("col")
    kh = vectors // 2
    span = n * HALF
    tiles = span // LANES

    lane1 = lax.broadcasted_iota(jnp.int32, (1, LANES), 1)
    lane8 = lax.broadcasted_iota(jnp.int32, (8, LANES), 1)
    lane_k = lax.broadcasted_iota(jnp.int32, (kh, LANES), 1)
    row_k = lax.broadcasted_iota(jnp.int32, (kh, LANES), 0)
    low1, low8, low_k = lane1 < HALF, lane8 < HALF, lane_k < HALF

    def swap(x):
        return pltpu.roll(x, HALF, 1)

    def to_row(src, dst, tag):
        def one(step, carry):
            peer = lax.rem(r + step, n)
            pltpu.make_async_remote_copy(
                src_ref=src(peer), dst_ref=dst.at[r], send_sem=send_sems.at[tag],
                recv_sem=recv_sems.at[tag], device_id=(peer, c), device_id_type=MESH,
            ).start()
            return carry
        lax.fori_loop(1, n, one, 0)

    def to_col(src, dst, tag):
        def one(step, carry):
            peer = lax.rem(c + step, n)
            pltpu.make_async_remote_copy(
                src_ref=src, dst_ref=dst.at[c], send_sem=send_sems.at[tag],
                recv_sem=recv_sems.at[tag], device_id=(r, peer), device_id_type=MESH,
            ).start()
            return carry
        lax.fori_loop(1, n, one, 0)

    def arrived(dst, tag):
        all_but_one = dst.at[pl.ds(0, n - 1)]
        pltpu.make_async_copy(all_but_one, all_but_one, recv_sems.at[tag]).wait()

    def departed(dst, tag):
        all_but_one = dst.at[pl.ds(0, n - 1)]
        pltpu.make_async_copy(all_but_one, all_but_one, send_sems.at[tag]).wait()

    def total(ref):
        parts = [ref[i] for i in range(n)]
        while len(parts) > 1:
            parts = [parts[i] + parts[i + 1] for i in range(0, len(parts), 2)]
        return parts[0]

    barrier = pltpu.get_barrier_semaphore()

    def greet(step, carry):
        pl.semaphore_signal(barrier, inc=1, device_id=(lax.rem(r + step, n), c), device_id_type=MESH)
        pl.semaphore_signal(barrier, inc=1, device_id=(r, lax.rem(c + step, n)), device_id_type=MESH)
        return carry
    lax.fori_loop(1, n, greet, 0)
    pl.semaphore_wait(barrier, 2 * (n - 1))

    to_col(geo_ref, gcol, 0)
    to_row(lambda peer: geo_ref, grow, 1)
    to_col(wp_ref, wcol, 2)
    gcol[c] = geo_ref[...]
    grow[r] = geo_ref[...]
    wcol[c] = wp_ref[...]

    def spread(ref, count):
        for p in range(tiles):
            tile = jnp.where(low8, ref[2 * p], ref[2 * p + 1])
            turned = tile.T
            for axis in range(count):
                src_b[axis, pl.ds(p * LANES, LANES), :] = jnp.broadcast_to(
                    turned[:, axis:axis + 1], (LANES, LANES)
                )

    arrived(gcol, 0)
    spread(gcol, 4)
    arrived(grow, 1)
    for q in range(tiles):
        tgt[:, q * LANES:(q + 1) * LANES] = jnp.where(low8, grow[2 * q], grow[2 * q + 1])

    def form_tile(q, carry):
        lanes = pl.ds(pl.multiple_of(q * LANES, LANES), LANES)
        tx, ty, tz, t_rad = [
            jnp.broadcast_to(tgt[axis:axis + 1, lanes], (8, LANES)) for axis in range(4)
        ]
        t_rad_sq = t_rad * t_rad
        own = self_scale / t_rad
        t_rel = lane8 + (q * LANES - r * HALF)
        t_key = jnp.where(jnp.logical_and(t_rel >= 0, t_rel < HALF), t_rel, -span)
        s_rel0 = lax.broadcasted_iota(jnp.int32, (8, LANES), 0) - c * HALF

        def form_row(i, inner):
            rows = pl.ds(pl.multiple_of(i * 8, 8), 8)
            sx, sy, sz, s_rad = [src_b[axis, rows, :] for axis in range(4)]
            s_rel = s_rel0 + i * 8
            same = s_rel == t_key
            dx, dy, dz = tx - sx, ty - sy, tz - sz
            dist_sq = dx * dx + dy * dy + dz * dz
            inv = lax.rsqrt(jnp.where(same, 1.0, dist_sq))
            inv_sq = inv * inv
            ratio = (t_rad_sq + s_rad * s_rad) * inv_sq
            scaled = far_scale * inv
            iso = jnp.where(same, own, scaled + scaled * (ratio * (1.0 / 3.0)))
            along = (scaled - scaled * ratio) * inv_sq
            ax, ay, az = along * dx, along * dy, along * dz
            mob[0, rows, lanes] = ax * dx + iso
            mob[1, rows, lanes] = ay * dy + iso
            mob[2, rows, lanes] = az * dz + iso
            mob[3, rows, lanes] = ax * dy
            mob[4, rows, lanes] = ay * dz
            mob[5, rows, lanes] = az * dx
            return inner
        lax.fori_loop(0, span // 8, form_row, 0, unroll=4)
        return carry
    lax.fori_loop(0, tiles, form_tile, 0)

    arrived(wcol, 2)
    for p in range(tiles):
        cols = slice(p * LANES, (p + 1) * LANES)
        for axis in range(3):
            first = wcol[2 * p, kh * axis:kh * (axis + 1), :]
            second = wcol[2 * p + 1, kh * axis:kh * (axis + 1), :]
            block = jnp.concatenate(
                [jnp.where(low_k, first, swap(second)), jnp.where(low_k, swap(first), second)], axis=0
            )
            high = block.astype(BF16)
            rest = (block - high.astype(F32)).astype(BF16)
            for copy in (axis, axis + 3):
                if copy < 4:
                    base = 2 * vectors * copy
                    fields[base:base + vectors, cols] = high
                    fields[base + vectors:base + 2 * vectors, cols] = rest

    chunk = 4 * HALF
    depth = 256

    def basis_chunk(step, carry):
        which = lax.rem(lax.div(r, 4) + 1 + step, n // 4)
        lanes = pl.ds(pl.multiple_of(which * chunk, chunk), chunk)
        sums = [jnp.zeros((vectors, chunk), F32) for _ in range(3)]
        for slot, (a, b) in enumerate(PAIRS):
            first_row = 2 * vectors * a
            count = 2 * vectors if a == b else 4 * vectors
            acc_high = jnp.zeros((count, chunk), F32)
            acc_rest = jnp.zeros((count, chunk), F32)
            for d in range(span // depth):
                entry = mob[slot, d * depth:(d + 1) * depth, lanes]
                high = entry.astype(BF16)
                rest = (entry - high.astype(F32)).astype(BF16)
                lhs = fields[first_row:first_row + count, d * depth:(d + 1) * depth]
                acc_high = acc_high + jnp.dot(lhs, high, preferred_element_type=F32)
                acc_rest = acc_rest + jnp.dot(lhs, rest, preferred_element_type=F32)

            def gather(base):
                return (
                    acc_high[base:base + vectors] + acc_high[base + vectors:base + 2 * vectors]
                    + acc_rest[base:base + vectors]
                )
            if a == b:
                sums[a] = sums[a] + gather(0)
            else:
                sums[b] = sums[b] + gather(0)
                sums[a] = sums[a] + gather(2 * vectors)
        for part in range(2):
            for axis in range(3):
                piece = sums[axis][:, part * LANES:(part + 1) * LANES]
                lower, upper = piece[:kh], piece[kh:]
                slot_rows = slice(kh * axis, kh * (axis + 1))
                aw_send[4 * which + 2 * part, slot_rows, :] = jnp.where(low_k, lower, swap(upper))
                aw_send[4 * which + 2 * part + 1, slot_rows, :] = jnp.where(low_k, swap(lower), upper)
        for part in range(4):
            target = 4 * which + part

            @pl.when(target != r)
            def _():
                pltpu.make_async_remote_copy(
                    src_ref=aw_send.at[target], dst_ref=aw_recv.at[r], send_sem=send_sems.at[3],
                    recv_sem=recv_sems.at[3], device_id=(target, c), device_id_type=MESH,
                ).start()
        return carry
    lax.fori_loop(0, n // 4, basis_chunk, 0)
    aw_recv[r] = aw_send[r]
    arrived(aw_recv, 3)
    aw[...] = total(aw_recv)

    rhs = [geo_ref[4 + axis:5 + axis, :] for axis in range(3)]
    row32 = lax.broadcasted_iota(jnp.int32, (vectors, LANES), 0)
    lane32 = lax.broadcasted_iota(jnp.int32, (vectors, LANES), 1)

    def unpacked(ref, axis):
        block = ref[kh * axis:kh * (axis + 1), :]
        return jnp.where(lane32 < HALF, jnp.concatenate([block, swap(block)], axis=0), 0.0)

    gram = None
    load = None
    for axis in range(3):
        w_axis = unpacked(wp_ref, axis)
        term = lax.dot_general(
            w_axis, unpacked(aw, axis), (((1,), (1,)), ((), ())),
            precision=lax.Precision.HIGHEST, preferred_element_type=F32,
        )
        load_term = w_axis * rhs[axis]
        gram = term if gram is None else gram + term
        load = load_term if load is None else load + load_term
    load = jnp.sum(load, axis=1, keepdims=True)
    wide = jnp.concatenate([gram, jnp.zeros((vectors, LANES - vectors), F32)], axis=1)
    groups = vectors // 8
    packed = wide[0:8]
    load_tile = jnp.where(lane8 == 0, load[0:8], 0.0)
    for g in range(1, groups):
        packed = packed + pltpu.roll(wide[8 * g:8 * g + 8], vectors * g, 1)
        load_tile = load_tile + jnp.where(lane8 == vectors * g, load[8 * g:8 * g + 8], 0.0)
    gram_a[0:8, :] = packed
    gram_a[8:16, :] = load_tile
    to_row(lambda peer: gram_a, gram_row, 4)
    gram_row[r] = gram_a[...]
    arrived(gram_row, 4)
    gram_b[...] = total(gram_row)
    to_col(gram_b, gram_col, 5)
    gram_col[c] = gram_b[...]
    arrived(gram_col, 5)
    both = total(gram_col)
    packed, load_tile = both[0:8], both[8:16]
    pieces, load_pieces = [packed], [load_tile]
    for g in range(1, groups):
        pieces.append(pltpu.roll(packed, LANES - vectors * g, 1))
        load_pieces.append(pltpu.roll(load_tile, LANES - vectors * g, 1))
    gram = jnp.concatenate(pieces, axis=0)
    load = jnp.concatenate(load_pieces, axis=0)[:, 0:1]

    system = jnp.where(lane32 < vectors, gram, jnp.where(lane32 == row32 + vectors, 1.0, 0.0))
    system = jnp.where(lane32 == 2 * vectors, load, system)
    for j in range(vectors):
        pivot_row = system[j:j + 1, :]
        scaled_row = pivot_row / pivot_row[:, j:j + 1]
        column = system[:, j:j + 1]
        system = jnp.where(row32 == j, scaled_row, system - column * scaled_row)
    inverse = jnp.where(jnp.logical_and(lane32 >= vectors, lane32 < 2 * vectors), system, 0.0)
    coarse = system[:, 2 * vectors:2 * vectors + 1]

    def weights_of(column):
        return jnp.where(low_k, column[:kh], column[kh:])

    def combine(ref, weights):
        out = []
        for axis in range(3):
            s = jnp.sum(ref[kh * axis:kh * (axis + 1), :] * weights, axis=0, keepdims=True)
            out.append(s + swap(s))
        return out

    def solve(vector_row):
        return weights_of(jnp.sum(inverse * vector_row, axis=1, keepdims=True))

    def dots_row(field):
        s = None
        for axis in range(3):
            term = aw[kh * axis:kh * (axis + 1), :] * field[axis]
            s = term if s is None else s + term
        lower = jnp.sum(jnp.where(low_k, s, 0.0), axis=1, keepdims=True)
        upper = jnp.sum(jnp.where(low_k, 0.0, s), axis=1, keepdims=True)
        spots = jnp.where(lane_k == row_k + vectors, lower, 0.0)
        spots = spots + jnp.where(lane_k == row_k + vectors + kh, upper, 0.0)
        return jnp.sum(spots, axis=0, keepdims=True)

    def dot_local(x, y):
        s = x[0] * y[0] + x[1] * y[1] + x[2] * y[2]
        return jnp.sum(jnp.where(low1, s, 0.0), axis=1, keepdims=True)

    def stat(ref, row_value):
        ref[...] = jnp.broadcast_to(row_value, (8, LANES))

    def at_lane(index, value):
        return jnp.where(lane1 == index, value, 0.0)

    def put(ref, field):
        ref[...] = jnp.zeros((8, LANES), F32)
        for axis in range(3):
            ref[axis:axis + 1, :] = field[axis]

    def product(vec_all, send):
        spread(vec_all, 3)
        half_tiles = tiles // 2
        for part in range(2):
            def one(i, sums):
                rows = pl.ds(pl.multiple_of(i * 8, 8), 8)
                value = [src_b[axis, rows, :] for axis in range(3)]
                out = []
                for q in range(half_tiles):
                    base = (part * half_tiles + q) * LANES
                    m = [mob[slot, rows, base:base + LANES] for slot in range(6)]
                    for axis in range(3):
                        out.append(
                            sums[3 * q + axis]
                            + (m[SLOT[axis, 0]] * value[0] + m[SLOT[axis, 1]] * value[1])
                            + m[SLOT[axis, 2]] * value[2]
                        )
                return tuple(out)
            zero = jnp.zeros((8, LANES), F32)
            sums = lax.fori_loop(0, span // 8, one, (zero,) * (3 * half_tiles), unroll=2)
            for q in range(half_tiles):
                send[part * half_tiles + q] = jnp.zeros((8, LANES), F32)
                for axis in range(3):
                    send[part * half_tiles + q, axis:axis + 1, :] = jnp.sum(
                        sums[3 * q + axis], axis=0, keepdims=True
                    )

    def mine(recv):
        tile = total(recv)
        odd = lax.rem(r, 2)
        keep = jnp.where(low1, 1 - odd, odd) == 1
        out = []
        for axis in range(3):
            half = jnp.where(keep, tile[axis:axis + 1, :], 0.0)
            out.append(half + swap(half))
        return out

    weights = weights_of(coarse)
    x0 = combine(wp_ref, weights)
    image0 = combine(aw, weights)
    r0 = [rhs[axis] - image0[axis] for axis in range(3)]

    put(vec_a, r0)
    to_col(vec_a, vec_col_a, 6)
    vec_col_a[c] = vec_a[...]
    stat(stat_a, dots_row(r0) + at_lane(0, dot_local(r0, r0)))
    to_row(lambda peer: stat_a, stat_row_a, 7)
    stat_row_a[r] = stat_a[...]
    arrived(vec_col_a, 6)
    product(vec_col_a, part_a)
    to_row(lambda peer: part_a.at[lax.div(peer, 2)], part_row_a, 8)
    part_row_a[r] = part_a[lax.div(r, 2)]
    arrived(stat_row_a, 7)
    stat_b[...] = total(stat_row_a)
    to_col(stat_b, stat_col_b, 9)
    stat_col_b[c] = stat_b[...]
    arrived(stat_col_b, 9)
    sums0 = total(stat_col_b)[0:1, :]
    norm0 = sums0[:, 0:1]
    weights = solve(sums0)
    shift = combine(wp_ref, weights)
    d0 = [r0[axis] - shift[axis] for axis in range(3)]
    shift_image = combine(aw, weights)
    arrived(part_row_a, 8)
    z0 = mine(part_row_a)
    q0 = [z0[axis] - shift_image[axis] for axis in range(3)]

    put(vec_c, q0)
    to_col(vec_c, vec_col_c, 10)
    vec_col_c[c] = vec_c[...]
    stat(
        stat_c,
        dots_row(q0) + at_lane(0, dot_local(d0, q0)) + at_lane(1, dot_local(r0, q0))
        + at_lane(2, dot_local(q0, q0)),
    )
    to_row(lambda peer: stat_c, stat_row_c, 11)
    stat_row_c[r] = stat_c[...]
    arrived(vec_col_c, 10)
    product(vec_col_c, part_c)
    to_row(lambda peer: part_c.at[lax.div(peer, 2)], part_row_c, 12)
    part_row_c[r] = part_c[lax.div(r, 2)]
    arrived(stat_row_c, 11)
    stat_d[...] = total(stat_row_c)
    to_col(stat_d, stat_col_d, 13)
    stat_col_d[c] = stat_d[...]
    arrived(stat_col_d, 13)
    sums1 = total(stat_col_d)[0:1, :]
    step0 = norm0 / sums1[:, 0:1]
    norm1 = norm0 - 2.0 * step0 * sums1[:, 1:2] + step0 * step0 * sums1[:, 2:3]
    beta = norm1 / norm0
    weights = solve(sums0 - step0 * sums1)
    shift = combine(wp_ref, weights)
    shift_image = combine(aw, weights)
    x1 = [x0[axis] + step0 * d0[axis] for axis in range(3)]
    r1 = [r0[axis] - step0 * q0[axis] for axis in range(3)]
    d1 = [r1[axis] + beta * d0[axis] - shift[axis] for axis in range(3)]
    arrived(part_row_c, 12)
    y0 = mine(part_row_c)
    q1 = [
        (z0[axis] - step0 * y0[axis]) + beta * q0[axis] - shift_image[axis] for axis in range(3)
    ]

    stat(stat_e, at_lane(0, dot_local(d1, q1)))
    to_row(lambda peer: stat_e, stat_row_e, 14)
    stat_row_e[r] = stat_e[...]
    arrived(stat_row_e, 14)
    stat_f[...] = total(stat_row_e)
    to_col(stat_f, stat_col_f, 15)
    stat_col_f[c] = stat_f[...]
    arrived(stat_col_f, 15)
    step1 = norm1 / total(stat_col_f)[0:1, 0:1]
    for axis in range(3):
        sol_ref[axis:axis + 1, :] = (x1[axis] + step1 * d1[axis])[:, :HALF]
        res_ref[axis:axis + 1, :] = (r1[axis] - step1 * q1[axis])[:, :HALF]

    for tag, dst in enumerate((
        gcol, grow, wcol, aw_recv, gram_row, gram_col, vec_col_a, stat_row_a, part_row_a,
        stat_col_b, vec_col_c, stat_row_c, part_row_c, stat_col_d, stat_row_e, stat_col_f,
    )):
        departed(dst, tag)


def body(n, positions, radii, basis, rhs):
    vectors = basis.shape[0]
    kh = vectors // 2
    span = n * HALF
    once = jnp.concatenate([positions, radii[None], rhs, jnp.zeros((1, HALF), F32)], axis=0)
    geo = jnp.concatenate([once, once], axis=1)
    wp = basis.reshape(2, kh, 3, HALF).transpose(2, 1, 0, 3).reshape(3 * kh, LANES)
    tile = pltpu.VMEM((8, LANES), F32)
    slots = pltpu.VMEM((n, 8, LANES), F32)
    parts = pltpu.VMEM((span // LANES, 8, LANES), F32)
    field_slots = pltpu.VMEM((n, 3 * kh, LANES), F32)
    two = pltpu.VMEM((16, LANES), F32)
    two_slots = pltpu.VMEM((n, 16, LANES), F32)
    vmem = pl.BlockSpec(memory_space=pltpu.VMEM)
    return pl.pallas_call(
        functools.partial(kernel, n, vectors),
        out_shape=(jax.ShapeDtypeStruct((3, HALF), F32), jax.ShapeDtypeStruct((3, HALF), F32)),
        in_specs=[vmem, vmem],
        out_specs=(vmem, vmem),
        scratch_shapes=[
            slots, slots, field_slots,
            pltpu.VMEM((4, span, LANES), F32),
            pltpu.VMEM((8, span), F32),
            pltpu.VMEM((6, span, span), F32),
            pltpu.VMEM((8 * vectors, span), BF16),
            field_slots, field_slots,
            pltpu.VMEM((3 * kh, LANES), F32),
            two, two_slots, two, two_slots,
            tile, slots, tile, slots, parts, slots, tile, slots,
            tile, slots, tile, slots, parts, slots, tile, slots,
            tile, slots, tile, slots,
            pltpu.SemaphoreType.DMA((16,)),
            pltpu.SemaphoreType.DMA((16,)),
        ],
        compiler_params=pltpu.CompilerParams(
            collective_id=0, has_side_effects=True, vmem_limit_bytes=56 << 20
        ),
    )(geo, wp)


def solution(mesh):
    return jax.shard_map(
        functools.partial(body, mesh.shape["row"]),
        mesh=mesh,
        in_specs=(
            P(None, ("row", "col")),
            P(("row", "col")),
            P(None, None, ("row", "col")),
            P(None, ("row", "col")),
        ),
        out_specs=(P(None, ("row", "col")), P(None, ("row", "col"))),
        check_vma=False,
    )
```

```python
import functools
import math

import jax
import jax.numpy as jnp
from jax import lax
from jax.experimental import pallas as pl
from jax.experimental.pallas import tpu as pltpu
from jax.sharding import PartitionSpec as P

MESH = pl.DeviceIdType.MESH
F32 = jnp.float32
BF16 = jnp.bfloat16

far_scale = 1.0 / (8.0 * math.pi)
self_scale = 1.0 / (6.0 * math.pi)

LANES = 128
HALF = 64
PAIRS = ((0, 0), (1, 1), (2, 2), (0, 1), (1, 2), (2, 0))
SLOT = {}
for _slot, (_a, _b) in enumerate(PAIRS):
    SLOT[_a, _b] = _slot
    SLOT[_b, _a] = _slot


def kernel(
    n, vectors,
    pos_ref, rad_ref, basis_ref, rhs_ref,
    out_ref,
    pos_in, rad_in, basis_in, rhs_in, geo, wp,
    grow, gcol, wcol, wrow, src_b, tgt, mob, fields, w_tgt, p_tgt, aw_send, aw_recv, aw,
    gram_a, gram_row, gram_b, gram_col,
    vec_a, vec_col_a, stat_a, stat_row_a, part_a, part_row_a, stat_b, stat_col_b,
    vec_c, vec_col_c, vec_row_c, part_c, part_row_c, stat_d, stat_col_d,
    stat_f, stat_col_f,
    in_sems, send_sems, recv_sems,
):
    at_row = lax.axis_index("row")
    at_col = lax.axis_index("col")
    core = lax.rem(at_row, 2)
    y_low = lax.rem(at_col, 2)
    r = lax.div(at_row, 2) * 2 + y_low
    c = lax.div(at_col, 2) * 2 + core

    def row_peer(index):
        return (lax.div(index, 2) * 2 + core, lax.div(at_col, 2) * 2 + lax.rem(index, 2))

    def col_peer(index):
        return (lax.div(at_row, 2) * 2 + lax.rem(index, 2), lax.div(index, 2) * 2 + y_low)

    kh = vectors // 2
    span = n * HALF
    tiles = span // LANES

    barrier = pltpu.get_barrier_semaphore()

    def greet(step, carry):
        pl.semaphore_signal(
            barrier, inc=1, device_id=row_peer(lax.rem(r + step, n)), device_id_type=MESH
        )
        pl.semaphore_signal(
            barrier, inc=1, device_id=col_peer(lax.rem(c + step, n)), device_id_type=MESH
        )
        return carry
    lax.fori_loop(1, n, greet, 0)

    reads = [
        pltpu.make_async_copy(src, dst, in_sems.at[i])
        for i, (src, dst) in enumerate((
            (pos_ref, pos_in), (rad_ref, rad_in), (basis_ref, basis_in), (rhs_ref, rhs_in)
        ))
    ]
    for read in reads:
        read.start()
    for read in reads:
        read.wait()
    for half in range(2):
        lanes = slice(half * HALF, (half + 1) * HALF)
        geo[0:3, lanes] = pos_in[...]
        geo[3:4, lanes] = rad_in[...]
        for axis in range(3):
            wp[kh * axis:kh * (axis + 1), lanes] = basis_in[axis, kh * half:kh * (half + 1), :]

    lane1 = lax.broadcasted_iota(jnp.int32, (1, LANES), 1)
    lane4 = lax.broadcasted_iota(jnp.int32, (4, LANES), 1)
    lane8 = lax.broadcasted_iota(jnp.int32, (8, LANES), 1)
    lane_k = lax.broadcasted_iota(jnp.int32, (kh, LANES), 1)
    row_k = lax.broadcasted_iota(jnp.int32, (kh, LANES), 0)
    low1, low4, low_k = lane1 < HALF, lane4 < HALF, lane_k < HALF

    def swap(x):
        return pltpu.roll(x, HALF, 1)

    def to_row(src, dst, tag):
        def one(step, carry):
            peer = lax.rem(r + step, n)
            pltpu.make_async_remote_copy(
                src_ref=src(peer), dst_ref=dst.at[r], send_sem=send_sems.at[tag],
                recv_sem=recv_sems.at[tag], device_id=row_peer(peer), device_id_type=MESH,
            ).start()
            return carry
        lax.fori_loop(1, n, one, 0)

    def to_col(src, dst, tag):
        def one(step, carry):
            peer = lax.rem(c + step, n)
            pltpu.make_async_remote_copy(
                src_ref=src, dst_ref=dst.at[c], send_sem=send_sems.at[tag],
                recv_sem=recv_sems.at[tag], device_id=col_peer(peer), device_id_type=MESH,
            ).start()
            return carry
        lax.fori_loop(1, n, one, 0)

    def arrived(dst, tag):
        all_but_one = dst.at[pl.ds(0, n - 1)]
        pltpu.make_async_copy(all_but_one, all_but_one, recv_sems.at[tag]).wait()

    def departed(dst, tag):
        all_but_one = dst.at[pl.ds(0, n - 1)]
        pltpu.make_async_copy(all_but_one, all_but_one, send_sems.at[tag]).wait()

    def total(ref):
        parts = [ref[i] for i in range(n)]
        while len(parts) > 1:
            parts = [parts[i] + parts[i + 1] for i in range(0, len(parts), 2)]
        return parts[0]

    pl.semaphore_wait(barrier, 2 * (n - 1))

    to_col(geo, gcol, 0)
    to_row(lambda peer: geo, grow, 1)
    to_col(wp, wcol, 2)
    to_row(lambda peer: wp, wrow, 14)
    gcol[c] = geo[...]
    grow[r] = geo[...]
    wcol[c] = wp[...]
    wrow[r] = wp[...]

    def spread(ref, count):
        for p in range(tiles):
            tile = jnp.where(low4, ref[2 * p], ref[2 * p + 1])
            turned = jnp.concatenate([tile, tile], axis=0).T
            for axis in range(count):
                src_b[axis, pl.ds(p * LANES, LANES), :] = jnp.broadcast_to(
                    turned[:, axis:axis + 1], (LANES, LANES)
                )

    arrived(gcol, 0)
    spread(gcol, 4)
    arrived(grow, 1)
    for q in range(tiles):
        tgt[:, q * LANES:(q + 1) * LANES] = jnp.where(low4, grow[2 * q], grow[2 * q + 1])

    def form_tile(q, carry):
        lanes = pl.ds(pl.multiple_of(q * LANES, LANES), LANES)
        tx, ty, tz, t_rad = [
            jnp.broadcast_to(tgt[axis:axis + 1, lanes], (8, LANES)) for axis in range(4)
        ]
        t_rad_sq = t_rad * t_rad
        own = self_scale / t_rad
        t_rel = lane8 + (q * LANES - r * HALF)
        t_key = jnp.where(jnp.logical_and(t_rel >= 0, t_rel < HALF), t_rel, -span)
        s_rel0 = lax.broadcasted_iota(jnp.int32, (8, LANES), 0) - c * HALF

        def form_row(i, inner):
            rows = pl.ds(pl.multiple_of(i * 8, 8), 8)
            sx, sy, sz, s_rad = [src_b[axis, rows, :] for axis in range(4)]
            s_rel = s_rel0 + i * 8
            same = s_rel == t_key
            dx, dy, dz = tx - sx, ty - sy, tz - sz
            dist_sq = dx * dx + dy * dy + dz * dz
            inv = lax.rsqrt(jnp.where(same, 1.0, dist_sq))
            inv_sq = inv * inv
            ratio = (t_rad_sq + s_rad * s_rad) * inv_sq
            scaled = far_scale * inv
            iso = jnp.where(same, own, scaled + scaled * (ratio * (1.0 / 3.0)))
            along = (scaled - scaled * ratio) * inv_sq
            ax, ay, az = along * dx, along * dy, along * dz
            mob[0, rows, lanes] = ax * dx + iso
            mob[1, rows, lanes] = ay * dy + iso
            mob[2, rows, lanes] = az * dz + iso
            mob[3, rows, lanes] = ax * dy
            mob[4, rows, lanes] = ay * dz
            mob[5, rows, lanes] = az * dx
            return inner
        lax.fori_loop(0, span // 8, form_row, 0, unroll=4)
        return carry
    lax.fori_loop(0, tiles, form_tile, 0)

    def unpack_pair(ref, p, axis):
        first = ref[2 * p, kh * axis:kh * (axis + 1), :]
        second = ref[2 * p + 1, kh * axis:kh * (axis + 1), :]
        return jnp.concatenate(
            [jnp.where(low_k, first, swap(second)), jnp.where(low_k, swap(first), second)], axis=0
        )

    arrived(wcol, 2)
    for p in range(tiles):
        cols = slice(p * LANES, (p + 1) * LANES)
        for axis in range(3):
            block = unpack_pair(wcol, p, axis)
            high = block.astype(BF16)
            rest = (block - high.astype(F32)).astype(BF16)
            for copy in (axis, axis + 3):
                if copy < 4:
                    base = 2 * vectors * copy
                    fields[base:base + vectors, cols] = high
                    fields[base + vectors:base + 2 * vectors, cols] = rest

    chunk = 4 * HALF
    depth = 256

    def basis_chunk(step, carry):
        which = lax.rem(lax.div(r, 4) + 1 + step, n // 4)
        lanes = pl.ds(pl.multiple_of(which * chunk, chunk), chunk)
        sums = [jnp.zeros((vectors, chunk), F32) for _ in range(3)]
        for slot, (a, b) in enumerate(PAIRS):
            first_row = 2 * vectors * a
            count = 2 * vectors if a == b else 4 * vectors
            acc_high = jnp.zeros((count, chunk), F32)
            acc_rest = jnp.zeros((count, chunk), F32)
            for d in range(span // depth):
                entry = mob[slot, d * depth:(d + 1) * depth, lanes]
                high = entry.astype(BF16)
                rest = (entry - high.astype(F32)).astype(BF16)
                lhs = fields[first_row:first_row + count, d * depth:(d + 1) * depth]
                acc_high = acc_high + jnp.dot(lhs, high, preferred_element_type=F32)
                acc_rest = acc_rest + jnp.dot(lhs, rest, preferred_element_type=F32)

            def gather(base):
                return (
                    acc_high[base:base + vectors] + acc_high[base + vectors:base + 2 * vectors]
                    + acc_rest[base:base + vectors]
                )
            if a == b:
                sums[a] = sums[a] + gather(0)
            else:
                sums[b] = sums[b] + gather(0)
                sums[a] = sums[a] + gather(2 * vectors)
        for axis in range(3):
            p_tgt[axis, :, lanes] = sums[axis]
        for part in range(2):
            for axis in range(3):
                piece = sums[axis][:, part * LANES:(part + 1) * LANES]
                lower, upper = piece[:kh], piece[kh:]
                slot_rows = slice(kh * axis, kh * (axis + 1))
                aw_send[4 * which + 2 * part, slot_rows, :] = jnp.where(low_k, lower, swap(upper))
                aw_send[4 * which + 2 * part + 1, slot_rows, :] = jnp.where(low_k, swap(lower), upper)
        for part in range(4):
            target = 4 * which + part

            @pl.when(target != r)
            def _():
                pltpu.make_async_remote_copy(
                    src_ref=aw_send.at[target], dst_ref=aw_recv.at[r], send_sem=send_sems.at[3],
                    recv_sem=recv_sems.at[3], device_id=row_peer(target), device_id_type=MESH,
                ).start()
        return carry
    lax.fori_loop(0, n // 4, basis_chunk, 0)
    aw_recv[r] = aw_send[r]

    rhs = [jnp.concatenate([rhs_in[axis:axis + 1, :]] * 2, axis=1) for axis in range(3)]
    row32 = lax.broadcasted_iota(jnp.int32, (vectors, LANES), 0)
    lane32 = lax.broadcasted_iota(jnp.int32, (vectors, LANES), 1)

    arrived(wrow, 14)
    for p in range(tiles):
        for axis in range(3):
            w_tgt[axis, :, p * LANES:(p + 1) * LANES] = unpack_pair(wrow, p, axis)
    gram = None
    load = None
    for axis in range(3):
        term = lax.dot_general(
            w_tgt[axis], p_tgt[axis], (((1,), (1,)), ((), ())),
            precision=lax.Precision.HIGHEST, preferred_element_type=F32,
        )
        block = wp[kh * axis:kh * (axis + 1), :]
        block = jnp.where(lane32 < HALF, jnp.concatenate([block, swap(block)], axis=0), 0.0)
        load_term = block * rhs[axis]
        gram = term if gram is None else gram + term
        load = load_term if load is None else load + load_term
    load = jnp.sum(load, axis=1, keepdims=True)
    wide = jnp.concatenate([gram, jnp.zeros((vectors, LANES - vectors), F32)], axis=1)
    groups = vectors // 8
    packed = wide[0:8]
    load_tile = jnp.where(lane8 == 0, load[0:8], 0.0)
    for g in range(1, groups):
        packed = packed + pltpu.roll(wide[8 * g:8 * g + 8], vectors * g, 1)
        load_tile = load_tile + jnp.where(lane8 == vectors * g, load[8 * g:8 * g + 8], 0.0)
    gram_a[0:8, :] = packed
    gram_a[8:16, :] = load_tile
    to_row(lambda peer: gram_a, gram_row, 4)
    gram_row[r] = gram_a[...]
    arrived(gram_row, 4)
    gram_b[...] = total(gram_row)
    to_col(gram_b, gram_col, 5)
    gram_col[c] = gram_b[...]
    arrived(gram_col, 5)
    both = total(gram_col)
    packed, load_tile = both[0:8], both[8:16]
    pieces, load_pieces = [packed], [load_tile]
    for g in range(1, groups):
        pieces.append(pltpu.roll(packed, LANES - vectors * g, 1))
        load_pieces.append(pltpu.roll(load_tile, LANES - vectors * g, 1))
    gram = jnp.concatenate(pieces, axis=0)
    load = jnp.concatenate(load_pieces, axis=0)[:, 0:1]

    system = jnp.where(lane32 < vectors, gram, jnp.where(lane32 == row32 + vectors, 1.0, 0.0))
    system = jnp.where(lane32 == 2 * vectors, load, system)
    for j in range(vectors):
        pivot_row = system[j:j + 1, :]
        scaled_row = pivot_row / pivot_row[:, j:j + 1]
        column = system[:, j:j + 1]
        system = jnp.where(row32 == j, scaled_row, system - column * scaled_row)
    inverse = jnp.where(jnp.logical_and(lane32 >= vectors, lane32 < 2 * vectors), system, 0.0)
    coarse = system[:, 2 * vectors:2 * vectors + 1]

    def weights_of(column):
        return jnp.where(low_k, column[:kh], column[kh:])

    def combine(ref, weights):
        out = []
        for axis in range(3):
            s = jnp.sum(ref[kh * axis:kh * (axis + 1), :] * weights, axis=0, keepdims=True)
            out.append(s + swap(s))
        return out

    def solve(vector_row):
        return weights_of(jnp.sum(inverse * vector_row, axis=1, keepdims=True))

    def dots_row(field):
        s = None
        for axis in range(3):
            term = aw[kh * axis:kh * (axis + 1), :] * field[axis]
            s = term if s is None else s + term
        lower = jnp.sum(jnp.where(low_k, s, 0.0), axis=1, keepdims=True)
        upper = jnp.sum(jnp.where(low_k, 0.0, s), axis=1, keepdims=True)
        spots = jnp.where(lane_k == row_k + vectors, lower, 0.0)
        spots = spots + jnp.where(lane_k == row_k + vectors + kh, upper, 0.0)
        return jnp.sum(spots, axis=0, keepdims=True)

    def dot_local(x, y):
        s = x[0] * y[0] + x[1] * y[1] + x[2] * y[2]
        return jnp.sum(jnp.where(low1, s, 0.0), axis=1, keepdims=True)

    def stat(ref, row_value):
        ref[...] = row_value

    def at_lane(index, value):
        return jnp.where(lane1 == index, value, 0.0)

    def put(ref, field, last):
        for axis in range(3):
            ref[axis:axis + 1, :] = field[axis]
        ref[3:4, :] = last

    def product(vec_all, send, weigh):
        spread(vec_all, 3)
        half_tiles = tiles // 2
        dots = []
        for part in range(2):
            def one(i, sums):
                rows = pl.ds(pl.multiple_of(i * 8, 8), 8)
                value = [src_b[axis, rows, :] for axis in range(3)]
                out = []
                for q in range(half_tiles):
                    base = (part * half_tiles + q) * LANES
                    m = [mob[slot, rows, base:base + LANES] for slot in range(6)]
                    for axis in range(3):
                        out.append(
                            sums[3 * q + axis]
                            + (m[SLOT[axis, 0]] * value[0] + m[SLOT[axis, 1]] * value[1])
                            + m[SLOT[axis, 2]] * value[2]
                        )
                return tuple(out)
            zero = jnp.zeros((8, LANES), F32)
            sums = lax.fori_loop(0, span // 8, one, (zero,) * (3 * half_tiles), unroll=2)
            for q in range(half_tiles):
                for axis in range(3):
                    value = jnp.sum(sums[3 * q + axis], axis=0, keepdims=True)
                    send[part * half_tiles + q, axis:axis + 1, :] = value
                    if weigh is not None:
                        tile = part * half_tiles + q
                        weight = jnp.where(
                            low1, weigh[2 * tile, axis:axis + 1, :], weigh[2 * tile + 1, axis:axis + 1, :]
                        )
                        dots.append(value * weight)
        last = jnp.zeros((1, LANES), F32)
        if weigh is not None:
            while len(dots) > 1:
                dots = [sum(dots[i:i + 2]) for i in range(0, len(dots), 2)]
            last = jnp.broadcast_to(jnp.sum(dots[0], axis=1, keepdims=True), (1, LANES))
        for q in range(tiles):
            send[q, 3:4, :] = last

    def mine(recv):
        tile = total(recv)
        odd = lax.rem(r, 2)
        keep = jnp.where(low1, 1 - odd, odd) == 1
        out = []
        for axis in range(3):
            half = jnp.where(keep, tile[axis:axis + 1, :], 0.0)
            out.append(half + swap(half))
        return out, tile[3:4, :]

    arrived(aw_recv, 3)
    aw[...] = total(aw_recv)
    weights = weights_of(coarse)
    x0 = combine(wp, weights)
    image0 = combine(aw, weights)
    r0 = [rhs[axis] - image0[axis] for axis in range(3)]

    put(vec_a, r0, jnp.zeros((1, LANES), F32))
    to_col(vec_a, vec_col_a, 6)
    vec_col_a[c] = vec_a[...]
    stat(stat_a, dots_row(r0) + at_lane(0, dot_local(r0, r0)))
    to_row(lambda peer: stat_a, stat_row_a, 7)
    stat_row_a[r] = stat_a[...]
    arrived(vec_col_a, 6)
    product(vec_col_a, part_a, None)
    to_row(lambda peer: part_a.at[lax.div(peer, 2)], part_row_a, 8)
    part_row_a[r] = part_a[lax.div(r, 2)]
    arrived(stat_row_a, 7)
    stat_b[...] = total(stat_row_a)
    to_col(stat_b, stat_col_b, 9)
    stat_col_b[c] = stat_b[...]
    arrived(stat_col_b, 9)
    sums0 = total(stat_col_b)[0:1, :]
    norm0 = sums0[:, 0:1]
    weights = solve(sums0)
    shift = combine(wp, weights)
    d0 = [r0[axis] - shift[axis] for axis in range(3)]
    shift_image = combine(aw, weights)
    arrived(part_row_a, 8)
    z0, _ = mine(part_row_a)
    q0 = [z0[axis] - shift_image[axis] for axis in range(3)]

    put(
        vec_c, q0,
        dots_row(q0) + at_lane(0, dot_local(d0, q0)) + at_lane(1, dot_local(r0, q0))
        + at_lane(2, dot_local(q0, q0)),
    )
    to_col(vec_c, vec_col_c, 10)
    to_row(lambda peer: vec_c, vec_row_c, 11)
    vec_col_c[c] = vec_c[...]
    vec_row_c[r] = vec_c[...]
    arrived(vec_row_c, 11)
    stat_d[...] = total(vec_row_c)[3:4, :]
    to_col(stat_d, stat_col_d, 13)
    stat_col_d[c] = stat_d[...]
    arrived(vec_col_c, 10)
    product(vec_col_c, part_c, vec_row_c)
    to_row(lambda peer: part_c.at[lax.div(peer, 2)], part_row_c, 12)
    part_row_c[r] = part_c[lax.div(r, 2)]
    arrived(stat_col_d, 13)
    sums1 = total(stat_col_d)
    step0 = norm0 / sums1[:, 0:1]
    norm1 = norm0 - 2.0 * step0 * sums1[:, 1:2] + step0 * step0 * sums1[:, 2:3]
    beta = norm1 / norm0
    weights = solve(sums0 - step0 * sums1)
    shift = combine(wp, weights)
    shift_image = combine(aw, weights)
    x1 = [x0[axis] + step0 * d0[axis] for axis in range(3)]
    r1 = [r0[axis] - step0 * q0[axis] for axis in range(3)]
    d1 = [r1[axis] + beta * d0[axis] - shift[axis] for axis in range(3)]
    inner = jnp.sum(inverse * sums1, axis=1, keepdims=True)
    column = jnp.sum(jnp.where(lane32 == row32 + vectors, sums1, 0.0), axis=1, keepdims=True)
    removed = jnp.sum(inner * column, axis=0, keepdims=True)
    factor = 1.0 + beta
    fixed = factor * factor * sums1[:, 0:1] - 2.0 * factor * step0 * sums1[:, 2:3]
    arrived(part_row_c, 12)
    y0, block_sum = mine(part_row_c)
    stat_f[...] = block_sum
    to_col(stat_f, stat_col_f, 15)
    stat_col_f[c] = stat_f[...]
    q1 = [
        (z0[axis] - step0 * y0[axis]) + beta * q0[axis] - shift_image[axis] for axis in range(3)
    ]
    arrived(stat_col_f, 15)
    curvature = fixed + step0 * step0 * (total(stat_col_f)[:, 0:1] - removed)
    step1 = norm1 / curvature
    for axis in range(3):
        out_ref[axis:axis + 1, :] = x1[axis] + step1 * d1[axis]
        out_ref[4 + axis:5 + axis, :] = r1[axis] - step1 * q1[axis]

    for tag, dst in enumerate((
        gcol, grow, wcol, aw_recv, gram_row, gram_col, vec_col_a, stat_row_a, part_row_a,
        stat_col_b, vec_col_c, vec_row_c, part_row_c, stat_col_d, wrow, stat_col_f,
    )):
        departed(dst, tag)


def body(n, positions, radii, basis, rhs):
    vectors = basis.shape[0]
    kh = vectors // 2
    span = n * HALF
    row, rows = pltpu.VMEM((1, LANES), F32), pltpu.VMEM((n, 1, LANES), F32)
    tile, tile_slots = pltpu.VMEM((4, LANES), F32), pltpu.VMEM((n, 4, LANES), F32)
    parts = pltpu.VMEM((span // LANES, 4, LANES), F32)
    field, field_slots = pltpu.VMEM((3 * kh, LANES), F32), pltpu.VMEM((n, 3 * kh, LANES), F32)
    two, two_slots = pltpu.VMEM((16, LANES), F32), pltpu.VMEM((n, 16, LANES), F32)
    vmem = pl.BlockSpec(memory_space=pltpu.VMEM)
    anywhere = pl.BlockSpec(memory_space=pl.ANY)
    out = pl.pallas_call(
        functools.partial(kernel, n, vectors),
        out_shape=jax.ShapeDtypeStruct((8, LANES), F32),
        in_specs=[anywhere] * 4,
        out_specs=vmem,
        scratch_shapes=[
            pltpu.VMEM((3, HALF), F32), pltpu.VMEM((1, HALF), F32),
            pltpu.VMEM((3, vectors, HALF), F32), pltpu.VMEM((3, HALF), F32),
            tile, field,
            tile_slots, tile_slots, field_slots, field_slots,
            pltpu.VMEM((4, span, LANES), F32),
            pltpu.VMEM((4, span), F32),
            pltpu.VMEM((6, span, span), F32),
            pltpu.VMEM((8 * vectors, span), BF16),
            pltpu.VMEM((3, vectors, span), F32), pltpu.VMEM((3, vectors, span), F32),
            field_slots, field_slots, field,
            two, two_slots, two, two_slots,
            tile, tile_slots, row, rows, parts, tile_slots, row, rows,
            tile, tile_slots, tile_slots, parts, tile_slots, row, rows,
            row, rows,
            pltpu.SemaphoreType.DMA((4,)),
            pltpu.SemaphoreType.DMA((16,)),
            pltpu.SemaphoreType.DMA((16,)),
        ],
        compiler_params=pltpu.CompilerParams(
            collective_id=0, has_side_effects=True, vmem_limit_bytes=56 << 20
        ),
    )(positions, radii[None], basis.transpose(1, 0, 2), rhs)
    return out[0:3, :HALF], out[4:7, :HALF]


def solution(mesh):
    return jax.shard_map(
        functools.partial(body, mesh.shape["row"]),
        mesh=mesh,
        in_specs=(
            P(None, ("row", "col")),
            P(("row", "col")),
            P(None, None, ("row", "col")),
            P(None, ("row", "col")),
        ),
        out_specs=(P(None, ("row", "col")), P(None, ("row", "col"))),
        check_vma=False,
    )
```

```python
import functools
import math

import jax
import jax.numpy as jnp
from jax import lax
from jax.experimental import pallas as pl
from jax.experimental.pallas import tpu as pltpu
from jax.sharding import PartitionSpec as P

MESH = pl.DeviceIdType.MESH
F32 = jnp.float32
BF16 = jnp.bfloat16

far_scale = 1.0 / (8.0 * math.pi)
self_scale = 1.0 / (6.0 * math.pi)

LANES = 128
HALF = 64
PAIRS = ((0, 0), (1, 1), (2, 2), (0, 1), (1, 2), (2, 0))
SLOT = {}
for _slot, (_a, _b) in enumerate(PAIRS):
    SLOT[_a, _b] = _slot
    SLOT[_b, _a] = _slot


def kernel(
    n, vectors,
    pos_ref, rad_ref, basis_ref, rhs_ref,
    out_ref,
    pos_in, rad_in, basis_in, rhs_in, geo, wp,
    grow, gcol, wcol, wrow, src_b, tgt, mob, fields, w_tgt, p_tgt, aw_send, aw_recv, aw,
    gram_a, gram_row, gram_b, gram_col,
    vec_a, vec_col_a, stat_a, stat_row_a, part_a, part_row_a, stat_b, stat_col_b,
    vec_c, vec_col_c, vec_row_c, part_c, part_row_c, stat_d, stat_col_d,
    stat_f, stat_col_f,
    in_sems, send_sems, recv_sems, chunk_sems,
):
    at_row = lax.axis_index("row")
    at_col = lax.axis_index("col")
    core = lax.rem(at_row, 2)
    y_low = lax.rem(at_col, 2)
    r = lax.div(at_row, 2) * 2 + y_low
    c = lax.div(at_col, 2) * 2 + core

    def row_peer(index):
        return (lax.div(index, 2) * 2 + core, lax.div(at_col, 2) * 2 + lax.rem(index, 2))

    def col_peer(index):
        return (lax.div(at_row, 2) * 2 + lax.rem(index, 2), lax.div(index, 2) * 2 + y_low)

    kh = vectors // 2
    span = n * HALF
    tiles = span // LANES

    barrier = pltpu.get_barrier_semaphore()

    def greet(step, carry):
        pl.semaphore_signal(
            barrier, inc=1, device_id=row_peer(lax.rem(r + step, n)), device_id_type=MESH
        )
        pl.semaphore_signal(
            barrier, inc=1, device_id=col_peer(lax.rem(c + step, n)), device_id_type=MESH
        )
        return carry
    lax.fori_loop(1, n, greet, 0)

    reads = [
        pltpu.make_async_copy(src, dst, in_sems.at[i])
        for i, (src, dst) in enumerate((
            (pos_ref, pos_in), (rad_ref, rad_in), (basis_ref, basis_in), (rhs_ref, rhs_in)
        ))
    ]
    for read in reads:
        read.start()
    for read in reads:
        read.wait()
    for half in range(2):
        lanes = slice(half * HALF, (half + 1) * HALF)
        geo[0:3, lanes] = pos_in[...]
        geo[3:4, lanes] = rad_in[...]
        for axis in range(3):
            wp[kh * axis:kh * (axis + 1), lanes] = basis_in[axis, kh * half:kh * (half + 1), :]

    lane1 = lax.broadcasted_iota(jnp.int32, (1, LANES), 1)
    lane4 = lax.broadcasted_iota(jnp.int32, (4, LANES), 1)
    lane8 = lax.broadcasted_iota(jnp.int32, (8, LANES), 1)
    lane_k = lax.broadcasted_iota(jnp.int32, (kh, LANES), 1)
    row_k = lax.broadcasted_iota(jnp.int32, (kh, LANES), 0)
    low1, low4, low_k = lane1 < HALF, lane4 < HALF, lane_k < HALF

    def swap(x):
        return pltpu.roll(x, HALF, 1)

    def to_row(src, dst, tag):
        def one(step, carry):
            peer = lax.rem(r + step, n)
            pltpu.make_async_remote_copy(
                src_ref=src(peer), dst_ref=dst.at[r], send_sem=send_sems.at[tag],
                recv_sem=recv_sems.at[tag], device_id=row_peer(peer), device_id_type=MESH,
            ).start()
            return carry
        lax.fori_loop(1, n, one, 0)

    def to_col(src, dst, tag):
        def one(step, carry):
            peer = lax.rem(c + step, n)
            pltpu.make_async_remote_copy(
                src_ref=src, dst_ref=dst.at[c], send_sem=send_sems.at[tag],
                recv_sem=recv_sems.at[tag], device_id=col_peer(peer), device_id_type=MESH,
            ).start()
            return carry
        lax.fori_loop(1, n, one, 0)

    chunks = n // 4
    order = sorted(range(chunks), key=lambda k: min(k, chunks - k))

    def to_col_chunks(src, dst, tag, which):
        def one(step, carry):
            peer = lax.rem(c + step, n)
            pltpu.make_async_remote_copy(
                src_ref=src, dst_ref=dst.at[c], send_sem=send_sems.at[tag],
                recv_sem=chunk_sems.at[which, lax.div(c, 4)], device_id=col_peer(peer),
                device_id_type=MESH,
            ).start()
            return carry
        lax.fori_loop(1, n, one, 0)

    def chunk_at(dst, which, step):
        chunk = lax.rem(lax.div(c, 4) + order[step], chunks)
        some = dst.at[pl.ds(0, 3 if step == 0 else 4)]
        pltpu.make_async_copy(some, some, chunk_sems.at[which, chunk]).wait()
        return chunk

    def arrived(dst, tag):
        all_but_one = dst.at[pl.ds(0, n - 1)]
        pltpu.make_async_copy(all_but_one, all_but_one, recv_sems.at[tag]).wait()

    def departed(dst, tag):
        all_but_one = dst.at[pl.ds(0, n - 1)]
        pltpu.make_async_copy(all_but_one, all_but_one, send_sems.at[tag]).wait()

    def total(ref):
        parts = [ref[i] for i in range(n)]
        while len(parts) > 1:
            parts = [parts[i] + parts[i + 1] for i in range(0, len(parts), 2)]
        return parts[0]

    pl.semaphore_wait(barrier, 2 * (n - 1))

    to_col(geo, gcol, 0)
    to_row(lambda peer: geo, grow, 1)
    to_col_chunks(wp, wcol, 2, 0)
    to_row(lambda peer: wp, wrow, 14)
    gcol[c] = geo[...]
    grow[r] = geo[...]
    wcol[c] = wp[...]
    wrow[r] = wp[...]

    def spread(ref, pair, count, place):
        tile = jnp.where(low4, ref[2 * pair], ref[2 * pair + 1])
        turned = jnp.concatenate([tile, tile], axis=0).T
        for axis in range(count):
            src_b[axis, place * LANES:(place + 1) * LANES, :] = jnp.broadcast_to(
                turned[:, axis:axis + 1], (LANES, LANES)
            )

    arrived(gcol, 0)
    for p in range(tiles):
        spread(gcol, p, 4, p)
    arrived(grow, 1)
    for q in range(tiles):
        tgt[:, q * LANES:(q + 1) * LANES] = jnp.where(low4, grow[2 * q], grow[2 * q + 1])

    def form_tile(q, carry):
        lanes = pl.ds(pl.multiple_of(q * LANES, LANES), LANES)
        tx, ty, tz, t_rad = [
            jnp.broadcast_to(tgt[axis:axis + 1, lanes], (8, LANES)) for axis in range(4)
        ]
        t_rad_sq = t_rad * t_rad
        own = self_scale / t_rad
        t_rel = lane8 + (q * LANES - r * HALF)
        t_key = jnp.where(jnp.logical_and(t_rel >= 0, t_rel < HALF), t_rel, -span)
        s_rel0 = lax.broadcasted_iota(jnp.int32, (8, LANES), 0) - c * HALF

        def form_row(i, inner):
            rows = pl.ds(pl.multiple_of(i * 8, 8), 8)
            sx, sy, sz, s_rad = [src_b[axis, rows, :] for axis in range(4)]
            s_rel = s_rel0 + i * 8
            same = s_rel == t_key
            dx, dy, dz = tx - sx, ty - sy, tz - sz
            dist_sq = dx * dx + dy * dy + dz * dz
            inv = lax.rsqrt(jnp.where(same, 1.0, dist_sq))
            inv_sq = inv * inv
            ratio = (t_rad_sq + s_rad * s_rad) * inv_sq
            scaled = far_scale * inv
            iso = jnp.where(same, own, scaled + scaled * (ratio * (1.0 / 3.0)))
            along = (scaled - scaled * ratio) * inv_sq
            ax, ay, az = along * dx, along * dy, along * dz
            mob[0, rows, lanes] = ax * dx + iso
            mob[1, rows, lanes] = ay * dy + iso
            mob[2, rows, lanes] = az * dz + iso
            mob[3, rows, lanes] = ax * dy
            mob[4, rows, lanes] = ay * dz
            mob[5, rows, lanes] = az * dx
            return inner
        lax.fori_loop(0, span // 8, form_row, 0, unroll=4)
        return carry
    lax.fori_loop(0, tiles, form_tile, 0)

    def unpack_pair(ref, p, axis):
        first = ref[2 * p, kh * axis:kh * (axis + 1), :]
        second = ref[2 * p + 1, kh * axis:kh * (axis + 1), :]
        return jnp.concatenate(
            [jnp.where(low_k, first, swap(second)), jnp.where(low_k, swap(first), second)], axis=0
        )

    def split(x):
        high = x.astype(BF16)
        return high, (x - high.astype(F32)).astype(BF16)

    arrived(wrow, 14)
    for p in range(tiles):
        cols = slice(p * LANES, (p + 1) * LANES)
        for axis in range(3):
            high, rest = split(unpack_pair(wrow, p, axis))
            w_tgt[axis, 0:vectors, cols] = high
            w_tgt[axis, vectors:2 * vectors, cols] = rest

    width = 4 * HALF
    for step in range(chunks):
        chunk = chunk_at(wcol, 0, step)
        for part in range(2):
            cols = slice(step * width + part * LANES, step * width + (part + 1) * LANES)
            for axis in range(3):
                high, rest = split(unpack_pair(wcol, 2 * chunk + part, axis))
                for copy in (axis, axis + 3):
                    if copy < 4:
                        base = 2 * vectors * copy
                        fields[base:base + vectors, cols] = high
                        fields[base + vectors:base + 2 * vectors, cols] = rest

        def basis_chunk(t, carry, step=step, chunk=chunk):
            lanes = pl.ds(pl.multiple_of(t * width, width), width)
            rows = pl.ds(pl.multiple_of(chunk * width, width), width)
            sums = [None] * 3

            def add(axis, value):
                sums[axis] = value if sums[axis] is None else sums[axis] + value
            for slot, (a, b) in enumerate(PAIRS):
                first_row = 2 * vectors * a
                count = 2 * vectors if a == b else 4 * vectors
                high, rest = split(mob[slot, rows, lanes])
                lhs = fields[first_row:first_row + count, step * width:(step + 1) * width]
                by_high = jnp.dot(lhs, high, preferred_element_type=F32)
                by_rest = jnp.dot(lhs, rest, preferred_element_type=F32)
                for base, axis in ((0, b), (2 * vectors, a))[:count // (2 * vectors)]:
                    add(axis, by_high[base:base + vectors])
                    add(axis, by_high[base + vectors:base + 2 * vectors])
                    add(axis, by_rest[base:base + vectors])
            for axis in range(3):
                if step:
                    p_tgt[axis, :, lanes] = p_tgt[axis, :, lanes] + sums[axis]
                else:
                    p_tgt[axis, :, lanes] = sums[axis]
            return carry
        lax.fori_loop(0, span // width, basis_chunk, 0)

    rhs = [jnp.concatenate([rhs_in[axis:axis + 1, :]] * 2, axis=1) for axis in range(3)]
    row32 = lax.broadcasted_iota(jnp.int32, (vectors, LANES), 0)
    lane32 = lax.broadcasted_iota(jnp.int32, (vectors, LANES), 1)

    gram = None
    load = None
    for axis in range(3):
        high, rest = split(p_tgt[axis])
        along_lanes = (((1,), (1,)), ((), ()))
        by_high = lax.dot_general(w_tgt[axis], high, along_lanes, preferred_element_type=F32)
        by_rest = lax.dot_general(
            w_tgt[axis, 0:vectors, :], rest, along_lanes, preferred_element_type=F32
        )
        term = by_high[0:vectors] + by_high[vectors:2 * vectors] + by_rest
        block = wp[kh * axis:kh * (axis + 1), :]
        block = jnp.where(lane32 < HALF, jnp.concatenate([block, swap(block)], axis=0), 0.0)
        load_term = block * rhs[axis]
        gram = term if gram is None else gram + term
        load = load_term if load is None else load + load_term
    load = jnp.sum(load, axis=1, keepdims=True)
    wide = jnp.concatenate([gram, jnp.zeros((vectors, LANES - vectors), F32)], axis=1)
    groups = vectors // 8
    packed = wide[0:8]
    load_tile = jnp.where(lane8 == 0, load[0:8], 0.0)
    for g in range(1, groups):
        packed = packed + pltpu.roll(wide[8 * g:8 * g + 8], vectors * g, 1)
        load_tile = load_tile + jnp.where(lane8 == vectors * g, load[8 * g:8 * g + 8], 0.0)
    gram_a[0:8, :] = packed
    gram_a[8:16, :] = load_tile
    to_row(lambda peer: gram_a, gram_row, 4)
    gram_row[r] = gram_a[...]

    for q in range(tiles):
        for axis in range(3):
            piece = p_tgt[axis, :, q * LANES:(q + 1) * LANES]
            lower, upper = piece[:kh], piece[kh:]
            slot_rows = slice(kh * axis, kh * (axis + 1))
            aw_send[2 * q, slot_rows, :] = jnp.where(low_k, lower, swap(upper))
            aw_send[2 * q + 1, slot_rows, :] = jnp.where(low_k, swap(lower), upper)
    to_row(lambda peer: aw_send.at[peer], aw_recv, 3)
    aw_recv[r] = aw_send[r]
    arrived(gram_row, 4)
    gram_b[...] = total(gram_row)
    to_col(gram_b, gram_col, 5)
    gram_col[c] = gram_b[...]
    arrived(gram_col, 5)
    both = total(gram_col)
    packed, load_tile = both[0:8], both[8:16]
    pieces, load_pieces = [packed], [load_tile]
    for g in range(1, groups):
        pieces.append(pltpu.roll(packed, LANES - vectors * g, 1))
        load_pieces.append(pltpu.roll(load_tile, LANES - vectors * g, 1))
    gram = jnp.concatenate(pieces, axis=0)
    load = jnp.concatenate(load_pieces, axis=0)[:, 0:1]

    system = jnp.where(lane32 < vectors, gram, jnp.where(lane32 == row32 + vectors, 1.0, 0.0))
    system = jnp.where(lane32 == 2 * vectors, load, system)
    for j in range(vectors):
        pivot_row = system[j:j + 1, :]
        scaled_row = pivot_row / pivot_row[:, j:j + 1]
        column = system[:, j:j + 1]
        system = jnp.where(row32 == j, scaled_row, system - column * scaled_row)
    inverse = jnp.where(jnp.logical_and(lane32 >= vectors, lane32 < 2 * vectors), system, 0.0)
    coarse = system[:, 2 * vectors:2 * vectors + 1]

    def weights_of(column):
        return jnp.where(low_k, column[:kh], column[kh:])

    def combine(ref, weights):
        out = []
        for axis in range(3):
            s = jnp.sum(ref[kh * axis:kh * (axis + 1), :] * weights, axis=0, keepdims=True)
            out.append(s + swap(s))
        return out

    def solve(vector_row):
        return weights_of(jnp.sum(inverse * vector_row, axis=1, keepdims=True))

    def dots_row(field):
        s = None
        for axis in range(3):
            term = aw[kh * axis:kh * (axis + 1), :] * field[axis]
            s = term if s is None else s + term
        lower = jnp.sum(jnp.where(low_k, s, 0.0), axis=1, keepdims=True)
        upper = jnp.sum(jnp.where(low_k, 0.0, s), axis=1, keepdims=True)
        spots = jnp.where(lane_k == row_k + vectors, lower, 0.0)
        spots = spots + jnp.where(lane_k == row_k + vectors + kh, upper, 0.0)
        return jnp.sum(spots, axis=0, keepdims=True)

    def dot_local(x, y):
        s = x[0] * y[0] + x[1] * y[1] + x[2] * y[2]
        return jnp.sum(jnp.where(low1, s, 0.0), axis=1, keepdims=True)

    def stat(ref, row_value):
        ref[...] = row_value

    def at_lane(index, value):
        return jnp.where(lane1 == index, value, 0.0)

    def put(ref, field, last):
        for axis in range(3):
            ref[axis:axis + 1, :] = field[axis]
        ref[3:4, :] = last

    def product(vec_all, which, send, weigh):
        zero = jnp.zeros((8, LANES), F32)
        sums = [zero] * (3 * tiles)
        half = 3 * tiles // 2
        for step in range(chunks):
            chunk = chunk_at(vec_all, which, step)
            for part in range(2):
                spread(vec_all, 2 * chunk + part, 3, 2 * step + part)
            for part in range(2):
                def one(i, carry, step=step, chunk=chunk, part=part):
                    rows = pl.ds(pl.multiple_of(chunk * width + i * 8, 8), 8)
                    at = pl.ds(pl.multiple_of(step * width + i * 8, 8), 8)
                    value = [src_b[axis, at, :] for axis in range(3)]
                    out = []
                    for q in range(tiles // 2):
                        base = (part * (tiles // 2) + q) * LANES
                        m = [mob[slot, rows, base:base + LANES] for slot in range(6)]
                        for axis in range(3):
                            out.append(
                                carry[3 * q + axis]
                                + (m[SLOT[axis, 0]] * value[0] + m[SLOT[axis, 1]] * value[1])
                                + m[SLOT[axis, 2]] * value[2]
                            )
                    return tuple(out)
                mine_sums = tuple(sums[part * half:(part + 1) * half])
                sums[part * half:(part + 1) * half] = lax.fori_loop(
                    0, width // 8, one, mine_sums, unroll=2
                )
        if weigh is not None:
            arrived(weigh, 11)
        dots = []
        for q in range(tiles):
            for axis in range(3):
                value = jnp.sum(sums[3 * q + axis], axis=0, keepdims=True)
                send[q, axis:axis + 1, :] = value
                if weigh is not None:
                    weight = jnp.where(
                        low1, weigh[2 * q, axis:axis + 1, :], weigh[2 * q + 1, axis:axis + 1, :]
                    )
                    dots.append(value * weight)
        last = jnp.zeros((1, LANES), F32)
        if weigh is not None:
            while len(dots) > 1:
                dots = [sum(dots[i:i + 2]) for i in range(0, len(dots), 2)]
            last = jnp.broadcast_to(jnp.sum(dots[0], axis=1, keepdims=True), (1, LANES))
        for q in range(tiles):
            send[q, 3:4, :] = last

    def mine(recv):
        tile = total(recv)
        odd = lax.rem(r, 2)
        keep = jnp.where(low1, 1 - odd, odd) == 1
        out = []
        for axis in range(3):
            half = jnp.where(keep, tile[axis:axis + 1, :], 0.0)
            out.append(half + swap(half))
        return out, tile[3:4, :]

    arrived(aw_recv, 3)
    aw[...] = total(aw_recv)
    weights = weights_of(coarse)
    x0 = combine(wp, weights)
    image0 = combine(aw, weights)
    r0 = [rhs[axis] - image0[axis] for axis in range(3)]

    put(vec_a, r0, jnp.zeros((1, LANES), F32))
    to_col_chunks(vec_a, vec_col_a, 6, 1)
    vec_col_a[c] = vec_a[...]
    stat(stat_a, dots_row(r0) + at_lane(0, dot_local(r0, r0)))
    to_row(lambda peer: stat_a, stat_row_a, 7)
    stat_row_a[r] = stat_a[...]
    product(vec_col_a, 1, part_a, None)
    to_row(lambda peer: part_a.at[lax.div(peer, 2)], part_row_a, 8)
    part_row_a[r] = part_a[lax.div(r, 2)]
    arrived(stat_row_a, 7)
    stat_b[...] = total(stat_row_a)
    to_col(stat_b, stat_col_b, 9)
    stat_col_b[c] = stat_b[...]
    arrived(stat_col_b, 9)
    sums0 = total(stat_col_b)[0:1, :]
    norm0 = sums0[:, 0:1]
    weights = solve(sums0)
    shift = combine(wp, weights)
    d0 = [r0[axis] - shift[axis] for axis in range(3)]
    shift_image = combine(aw, weights)
    arrived(part_row_a, 8)
    z0, _ = mine(part_row_a)
    q0 = [z0[axis] - shift_image[axis] for axis in range(3)]

    put(
        vec_c, q0,
        dots_row(q0) + at_lane(0, dot_local(d0, q0)) + at_lane(1, dot_local(r0, q0))
        + at_lane(2, dot_local(q0, q0)),
    )
    to_col_chunks(vec_c, vec_col_c, 10, 2)
    to_row(lambda peer: vec_c, vec_row_c, 11)
    vec_col_c[c] = vec_c[...]
    vec_row_c[r] = vec_c[...]
    product(vec_col_c, 2, part_c, vec_row_c)
    to_row(lambda peer: part_c.at[lax.div(peer, 2)], part_row_c, 12)
    part_row_c[r] = part_c[lax.div(r, 2)]
    stat_d[...] = total(vec_row_c)[3:4, :]
    to_col(stat_d, stat_col_d, 13)
    stat_col_d[c] = stat_d[...]
    arrived(stat_col_d, 13)
    sums1 = total(stat_col_d)
    step0 = norm0 / sums1[:, 0:1]
    norm1 = norm0 - 2.0 * step0 * sums1[:, 1:2] + step0 * step0 * sums1[:, 2:3]
    beta = norm1 / norm0
    weights = solve(sums0 - step0 * sums1)
    shift = combine(wp, weights)
    shift_image = combine(aw, weights)
    x1 = [x0[axis] + step0 * d0[axis] for axis in range(3)]
    r1 = [r0[axis] - step0 * q0[axis] for axis in range(3)]
    d1 = [r1[axis] + beta * d0[axis] - shift[axis] for axis in range(3)]
    inner = jnp.sum(inverse * sums1, axis=1, keepdims=True)
    column = jnp.sum(jnp.where(lane32 == row32 + vectors, sums1, 0.0), axis=1, keepdims=True)
    removed = jnp.sum(inner * column, axis=0, keepdims=True)
    factor = 1.0 + beta
    fixed = factor * factor * sums1[:, 0:1] - 2.0 * factor * step0 * sums1[:, 2:3]
    arrived(part_row_c, 12)
    y0, block_sum = mine(part_row_c)
    stat_f[...] = block_sum
    to_col(stat_f, stat_col_f, 15)
    stat_col_f[c] = stat_f[...]
    q1 = [
        (z0[axis] - step0 * y0[axis]) + beta * q0[axis] - shift_image[axis] for axis in range(3)
    ]
    arrived(stat_col_f, 15)
    curvature = fixed + step0 * step0 * (total(stat_col_f)[:, 0:1] - removed)
    step1 = norm1 / curvature
    for axis in range(3):
        out_ref[axis:axis + 1, :] = x1[axis] + step1 * d1[axis]
        out_ref[4 + axis:5 + axis, :] = r1[axis] - step1 * q1[axis]

    for tag, dst in enumerate((
        gcol, grow, wcol, aw_recv, gram_row, gram_col, vec_col_a, stat_row_a, part_row_a,
        stat_col_b, vec_col_c, vec_row_c, part_row_c, stat_col_d, wrow, stat_col_f,
    )):
        departed(dst, tag)


def body(n, positions, radii, basis, rhs):
    vectors = basis.shape[0]
    kh = vectors // 2
    span = n * HALF
    row, rows = pltpu.VMEM((1, LANES), F32), pltpu.VMEM((n, 1, LANES), F32)
    tile, tile_slots = pltpu.VMEM((4, LANES), F32), pltpu.VMEM((n, 4, LANES), F32)
    parts = pltpu.VMEM((span // LANES, 4, LANES), F32)
    field, field_slots = pltpu.VMEM((3 * kh, LANES), F32), pltpu.VMEM((n, 3 * kh, LANES), F32)
    two, two_slots = pltpu.VMEM((16, LANES), F32), pltpu.VMEM((n, 16, LANES), F32)
    vmem = pl.BlockSpec(memory_space=pltpu.VMEM)
    anywhere = pl.BlockSpec(memory_space=pl.ANY)
    out = pl.pallas_call(
        functools.partial(kernel, n, vectors),
        out_shape=jax.ShapeDtypeStruct((8, LANES), F32),
        in_specs=[anywhere] * 4,
        out_specs=vmem,
        scratch_shapes=[
            pltpu.VMEM((3, HALF), F32), pltpu.VMEM((1, HALF), F32),
            pltpu.VMEM((3, vectors, HALF), F32), pltpu.VMEM((3, HALF), F32),
            tile, field,
            tile_slots, tile_slots, field_slots, field_slots,
            pltpu.VMEM((4, span, LANES), F32),
            pltpu.VMEM((4, span), F32),
            pltpu.VMEM((6, span, span), F32),
            pltpu.VMEM((8 * vectors, span), BF16),
            pltpu.VMEM((3, 2 * vectors, span), BF16), pltpu.VMEM((3, vectors, span), F32),
            field_slots, field_slots, field,
            two, two_slots, two, two_slots,
            tile, tile_slots, row, rows, parts, tile_slots, row, rows,
            tile, tile_slots, tile_slots, parts, tile_slots, row, rows,
            row, rows,
            pltpu.SemaphoreType.DMA((4,)),
            pltpu.SemaphoreType.DMA((16,)),
            pltpu.SemaphoreType.DMA((16,)),
            pltpu.SemaphoreType.DMA((3, n // 4)),
        ],
        compiler_params=pltpu.CompilerParams(
            collective_id=0, has_side_effects=True, vmem_limit_bytes=56 << 20
        ),
    )(positions, radii[None], basis.transpose(1, 0, 2), rhs)
    return out[0:3, :HALF], out[4:7, :HALF]


def solution(mesh):
    return jax.shard_map(
        functools.partial(body, mesh.shape["row"]),
        mesh=mesh,
        in_specs=(
            P(None, ("row", "col")),
            P(("row", "col")),
            P(None, None, ("row", "col")),
            P(None, ("row", "col")),
        ),
        out_specs=(P(None, ("row", "col")), P(None, ("row", "col"))),
        check_vma=False,
    )
```

```python
import functools
import math

import jax
import jax.numpy as jnp
from jax import lax
from jax.experimental import pallas as pl
from jax.experimental.pallas import tpu as pltpu
from jax.sharding import PartitionSpec as P

MESH = pl.DeviceIdType.MESH
F32 = jnp.float32
BF16 = jnp.bfloat16

far_scale = 1.0 / (8.0 * math.pi)
self_scale = 1.0 / (6.0 * math.pi)

LANES = 128
HALF = 64
PAIRS = ((0, 0), (1, 1), (2, 2), (0, 1), (1, 2), (2, 0))
SLOT = {}
for _slot, (_a, _b) in enumerate(PAIRS):
    SLOT[_a, _b] = _slot
    SLOT[_b, _a] = _slot


def kernel(
    n, vectors,
    pos_ref, rad_ref, basis_ref, rhs_ref,
    out_ref,
    pos_in, rad_in, basis_in, rhs_in, geo, wp,
    grow, gcol, wcol, wrow, src_b, tgt, mob, mob_high, mob_rest, fields, w_tgt, p_tgt, aw_send, aw_recv, aw,
    gram_a, gram_row, gram_b, gram_col,
    vec_a, vec_col_a, stat_a, stat_row_a, part_a, part_row_a, stat_b, stat_col_b,
    vec_c, vec_d, vec_col_c, vec_row_c, part_c, part_row_c, stat_d, stat_col_d,
    stat_f, stat_col_f,
    in_sems, send_sems, recv_sems, chunk_sems,
):
    at_row = lax.axis_index("row")
    at_col = lax.axis_index("col")
    core = lax.rem(at_row, 2)
    y_low = lax.rem(at_col, 2)
    r = lax.div(at_row, 2) * 2 + y_low
    c = lax.div(at_col, 2) * 2 + core

    def row_peer(index):
        return (lax.div(index, 2) * 2 + core, lax.div(at_col, 2) * 2 + lax.rem(index, 2))

    def col_peer(index):
        return (lax.div(at_row, 2) * 2 + lax.rem(index, 2), lax.div(index, 2) * 2 + y_low)

    kh = vectors // 2
    span = n * HALF
    tiles = span // LANES

    barrier = pltpu.get_barrier_semaphore()

    def greet(step, carry):
        pl.semaphore_signal(
            barrier, inc=1, device_id=row_peer(lax.rem(r + step, n)), device_id_type=MESH
        )
        pl.semaphore_signal(
            barrier, inc=1, device_id=col_peer(lax.rem(c + step, n)), device_id_type=MESH
        )
        return carry
    lax.fori_loop(1, n, greet, 0)

    reads = [
        pltpu.make_async_copy(src, dst, in_sems.at[i])
        for i, (src, dst) in enumerate((
            (pos_ref, pos_in), (rad_ref, rad_in), (basis_ref, basis_in), (rhs_ref, rhs_in)
        ))
    ]
    for read in reads:
        read.start()
    for read in reads:
        read.wait()
    for half in range(2):
        lanes = slice(half * HALF, (half + 1) * HALF)
        geo[0:3, lanes] = pos_in[...]
        geo[3:4, lanes] = rad_in[...]
        for axis in range(3):
            wp[kh * axis:kh * (axis + 1), lanes] = basis_in[axis, kh * half:kh * (half + 1), :]

    lane1 = lax.broadcasted_iota(jnp.int32, (1, LANES), 1)
    lane4 = lax.broadcasted_iota(jnp.int32, (4, LANES), 1)
    lane8 = lax.broadcasted_iota(jnp.int32, (8, LANES), 1)
    lane_k = lax.broadcasted_iota(jnp.int32, (kh, LANES), 1)
    row_k = lax.broadcasted_iota(jnp.int32, (kh, LANES), 0)
    low1, low4, low_k = lane1 < HALF, lane4 < HALF, lane_k < HALF

    def swap(x):
        return pltpu.roll(x, HALF, 1)

    def to_row(src, dst, tag):
        def one(step, carry):
            peer = lax.rem(r + step, n)
            pltpu.make_async_remote_copy(
                src_ref=src(peer), dst_ref=dst.at[r], send_sem=send_sems.at[tag],
                recv_sem=recv_sems.at[tag], device_id=row_peer(peer), device_id_type=MESH,
            ).start()
            return carry
        lax.fori_loop(1, n, one, 0)

    def to_col(src, dst, tag):
        def one(step, carry):
            peer = lax.rem(c + step, n)
            pltpu.make_async_remote_copy(
                src_ref=src, dst_ref=dst.at[c], send_sem=send_sems.at[tag],
                recv_sem=recv_sems.at[tag], device_id=col_peer(peer), device_id_type=MESH,
            ).start()
            return carry
        lax.fori_loop(1, n, one, 0)

    chunks = n // 4
    order = sorted(range(chunks), key=lambda k: min(k, chunks - k))

    def to_col_chunks(src, dst, tag, which):
        def one(step, carry):
            peer = lax.rem(c + step, n)
            pltpu.make_async_remote_copy(
                src_ref=src, dst_ref=dst.at[c], send_sem=send_sems.at[tag],
                recv_sem=chunk_sems.at[which, lax.div(c, 4)], device_id=col_peer(peer),
                device_id_type=MESH,
            ).start()
            return carry
        lax.fori_loop(1, n, one, 0)

    def chunk_at(dst, which, step):
        chunk = lax.rem(lax.div(c, 4) + order[step], chunks)
        some = dst.at[pl.ds(0, 3 if step == 0 else 4)]
        pltpu.make_async_copy(some, some, chunk_sems.at[which, chunk]).wait()
        return chunk

    def arrived(dst, tag):
        all_but_one = dst.at[pl.ds(0, n - 1)]
        pltpu.make_async_copy(all_but_one, all_but_one, recv_sems.at[tag]).wait()

    def departed(dst, tag):
        all_but_one = dst.at[pl.ds(0, n - 1)]
        pltpu.make_async_copy(all_but_one, all_but_one, send_sems.at[tag]).wait()

    def total(ref):
        parts = [ref[i] for i in range(n)]
        while len(parts) > 1:
            parts = [parts[i] + parts[i + 1] for i in range(0, len(parts), 2)]
        return parts[0]

    pl.semaphore_wait(barrier, 2 * (n - 1))

    to_col(geo, gcol, 0)
    to_row(lambda peer: geo, grow, 1)
    to_col_chunks(wp, wcol, 2, 0)
    to_row(lambda peer: wp, wrow, 14)
    gcol[c] = geo[...]
    grow[r] = geo[...]
    wcol[c] = wp[...]
    wrow[r] = wp[...]

    def spread(ref, pair, count, place):
        tile = jnp.where(low4, ref[2 * pair], ref[2 * pair + 1])
        turned = jnp.concatenate([tile, tile], axis=0).T
        for axis in range(count):
            src_b[axis, place * LANES:(place + 1) * LANES, :] = jnp.broadcast_to(
                turned[:, axis:axis + 1], (LANES, LANES)
            )

    arrived(gcol, 0)
    for p in range(tiles):
        spread(gcol, p, 4, p)
    arrived(grow, 1)
    for q in range(tiles):
        tgt[:, q * LANES:(q + 1) * LANES] = jnp.where(low4, grow[2 * q], grow[2 * q + 1])

    def split(x):
        high = x.astype(BF16)
        return high, (x - high.astype(F32)).astype(BF16)

    def form_tile(q, carry):
        lanes = pl.ds(pl.multiple_of(q * LANES, LANES), LANES)
        tx, ty, tz, t_rad = [
            jnp.broadcast_to(tgt[axis:axis + 1, lanes], (16, LANES)) for axis in range(4)
        ]
        t_rad_sq = t_rad * t_rad
        own = self_scale / t_rad
        t_rel = lax.broadcasted_iota(jnp.int32, (16, LANES), 1) + (q * LANES - r * HALF)
        t_key = jnp.where(jnp.logical_and(t_rel >= 0, t_rel < HALF), t_rel, -span)
        s_rel0 = lax.broadcasted_iota(jnp.int32, (16, LANES), 0) - c * HALF

        def form_row(i, inner):
            rows = pl.ds(pl.multiple_of(i * 16, 16), 16)
            sx, sy, sz, s_rad = [src_b[axis, rows, :] for axis in range(4)]
            s_rel = s_rel0 + i * 16
            same = s_rel == t_key
            dx, dy, dz = tx - sx, ty - sy, tz - sz
            dist_sq = dx * dx + dy * dy + dz * dz
            inv = lax.rsqrt(jnp.where(same, 1.0, dist_sq))
            inv_sq = inv * inv
            ratio = (t_rad_sq + s_rad * s_rad) * inv_sq
            scaled = far_scale * inv
            iso = jnp.where(same, own, scaled + scaled * (ratio * (1.0 / 3.0)))
            along = (scaled - scaled * ratio) * inv_sq
            ax, ay, az = along * dx, along * dy, along * dz
            for slot, entry in enumerate((
                ax * dx + iso, ay * dy + iso, az * dz + iso, ax * dy, ay * dz, az * dx
            )):
                mob[slot, rows, lanes] = entry
                high, rest = split(entry)
                mob_high[slot, rows, lanes] = high
                mob_rest[slot, rows, lanes] = rest
            return inner
        lax.fori_loop(0, span // 16, form_row, 0, unroll=2)
        return carry
    lax.fori_loop(0, tiles, form_tile, 0)

    def unpack_pair(ref, p, axis):
        first = ref[2 * p, kh * axis:kh * (axis + 1), :]
        second = ref[2 * p + 1, kh * axis:kh * (axis + 1), :]
        return jnp.concatenate(
            [jnp.where(low_k, first, swap(second)), jnp.where(low_k, swap(first), second)], axis=0
        )

    arrived(wrow, 14)
    for p in range(tiles):
        cols = slice(p * LANES, (p + 1) * LANES)
        for axis in range(3):
            high, rest = split(unpack_pair(wrow, p, axis))
            w_tgt[axis, 0:vectors, cols] = high
            w_tgt[axis, vectors:2 * vectors, cols] = rest

    width = 4 * HALF
    for step in range(chunks):
        chunk = chunk_at(wcol, 0, step)
        for part in range(2):
            cols = pl.ds(pl.multiple_of(chunk * width + part * LANES, LANES), LANES)
            for axis in range(3):
                high, rest = split(unpack_pair(wcol, 2 * chunk + part, axis))
                for copy in (axis, axis + 3):
                    if copy < 4:
                        base = 2 * vectors * copy
                        fields[base:base + vectors, cols] = high
                        fields[base + vectors:base + 2 * vectors, cols] = rest

    def basis_chunk(t, carry):
        lanes = pl.ds(pl.multiple_of(t * width, width), width)
        sums = [None] * 3

        def add(axis, value):
            sums[axis] = value if sums[axis] is None else sums[axis] + value
        for slot, (a, b) in enumerate(PAIRS):
            first_row = 2 * vectors * a
            count = 2 * vectors if a == b else 4 * vectors
            lhs = fields[first_row:first_row + count, :]
            by_high = jnp.dot(lhs, mob_high[slot, :, lanes], preferred_element_type=F32)
            by_rest = jnp.dot(lhs, mob_rest[slot, :, lanes], preferred_element_type=F32)
            for base, axis in ((0, b), (2 * vectors, a))[:count // (2 * vectors)]:
                add(axis, by_high[base:base + vectors])
                add(axis, by_high[base + vectors:base + 2 * vectors])
                add(axis, by_rest[base:base + vectors])
        for axis in range(3):
            p_tgt[axis, :, lanes] = sums[axis]
        return carry
    lax.fori_loop(0, span // width, basis_chunk, 0)

    rhs = [jnp.concatenate([rhs_in[axis:axis + 1, :]] * 2, axis=1) for axis in range(3)]
    row32 = lax.broadcasted_iota(jnp.int32, (vectors, LANES), 0)
    lane32 = lax.broadcasted_iota(jnp.int32, (vectors, LANES), 1)

    gram = None
    load = None
    for axis in range(3):
        high, rest = split(p_tgt[axis])
        along_lanes = (((1,), (1,)), ((), ()))
        by_high = lax.dot_general(w_tgt[axis], high, along_lanes, preferred_element_type=F32)
        by_rest = lax.dot_general(
            w_tgt[axis, 0:vectors, :], rest, along_lanes, preferred_element_type=F32
        )
        term = by_high[0:vectors] + by_high[vectors:2 * vectors] + by_rest
        block = wp[kh * axis:kh * (axis + 1), :]
        block = jnp.where(lane32 < HALF, jnp.concatenate([block, swap(block)], axis=0), 0.0)
        load_term = block * rhs[axis]
        gram = term if gram is None else gram + term
        load = load_term if load is None else load + load_term
    load = jnp.sum(load, axis=1, keepdims=True)
    wide = jnp.concatenate([gram, jnp.zeros((vectors, LANES - vectors), F32)], axis=1)
    groups = vectors // 8
    packed = wide[0:8]
    load_tile = jnp.where(lane8 == 0, load[0:8], 0.0)
    for g in range(1, groups):
        packed = packed + pltpu.roll(wide[8 * g:8 * g + 8], vectors * g, 1)
        load_tile = load_tile + jnp.where(lane8 == vectors * g, load[8 * g:8 * g + 8], 0.0)
    gram_a[0:8, :] = packed
    gram_a[8:16, :] = load_tile
    to_row(lambda peer: gram_a, gram_row, 4)
    gram_row[r] = gram_a[...]

    for q in range(tiles):
        for axis in range(3):
            piece = p_tgt[axis, :, q * LANES:(q + 1) * LANES]
            lower, upper = piece[:kh], piece[kh:]
            slot_rows = slice(kh * axis, kh * (axis + 1))
            aw_send[2 * q, slot_rows, :] = jnp.where(low_k, lower, swap(upper))
            aw_send[2 * q + 1, slot_rows, :] = jnp.where(low_k, swap(lower), upper)
    to_row(lambda peer: aw_send.at[peer], aw_recv, 3)
    aw_recv[r] = aw_send[r]
    arrived(gram_row, 4)
    gram_b[...] = total(gram_row)
    to_col(gram_b, gram_col, 5)
    gram_col[c] = gram_b[...]
    arrived(gram_col, 5)
    both = total(gram_col)
    packed, load_tile = both[0:8], both[8:16]
    pieces, load_pieces = [packed], [load_tile]
    for g in range(1, groups):
        pieces.append(pltpu.roll(packed, LANES - vectors * g, 1))
        load_pieces.append(pltpu.roll(load_tile, LANES - vectors * g, 1))
    gram = jnp.concatenate(pieces, axis=0)
    load = jnp.concatenate(load_pieces, axis=0)[:, 0:1]

    system = jnp.where(lane32 < vectors, gram, jnp.where(lane32 == row32 + vectors, 1.0, 0.0))
    system = jnp.where(lane32 == 2 * vectors, load, system)
    for j in range(vectors):
        pivot_row = system[j:j + 1, :]
        scaled_row = pivot_row / pivot_row[:, j:j + 1]
        column = system[:, j:j + 1]
        system = jnp.where(row32 == j, scaled_row, system - column * scaled_row)
    inverse = jnp.where(jnp.logical_and(lane32 >= vectors, lane32 < 2 * vectors), system, 0.0)
    coarse = system[:, 2 * vectors:2 * vectors + 1]

    def weights_of(column):
        return jnp.where(low_k, column[:kh], column[kh:])

    def combine(ref, weights):
        out = []
        for axis in range(3):
            s = jnp.sum(ref[kh * axis:kh * (axis + 1), :] * weights, axis=0, keepdims=True)
            out.append(s + swap(s))
        return out

    def solve(vector_row):
        return weights_of(jnp.sum(inverse * vector_row, axis=1, keepdims=True))

    def dots_row(field):
        s = None
        for axis in range(3):
            term = aw[kh * axis:kh * (axis + 1), :] * field[axis]
            s = term if s is None else s + term
        lower = jnp.sum(jnp.where(low_k, s, 0.0), axis=1, keepdims=True)
        upper = jnp.sum(jnp.where(low_k, 0.0, s), axis=1, keepdims=True)
        spots = jnp.where(lane_k == row_k + vectors, lower, 0.0)
        spots = spots + jnp.where(lane_k == row_k + vectors + kh, upper, 0.0)
        return jnp.sum(spots, axis=0, keepdims=True)

    def dot_local(x, y):
        s = x[0] * y[0] + x[1] * y[1] + x[2] * y[2]
        return jnp.sum(jnp.where(low1, s, 0.0), axis=1, keepdims=True)

    def stat(ref, row_value):
        ref[...] = row_value

    def at_lane(index, value):
        return jnp.where(lane1 == index, value, 0.0)

    def put(ref, field, last):
        for axis in range(3):
            ref[axis:axis + 1, :] = field[axis]
        ref[3:4, :] = last

    def product(vec_all, which, send, weigh, forward):
        zero = jnp.zeros((8, LANES), F32)
        sums = [zero] * (3 * tiles)
        half = 3 * tiles // 2
        for step in range(chunks):
            chunk = chunk_at(vec_all, which, step)
            if step == chunks - 1:
                forward()
            for part in range(2):
                spread(vec_all, 2 * chunk + part, 3, 2 * step + part)
            for part in range(2):
                def one(i, carry, step=step, chunk=chunk, part=part):
                    rows = pl.ds(pl.multiple_of(chunk * width + i * 8, 8), 8)
                    at = pl.ds(pl.multiple_of(step * width + i * 8, 8), 8)
                    value = [src_b[axis, at, :] for axis in range(3)]
                    out = []
                    for q in range(tiles // 2):
                        base = (part * (tiles // 2) + q) * LANES
                        m = [mob[slot, rows, base:base + LANES] for slot in range(6)]
                        for axis in range(3):
                            out.append(
                                carry[3 * q + axis]
                                + (m[SLOT[axis, 0]] * value[0] + m[SLOT[axis, 1]] * value[1])
                                + m[SLOT[axis, 2]] * value[2]
                            )
                    return tuple(out)
                mine_sums = tuple(sums[part * half:(part + 1) * half])
                sums[part * half:(part + 1) * half] = lax.fori_loop(
                    0, width // 8, one, mine_sums, unroll=2
                )
        dots = []
        for q in range(tiles):
            for axis in range(3):
                value = jnp.sum(sums[3 * q + axis], axis=0, keepdims=True)
                send[q, axis:axis + 1, :] = value
                if weigh is not None:
                    weight = jnp.where(
                        low1, weigh[2 * q, axis:axis + 1, :], weigh[2 * q + 1, axis:axis + 1, :]
                    )
                    dots.append(value * weight)
        last = jnp.zeros((1, LANES), F32)
        if weigh is not None:
            while len(dots) > 1:
                dots = [sum(dots[i:i + 2]) for i in range(0, len(dots), 2)]
            last = jnp.broadcast_to(jnp.sum(dots[0], axis=1, keepdims=True), (1, LANES))
        for q in range(tiles):
            send[q, 3:4, :] = last

    def mine(recv):
        tile = total(recv)
        odd = lax.rem(r, 2)
        keep = jnp.where(low1, 1 - odd, odd) == 1
        out = []
        for axis in range(3):
            half = jnp.where(keep, tile[axis:axis + 1, :], 0.0)
            out.append(half + swap(half))
        return out, tile[3:4, :]

    arrived(aw_recv, 3)
    aw[...] = total(aw_recv)
    weights = weights_of(coarse)
    x0 = combine(wp, weights)
    image0 = combine(aw, weights)
    r0 = [rhs[axis] - image0[axis] for axis in range(3)]

    put(vec_a, r0, jnp.zeros((1, LANES), F32))
    to_col_chunks(vec_a, vec_col_a, 6, 1)
    vec_col_a[c] = vec_a[...]
    stat(stat_a, dots_row(r0) + at_lane(0, dot_local(r0, r0)))
    to_row(lambda peer: stat_a, stat_row_a, 7)
    stat_row_a[r] = stat_a[...]

    def forward_a():
        arrived(stat_row_a, 7)
        stat_b[...] = total(stat_row_a)
        to_col(stat_b, stat_col_b, 9)
        stat_col_b[c] = stat_b[...]
    product(vec_col_a, 1, part_a, None, forward_a)
    to_row(lambda peer: part_a.at[lax.div(peer, 2)], part_row_a, 8)
    part_row_a[r] = part_a[lax.div(r, 2)]
    arrived(stat_col_b, 9)
    sums0 = total(stat_col_b)[0:1, :]
    norm0 = sums0[:, 0:1]
    weights = solve(sums0)
    shift = combine(wp, weights)
    d0 = [r0[axis] - shift[axis] for axis in range(3)]
    shift_image = combine(aw, weights)
    arrived(part_row_a, 8)
    z0, _ = mine(part_row_a)
    q0 = [z0[axis] - shift_image[axis] for axis in range(3)]

    put(vec_c, q0, jnp.zeros((1, LANES), F32))
    to_col_chunks(vec_c, vec_col_c, 10, 2)
    vec_col_c[c] = vec_c[...]
    put(
        vec_d, q0,
        dots_row(q0) + at_lane(0, dot_local(d0, q0)) + at_lane(1, dot_local(r0, q0))
        + at_lane(2, dot_local(q0, q0)),
    )
    to_row(lambda peer: vec_d, vec_row_c, 11)
    vec_row_c[r] = vec_d[...]

    def forward_c():
        arrived(vec_row_c, 11)
        stat_d[...] = total(vec_row_c)[3:4, :]
        to_col(stat_d, stat_col_d, 13)
        stat_col_d[c] = stat_d[...]
    product(vec_col_c, 2, part_c, vec_row_c, forward_c)
    to_row(lambda peer: part_c.at[lax.div(peer, 2)], part_row_c, 12)
    part_row_c[r] = part_c[lax.div(r, 2)]
    arrived(stat_col_d, 13)
    sums1 = total(stat_col_d)
    step0 = norm0 / sums1[:, 0:1]
    norm1 = norm0 - 2.0 * step0 * sums1[:, 1:2] + step0 * step0 * sums1[:, 2:3]
    beta = norm1 / norm0
    weights = solve(sums0 - step0 * sums1)
    shift = combine(wp, weights)
    shift_image = combine(aw, weights)
    x1 = [x0[axis] + step0 * d0[axis] for axis in range(3)]
    r1 = [r0[axis] - step0 * q0[axis] for axis in range(3)]
    d1 = [r1[axis] + beta * d0[axis] - shift[axis] for axis in range(3)]
    inner = jnp.sum(inverse * sums1, axis=1, keepdims=True)
    column = jnp.sum(jnp.where(lane32 == row32 + vectors, sums1, 0.0), axis=1, keepdims=True)
    removed = jnp.sum(inner * column, axis=0, keepdims=True)
    factor = 1.0 + beta
    fixed = factor * factor * sums1[:, 0:1] - 2.0 * factor * step0 * sums1[:, 2:3]
    arrived(part_row_c, 12)
    y0, block_sum = mine(part_row_c)
    stat_f[...] = block_sum
    to_col(stat_f, stat_col_f, 15)
    stat_col_f[c] = stat_f[...]
    q1 = [
        (z0[axis] - step0 * y0[axis]) + beta * q0[axis] - shift_image[axis] for axis in range(3)
    ]
    arrived(stat_col_f, 15)
    curvature = fixed + step0 * step0 * (total(stat_col_f)[:, 0:1] - removed)
    step1 = norm1 / curvature
    for axis in range(3):
        out_ref[axis:axis + 1, :] = x1[axis] + step1 * d1[axis]
        out_ref[4 + axis:5 + axis, :] = r1[axis] - step1 * q1[axis]

    for tag, dst in enumerate((
        gcol, grow, wcol, aw_recv, gram_row, gram_col, vec_col_a, stat_row_a, part_row_a,
        stat_col_b, vec_col_c, vec_row_c, part_row_c, stat_col_d, wrow, stat_col_f,
    )):
        departed(dst, tag)


def body(n, positions, radii, basis, rhs):
    vectors = basis.shape[0]
    kh = vectors // 2
    span = n * HALF
    row, rows = pltpu.VMEM((1, LANES), F32), pltpu.VMEM((n, 1, LANES), F32)
    tile, tile_slots = pltpu.VMEM((4, LANES), F32), pltpu.VMEM((n, 4, LANES), F32)
    parts = pltpu.VMEM((span // LANES, 4, LANES), F32)
    field, field_slots = pltpu.VMEM((3 * kh, LANES), F32), pltpu.VMEM((n, 3 * kh, LANES), F32)
    two, two_slots = pltpu.VMEM((16, LANES), F32), pltpu.VMEM((n, 16, LANES), F32)
    vmem = pl.BlockSpec(memory_space=pltpu.VMEM)
    anywhere = pl.BlockSpec(memory_space=pl.ANY)
    out = pl.pallas_call(
        functools.partial(kernel, n, vectors),
        out_shape=jax.ShapeDtypeStruct((8, LANES), F32),
        in_specs=[anywhere] * 4,
        out_specs=vmem,
        scratch_shapes=[
            pltpu.VMEM((3, HALF), F32), pltpu.VMEM((1, HALF), F32),
            pltpu.VMEM((3, vectors, HALF), F32), pltpu.VMEM((3, HALF), F32),
            tile, field,
            tile_slots, tile_slots, field_slots, field_slots,
            pltpu.VMEM((4, span, LANES), F32),
            pltpu.VMEM((4, span), F32),
            pltpu.VMEM((6, span, span), F32),
            pltpu.VMEM((6, span, span), BF16), pltpu.VMEM((6, span, span), BF16),
            pltpu.VMEM((8 * vectors, span), BF16),
            pltpu.VMEM((3, 2 * vectors, span), BF16), pltpu.VMEM((3, vectors, span), F32),
            field_slots, field_slots, field,
            two, two_slots, two, two_slots,
            tile, tile_slots, row, rows, parts, tile_slots, row, rows,
            tile, tile, tile_slots, tile_slots, parts, tile_slots, row, rows,
            row, rows,
            pltpu.SemaphoreType.DMA((4,)),
            pltpu.SemaphoreType.DMA((16,)),
            pltpu.SemaphoreType.DMA((16,)),
            pltpu.SemaphoreType.DMA((3, n // 4)),
        ],
        compiler_params=pltpu.CompilerParams(
            collective_id=0, has_side_effects=True, vmem_limit_bytes=60 << 20
        ),
    )(positions, radii[None], basis.transpose(1, 0, 2), rhs)
    return out[0:3, :HALF], out[4:7, :HALF]


def solution(mesh):
    return jax.shard_map(
        functools.partial(body, mesh.shape["row"]),
        mesh=mesh,
        in_specs=(
            P(None, ("row", "col")),
            P(("row", "col")),
            P(None, None, ("row", "col")),
            P(None, ("row", "col")),
        ),
        out_specs=(P(None, ("row", "col")), P(None, ("row", "col"))),
        check_vma=False,
    )
```

```python
import functools
import math

import jax
import jax.numpy as jnp
from jax import lax
from jax.experimental import pallas as pl
from jax.experimental.pallas import tpu as pltpu
from jax.sharding import PartitionSpec as P

MESH = pl.DeviceIdType.MESH
F32 = jnp.float32
BF16 = jnp.bfloat16

far_scale = 1.0 / (8.0 * math.pi)
self_scale = 1.0 / (6.0 * math.pi)

LANES = 128
HALF = 64
PAIRS = ((0, 0), (1, 1), (2, 2), (0, 1), (1, 2), (2, 0))
SLOT = {}
for _slot, (_a, _b) in enumerate(PAIRS):
    SLOT[_a, _b] = _slot
    SLOT[_b, _a] = _slot


def kernel(
    n, vectors,
    pos_ref, rad_ref, basis_ref, rhs_ref,
    out_ref,
    pos_in, rad_in, basis_in, rhs_in, geo, wp,
    grow, gcol, wcol, wrow, src_b, tgt, mob, mob_high, mob_rest, fields, w_tgt, p_tgt, aw_send, aw_recv, aw,
    gram_a, gram_row, gram_b, gram_col,
    vec_a, vec_col_a, stat_a, stat_row_a, part_a, part_row_a, stat_b, stat_col_b,
    vec_c, vec_d, vec_col_c, vec_row_c, part_c, part_row_c, stat_d, stat_col_d,
    stat_f, stat_col_f,
    in_sems, send_sems, recv_sems, chunk_sems,
):
    at_row = lax.axis_index("row")
    at_col = lax.axis_index("col")
    core = lax.rem(at_row, 2)
    y_low = lax.rem(at_col, 2)
    r = lax.div(at_row, 2) * 2 + y_low
    c = lax.div(at_col, 2) * 2 + core

    def row_peer(index):
        return (lax.div(index, 2) * 2 + core, lax.div(at_col, 2) * 2 + lax.rem(index, 2))

    def col_peer(index):
        return (lax.div(at_row, 2) * 2 + lax.rem(index, 2), lax.div(index, 2) * 2 + y_low)

    kh = vectors // 2
    span = n * HALF
    tiles = span // LANES

    barrier = pltpu.get_barrier_semaphore()

    def greet(step, carry):
        pl.semaphore_signal(
            barrier, inc=1, device_id=row_peer(lax.rem(r + step, n)), device_id_type=MESH
        )
        pl.semaphore_signal(
            barrier, inc=1, device_id=col_peer(lax.rem(c + step, n)), device_id_type=MESH
        )
        return carry
    lax.fori_loop(1, n, greet, 0)

    reads = [
        pltpu.make_async_copy(src, dst, in_sems.at[i])
        for i, (src, dst) in enumerate((
            (pos_ref, pos_in), (rad_ref, rad_in), (basis_ref, basis_in), (rhs_ref, rhs_in)
        ))
    ]
    for read in reads:
        read.start()
    for read in reads:
        read.wait()
    for half in range(2):
        lanes = slice(half * HALF, (half + 1) * HALF)
        geo[0:3, lanes] = pos_in[...]
        geo[3:4, lanes] = rad_in[...]
        for axis in range(3):
            wp[kh * axis:kh * (axis + 1), lanes] = basis_in[axis, kh * half:kh * (half + 1), :]

    lane1 = lax.broadcasted_iota(jnp.int32, (1, LANES), 1)
    lane4 = lax.broadcasted_iota(jnp.int32, (4, LANES), 1)
    lane8 = lax.broadcasted_iota(jnp.int32, (8, LANES), 1)
    lane_k = lax.broadcasted_iota(jnp.int32, (kh, LANES), 1)
    row_k = lax.broadcasted_iota(jnp.int32, (kh, LANES), 0)
    low1, low4, low_k = lane1 < HALF, lane4 < HALF, lane_k < HALF

    def swap(x):
        return pltpu.roll(x, HALF, 1)

    def to_row(src, dst, tag):
        def one(step, carry):
            peer = lax.rem(r + step, n)
            pltpu.make_async_remote_copy(
                src_ref=src(peer), dst_ref=dst.at[r], send_sem=send_sems.at[tag],
                recv_sem=recv_sems.at[tag], device_id=row_peer(peer), device_id_type=MESH,
            ).start()
            return carry
        lax.fori_loop(1, n, one, 0)

    def to_col(src, dst, tag):
        def one(step, carry):
            peer = lax.rem(c + step, n)
            pltpu.make_async_remote_copy(
                src_ref=src, dst_ref=dst.at[c], send_sem=send_sems.at[tag],
                recv_sem=recv_sems.at[tag], device_id=col_peer(peer), device_id_type=MESH,
            ).start()
            return carry
        lax.fori_loop(1, n, one, 0)

    chunks = n // 4
    order = sorted(range(chunks), key=lambda k: min(k, chunks - k))

    def to_col_chunks(src, dst, tag, which):
        def one(step, carry):
            peer = lax.rem(c + step, n)
            pltpu.make_async_remote_copy(
                src_ref=src, dst_ref=dst.at[c], send_sem=send_sems.at[tag],
                recv_sem=chunk_sems.at[which, lax.div(c, 4)], device_id=col_peer(peer),
                device_id_type=MESH,
            ).start()
            return carry
        lax.fori_loop(1, n, one, 0)

    def chunk_at(dst, which, step):
        chunk = lax.rem(lax.div(c, 4) + order[step], chunks)
        some = dst.at[pl.ds(0, 3 if step == 0 else 4)]
        pltpu.make_async_copy(some, some, chunk_sems.at[which, chunk]).wait()
        return chunk

    def arrived(dst, tag):
        all_but_one = dst.at[pl.ds(0, n - 1)]
        pltpu.make_async_copy(all_but_one, all_but_one, recv_sems.at[tag]).wait()

    def departed(dst, tag):
        all_but_one = dst.at[pl.ds(0, n - 1)]
        pltpu.make_async_copy(all_but_one, all_but_one, send_sems.at[tag]).wait()

    def total(ref):
        parts = [ref[i] for i in range(n)]
        while len(parts) > 1:
            parts = [parts[i] + parts[i + 1] for i in range(0, len(parts), 2)]
        return parts[0]

    pl.semaphore_wait(barrier, 2 * (n - 1))

    to_col(geo, gcol, 0)
    to_row(lambda peer: geo, grow, 1)
    to_col_chunks(wp, wcol, 2, 0)
    to_row(lambda peer: wp, wrow, 14)
    gcol[c] = geo[...]
    grow[r] = geo[...]
    wcol[c] = wp[...]
    wrow[r] = wp[...]

    def spread(ref, pair, count, place):
        tile = jnp.where(low4, ref[2 * pair], ref[2 * pair + 1])
        turned = jnp.concatenate([tile, tile], axis=0).T
        for axis in range(count):
            src_b[axis, place * LANES:(place + 1) * LANES, :] = jnp.broadcast_to(
                turned[:, axis:axis + 1], (LANES, LANES)
            )

    arrived(gcol, 0)
    for p in range(tiles):
        spread(gcol, p, 4, p)
    arrived(grow, 1)
    for q in range(tiles):
        tgt[:, q * LANES:(q + 1) * LANES] = jnp.where(low4, grow[2 * q], grow[2 * q + 1])

    def split(x):
        high = x.astype(BF16)
        return high, (x - high.astype(F32)).astype(BF16)

    def form_tile(q, carry):
        lanes = pl.ds(pl.multiple_of(q * LANES, LANES), LANES)
        tx, ty, tz, t_rad = [
            jnp.broadcast_to(tgt[axis:axis + 1, lanes], (8, LANES)) for axis in range(4)
        ]
        t_rad_sq = t_rad * t_rad
        own = self_scale / t_rad
        t_rel = lane8 + (q * LANES - r * HALF)
        t_key = jnp.where(jnp.logical_and(t_rel >= 0, t_rel < HALF), t_rel, -span)
        s_rel0 = lax.broadcasted_iota(jnp.int32, (8, LANES), 0) - c * HALF

        def form_row(i, inner):
            rows = pl.ds(pl.multiple_of(i * 8, 8), 8)
            sx, sy, sz, s_rad = [src_b[axis, rows, :] for axis in range(4)]
            s_rel = s_rel0 + i * 8
            same = s_rel == t_key
            dx, dy, dz = tx - sx, ty - sy, tz - sz
            dist_sq = dx * dx + dy * dy + dz * dz
            inv = lax.rsqrt(jnp.where(same, 1.0, dist_sq))
            inv_sq = inv * inv
            ratio = (t_rad_sq + s_rad * s_rad) * inv_sq
            scaled = far_scale * inv
            iso = jnp.where(same, own, scaled + scaled * (ratio * (1.0 / 3.0)))
            along = (scaled - scaled * ratio) * inv_sq
            ax, ay, az = along * dx, along * dy, along * dz
            mob[0, rows, lanes] = ax * dx + iso
            mob[1, rows, lanes] = ay * dy + iso
            mob[2, rows, lanes] = az * dz + iso
            mob[3, rows, lanes] = ax * dy
            mob[4, rows, lanes] = ay * dz
            mob[5, rows, lanes] = az * dx
            return inner
        lax.fori_loop(0, span // 8, form_row, 0, unroll=4)
        return carry
    lax.fori_loop(0, tiles, form_tile, 0)

    def split_rows(i, carry):
        rows = pl.ds(pl.multiple_of(i * 16, 16), 16)
        for slot in range(6):
            high, rest = split(mob[slot, rows, :])
            mob_high[slot, rows, :] = high
            mob_rest[slot, rows, :] = rest
        return carry
    lax.fori_loop(0, span // 16, split_rows, 0)

    def unpack_pair(ref, p, axis):
        first = ref[2 * p, kh * axis:kh * (axis + 1), :]
        second = ref[2 * p + 1, kh * axis:kh * (axis + 1), :]
        return jnp.concatenate(
            [jnp.where(low_k, first, swap(second)), jnp.where(low_k, swap(first), second)], axis=0
        )

    arrived(wrow, 14)
    for p in range(tiles):
        cols = slice(p * LANES, (p + 1) * LANES)
        for axis in range(3):
            high, rest = split(unpack_pair(wrow, p, axis))
            w_tgt[axis, 0:vectors, cols] = high
            w_tgt[axis, vectors:2 * vectors, cols] = rest

    width = 4 * HALF
    for step in range(chunks):
        chunk = chunk_at(wcol, 0, step)
        for part in range(2):
            cols = pl.ds(pl.multiple_of(chunk * width + part * LANES, LANES), LANES)
            for axis in range(3):
                high, rest = split(unpack_pair(wcol, 2 * chunk + part, axis))
                for copy in (axis, axis + 3):
                    if copy < 4:
                        base = 2 * vectors * copy
                        fields[base:base + vectors, cols] = high
                        fields[base + vectors:base + 2 * vectors, cols] = rest

    def basis_chunk(t, carry):
        lanes = pl.ds(pl.multiple_of(t * width, width), width)
        sums = [None] * 3

        def add(axis, value):
            sums[axis] = value if sums[axis] is None else sums[axis] + value
        for slot, (a, b) in enumerate(PAIRS):
            first_row = 2 * vectors * a
            count = 2 * vectors if a == b else 4 * vectors
            lhs = fields[first_row:first_row + count, :]
            by_high = jnp.dot(lhs, mob_high[slot, :, lanes], preferred_element_type=F32)
            by_rest = jnp.dot(lhs, mob_rest[slot, :, lanes], preferred_element_type=F32)
            for base, axis in ((0, b), (2 * vectors, a))[:count // (2 * vectors)]:
                add(axis, by_high[base:base + vectors])
                add(axis, by_high[base + vectors:base + 2 * vectors])
                add(axis, by_rest[base:base + vectors])
        for axis in range(3):
            p_tgt[axis, :, lanes] = sums[axis]
        return carry
    lax.fori_loop(0, span // width, basis_chunk, 0)

    rhs = [jnp.concatenate([rhs_in[axis:axis + 1, :]] * 2, axis=1) for axis in range(3)]
    row32 = lax.broadcasted_iota(jnp.int32, (vectors, LANES), 0)
    lane32 = lax.broadcasted_iota(jnp.int32, (vectors, LANES), 1)

    gram = None
    load = None
    for axis in range(3):
        high, rest = split(p_tgt[axis])
        along_lanes = (((1,), (1,)), ((), ()))
        by_high = lax.dot_general(w_tgt[axis], high, along_lanes, preferred_element_type=F32)
        by_rest = lax.dot_general(
            w_tgt[axis, 0:vectors, :], rest, along_lanes, preferred_element_type=F32
        )
        term = by_high[0:vectors] + by_high[vectors:2 * vectors] + by_rest
        block = wp[kh * axis:kh * (axis + 1), :]
        block = jnp.where(lane32 < HALF, jnp.concatenate([block, swap(block)], axis=0), 0.0)
        load_term = block * rhs[axis]
        gram = term if gram is None else gram + term
        load = load_term if load is None else load + load_term
    load = jnp.sum(load, axis=1, keepdims=True)
    wide = jnp.concatenate([gram, jnp.zeros((vectors, LANES - vectors), F32)], axis=1)
    groups = vectors // 8
    packed = wide[0:8]
    load_tile = jnp.where(lane8 == 0, load[0:8], 0.0)
    for g in range(1, groups):
        packed = packed + pltpu.roll(wide[8 * g:8 * g + 8], vectors * g, 1)
        load_tile = load_tile + jnp.where(lane8 == vectors * g, load[8 * g:8 * g + 8], 0.0)
    gram_a[0:8, :] = packed
    gram_a[8:16, :] = load_tile
    to_row(lambda peer: gram_a, gram_row, 4)
    gram_row[r] = gram_a[...]

    for q in range(tiles):
        for axis in range(3):
            piece = p_tgt[axis, :, q * LANES:(q + 1) * LANES]
            lower, upper = piece[:kh], piece[kh:]
            slot_rows = slice(kh * axis, kh * (axis + 1))
            aw_send[2 * q, slot_rows, :] = jnp.where(low_k, lower, swap(upper))
            aw_send[2 * q + 1, slot_rows, :] = jnp.where(low_k, swap(lower), upper)
    to_row(lambda peer: aw_send.at[peer], aw_recv, 3)
    aw_recv[r] = aw_send[r]
    arrived(gram_row, 4)
    gram_b[...] = total(gram_row)
    to_col(gram_b, gram_col, 5)
    gram_col[c] = gram_b[...]
    arrived(gram_col, 5)
    both = total(gram_col)
    packed, load_tile = both[0:8], both[8:16]
    pieces, load_pieces = [packed], [load_tile]
    for g in range(1, groups):
        pieces.append(pltpu.roll(packed, LANES - vectors * g, 1))
        load_pieces.append(pltpu.roll(load_tile, LANES - vectors * g, 1))
    gram = jnp.concatenate(pieces, axis=0)
    load = jnp.concatenate(load_pieces, axis=0)[:, 0:1]

    system = jnp.where(lane32 < vectors, gram, jnp.where(lane32 == row32 + vectors, 1.0, 0.0))
    system = jnp.where(lane32 == 2 * vectors, load, system)
    for j in range(0, vectors, 2):
        first, second = system[j:j + 1, :], system[j + 1:j + 2, :]
        column0, column1 = system[:, j:j + 1], system[:, j + 1:j + 2]
        p00, p01 = first[:, j:j + 1], first[:, j + 1:j + 2]
        p10, p11 = second[:, j:j + 1], second[:, j + 1:j + 2]
        inverse0 = 1.0 / p00
        ahead = p01 * inverse0
        inverse1 = 1.0 / (p11 - p10 * ahead)
        scaled = first * inverse0
        new1 = (second - p10 * scaled) * inverse1
        new0 = scaled - ahead * new1
        system = jnp.where(
            row32 == j, new0,
            jnp.where(row32 == j + 1, new1, system - column0 * new0 - column1 * new1),
        )
    inverse = jnp.where(jnp.logical_and(lane32 >= vectors, lane32 < 2 * vectors), system, 0.0)
    coarse = system[:, 2 * vectors:2 * vectors + 1]

    def weights_of(column):
        return jnp.where(low_k, column[:kh], column[kh:])

    def combine(ref, weights):
        out = []
        for axis in range(3):
            s = jnp.sum(ref[kh * axis:kh * (axis + 1), :] * weights, axis=0, keepdims=True)
            out.append(s + swap(s))
        return out

    def solve(vector_row):
        return weights_of(jnp.sum(inverse * vector_row, axis=1, keepdims=True))

    def dots_row(field):
        s = None
        for axis in range(3):
            term = aw[kh * axis:kh * (axis + 1), :] * field[axis]
            s = term if s is None else s + term
        lower = jnp.sum(jnp.where(low_k, s, 0.0), axis=1, keepdims=True)
        upper = jnp.sum(jnp.where(low_k, 0.0, s), axis=1, keepdims=True)
        spots = jnp.where(lane_k == row_k + vectors, lower, 0.0)
        spots = spots + jnp.where(lane_k == row_k + vectors + kh, upper, 0.0)
        return jnp.sum(spots, axis=0, keepdims=True)

    def dot_local(x, y):
        s = x[0] * y[0] + x[1] * y[1] + x[2] * y[2]
        return jnp.sum(jnp.where(low1, s, 0.0), axis=1, keepdims=True)

    def stat(ref, row_value):
        ref[...] = row_value

    def at_lane(index, value):
        return jnp.where(lane1 == index, value, 0.0)

    def put(ref, field, last):
        for axis in range(3):
            ref[axis:axis + 1, :] = field[axis]
        ref[3:4, :] = last

    def product(vec_all, which, send, weigh, forward):
        zero = jnp.zeros((8, LANES), F32)
        sums = [zero] * (3 * tiles)
        half = 3 * tiles // 2
        for step in range(chunks):
            chunk = chunk_at(vec_all, which, step)
            for part in range(2):
                spread(vec_all, 2 * chunk + part, 3, 2 * step + part)
            for part in range(2):
                def one(i, carry, step=step, chunk=chunk, part=part):
                    rows = pl.ds(pl.multiple_of(chunk * width + i * 8, 8), 8)
                    at = pl.ds(pl.multiple_of(step * width + i * 8, 8), 8)
                    value = [src_b[axis, at, :] for axis in range(3)]
                    out = []
                    for q in range(tiles // 2):
                        base = (part * (tiles // 2) + q) * LANES
                        m = [mob[slot, rows, base:base + LANES] for slot in range(6)]
                        for axis in range(3):
                            out.append(
                                carry[3 * q + axis]
                                + (m[SLOT[axis, 0]] * value[0] + m[SLOT[axis, 1]] * value[1])
                                + m[SLOT[axis, 2]] * value[2]
                            )
                    return tuple(out)
                mine_sums = tuple(sums[part * half:(part + 1) * half])
                sums[part * half:(part + 1) * half] = lax.fori_loop(
                    0, width // 8, one, mine_sums, unroll=2
                )
        forward()
        dots = []
        for q in range(tiles):
            for axis in range(3):
                value = jnp.sum(sums[3 * q + axis], axis=0, keepdims=True)
                send[q, axis:axis + 1, :] = value
                if weigh is not None:
                    weight = jnp.where(
                        low1, weigh[2 * q, axis:axis + 1, :], weigh[2 * q + 1, axis:axis + 1, :]
                    )
                    dots.append(value * weight)
        last = jnp.zeros((1, LANES), F32)
        if weigh is not None:
            while len(dots) > 1:
                dots = [sum(dots[i:i + 2]) for i in range(0, len(dots), 2)]
            last = jnp.broadcast_to(jnp.sum(dots[0], axis=1, keepdims=True), (1, LANES))
        for q in range(tiles):
            send[q, 3:4, :] = last

    def mine(recv):
        tile = total(recv)
        odd = lax.rem(r, 2)
        keep = jnp.where(low1, 1 - odd, odd) == 1
        out = []
        for axis in range(3):
            half = jnp.where(keep, tile[axis:axis + 1, :], 0.0)
            out.append(half + swap(half))
        return out, tile[3:4, :]

    arrived(aw_recv, 3)
    aw[...] = total(aw_recv)
    weights = weights_of(coarse)
    x0 = combine(wp, weights)
    image0 = combine(aw, weights)
    r0 = [rhs[axis] - image0[axis] for axis in range(3)]

    put(vec_a, r0, jnp.zeros((1, LANES), F32))
    to_col_chunks(vec_a, vec_col_a, 6, 1)
    vec_col_a[c] = vec_a[...]
    stat(stat_a, dots_row(r0) + at_lane(0, dot_local(r0, r0)))
    to_row(lambda peer: stat_a, stat_row_a, 7)
    stat_row_a[r] = stat_a[...]

    def forward_a():
        arrived(stat_row_a, 7)
        stat_b[...] = total(stat_row_a)
        to_col(stat_b, stat_col_b, 9)
        stat_col_b[c] = stat_b[...]
    product(vec_col_a, 1, part_a, None, forward_a)
    to_row(lambda peer: part_a.at[lax.div(peer, 2)], part_row_a, 8)
    part_row_a[r] = part_a[lax.div(r, 2)]
    arrived(stat_col_b, 9)
    sums0 = total(stat_col_b)[0:1, :]
    norm0 = sums0[:, 0:1]
    weights = solve(sums0)
    shift = combine(wp, weights)
    d0 = [r0[axis] - shift[axis] for axis in range(3)]
    shift_image = combine(aw, weights)
    arrived(part_row_a, 8)
    z0, _ = mine(part_row_a)
    q0 = [z0[axis] - shift_image[axis] for axis in range(3)]

    put(vec_c, q0, jnp.zeros((1, LANES), F32))
    to_col_chunks(vec_c, vec_col_c, 10, 2)
    vec_col_c[c] = vec_c[...]
    put(
        vec_d, q0,
        dots_row(q0) + at_lane(0, dot_local(d0, q0)) + at_lane(1, dot_local(r0, q0))
        + at_lane(2, dot_local(q0, q0)),
    )
    to_row(lambda peer: vec_d, vec_row_c, 11)
    vec_row_c[r] = vec_d[...]

    def forward_c():
        arrived(vec_row_c, 11)
        stat_d[...] = total(vec_row_c)[3:4, :]
        to_col(stat_d, stat_col_d, 13)
        stat_col_d[c] = stat_d[...]
    product(vec_col_c, 2, part_c, vec_row_c, forward_c)
    to_row(lambda peer: part_c.at[lax.div(peer, 2)], part_row_c, 12)
    part_row_c[r] = part_c[lax.div(r, 2)]
    arrived(stat_col_d, 13)
    sums1 = total(stat_col_d)
    step0 = norm0 / sums1[:, 0:1]
    norm1 = norm0 - 2.0 * step0 * sums1[:, 1:2] + step0 * step0 * sums1[:, 2:3]
    beta = norm1 / norm0
    weights = solve(sums0 - step0 * sums1)
    shift = combine(wp, weights)
    shift_image = combine(aw, weights)
    x1 = [x0[axis] + step0 * d0[axis] for axis in range(3)]
    r1 = [r0[axis] - step0 * q0[axis] for axis in range(3)]
    d1 = [r1[axis] + beta * d0[axis] - shift[axis] for axis in range(3)]
    inner = jnp.sum(inverse * sums1, axis=1, keepdims=True)
    column = jnp.sum(jnp.where(lane32 == row32 + vectors, sums1, 0.0), axis=1, keepdims=True)
    removed = jnp.sum(inner * column, axis=0, keepdims=True)
    factor = 1.0 + beta
    fixed = factor * factor * sums1[:, 0:1] - 2.0 * factor * step0 * sums1[:, 2:3]
    arrived(part_row_c, 12)
    y0, block_sum = mine(part_row_c)
    stat_f[...] = block_sum
    to_col(stat_f, stat_col_f, 15)
    stat_col_f[c] = stat_f[...]
    q1 = [
        (z0[axis] - step0 * y0[axis]) + beta * q0[axis] - shift_image[axis] for axis in range(3)
    ]
    arrived(stat_col_f, 15)
    curvature = fixed + step0 * step0 * (total(stat_col_f)[:, 0:1] - removed)
    step1 = norm1 / curvature
    for axis in range(3):
        out_ref[axis:axis + 1, :] = x1[axis] + step1 * d1[axis]
        out_ref[4 + axis:5 + axis, :] = r1[axis] - step1 * q1[axis]

    for tag, dst in enumerate((
        gcol, grow, wcol, aw_recv, gram_row, gram_col, vec_col_a, stat_row_a, part_row_a,
        stat_col_b, vec_col_c, vec_row_c, part_row_c, stat_col_d, wrow, stat_col_f,
    )):
        departed(dst, tag)


def body(n, positions, radii, basis, rhs):
    vectors = basis.shape[0]
    kh = vectors // 2
    span = n * HALF
    row, rows = pltpu.VMEM((1, LANES), F32), pltpu.VMEM((n, 1, LANES), F32)
    tile, tile_slots = pltpu.VMEM((4, LANES), F32), pltpu.VMEM((n, 4, LANES), F32)
    parts = pltpu.VMEM((span // LANES, 4, LANES), F32)
    field, field_slots = pltpu.VMEM((3 * kh, LANES), F32), pltpu.VMEM((n, 3 * kh, LANES), F32)
    two, two_slots = pltpu.VMEM((16, LANES), F32), pltpu.VMEM((n, 16, LANES), F32)
    vmem = pl.BlockSpec(memory_space=pltpu.VMEM)
    anywhere = pl.BlockSpec(memory_space=pl.ANY)
    out = pl.pallas_call(
        functools.partial(kernel, n, vectors),
        out_shape=jax.ShapeDtypeStruct((8, LANES), F32),
        in_specs=[anywhere] * 4,
        out_specs=vmem,
        scratch_shapes=[
            pltpu.VMEM((3, HALF), F32), pltpu.VMEM((1, HALF), F32),
            pltpu.VMEM((3, vectors, HALF), F32), pltpu.VMEM((3, HALF), F32),
            tile, field,
            tile_slots, tile_slots, field_slots, field_slots,
            pltpu.VMEM((4, span, LANES), F32),
            pltpu.VMEM((4, span), F32),
            pltpu.VMEM((6, span, span), F32),
            pltpu.VMEM((6, span, span), BF16), pltpu.VMEM((6, span, span), BF16),
            pltpu.VMEM((8 * vectors, span), BF16),
            pltpu.VMEM((3, 2 * vectors, span), BF16), pltpu.VMEM((3, vectors, span), F32),
            field_slots, field_slots, field,
            two, two_slots, two, two_slots,
            tile, tile_slots, row, rows, parts, tile_slots, row, rows,
            tile, tile, tile_slots, tile_slots, parts, tile_slots, row, rows,
            row, rows,
            pltpu.SemaphoreType.DMA((4,)),
            pltpu.SemaphoreType.DMA((16,)),
            pltpu.SemaphoreType.DMA((16,)),
            pltpu.SemaphoreType.DMA((3, n // 4)),
        ],
        compiler_params=pltpu.CompilerParams(
            collective_id=0, has_side_effects=True, vmem_limit_bytes=60 << 20
        ),
    )(positions, radii[None], basis.transpose(1, 0, 2), rhs)
    return out[0:3, :HALF], out[4:7, :HALF]


def solution(mesh):
    return jax.shard_map(
        functools.partial(body, mesh.shape["row"]),
        mesh=mesh,
        in_specs=(
            P(None, ("row", "col")),
            P(("row", "col")),
            P(None, None, ("row", "col")),
            P(None, ("row", "col")),
        ),
        out_specs=(P(None, ("row", "col")), P(None, ("row", "col"))),
        check_vma=False,
    )
```

```python
import functools
import math

import jax
import jax.numpy as jnp
from jax import lax
from jax.experimental import pallas as pl
from jax.experimental.pallas import tpu as pltpu
from jax.sharding import PartitionSpec as P

MESH = pl.DeviceIdType.MESH
F32 = jnp.float32
BF16 = jnp.bfloat16

far_scale = 1.0 / (8.0 * math.pi)
self_scale = 1.0 / (6.0 * math.pi)

LANES = 128
HALF = 64
PAIRS = ((0, 0), (1, 1), (2, 2), (0, 1), (1, 2), (2, 0))
SLOT = {}
for _slot, (_a, _b) in enumerate(PAIRS):
    SLOT[_a, _b] = _slot
    SLOT[_b, _a] = _slot


def kernel(
    n, vectors,
    pos_ref, rad_ref, basis_ref, rhs_ref,
    out_ref,
    pos_in, rad_in, basis_in, rhs_in, geo, wp,
    grow, gcol, wcol, wrow, src_b, tgt, mob, fields, w_tgt, p_tgt, aw_send, aw_recv, aw,
    gram_a, gram_row, gram_b, gram_col,
    vec_a, vec_col_a, stat_a, stat_row_a, part_a, part_row_a, stat_b, stat_col_b,
    vec_c, vec_d, vec_col_c, vec_row_c, part_c, part_row_c, stat_d, stat_col_d,
    stat_f, stat_col_f,
    in_sems, send_sems, recv_sems, chunk_sems,
):
    at_row = lax.axis_index("row")
    at_col = lax.axis_index("col")
    core = lax.rem(at_row, 2)
    y_low = lax.rem(at_col, 2)
    r = lax.div(at_row, 2) * 2 + y_low
    c = lax.div(at_col, 2) * 2 + core

    def row_peer(index):
        return (lax.div(index, 2) * 2 + core, lax.div(at_col, 2) * 2 + lax.rem(index, 2))

    def col_peer(index):
        return (lax.div(at_row, 2) * 2 + lax.rem(index, 2), lax.div(index, 2) * 2 + y_low)

    kh = vectors // 2
    span = n * HALF
    tiles = span // LANES

    barrier = pltpu.get_barrier_semaphore()

    def greet(step, carry):
        pl.semaphore_signal(
            barrier, inc=1, device_id=row_peer(lax.rem(r + step, n)), device_id_type=MESH
        )
        pl.semaphore_signal(
            barrier, inc=1, device_id=col_peer(lax.rem(c + step, n)), device_id_type=MESH
        )
        return carry
    lax.fori_loop(1, n, greet, 0)

    reads = [
        pltpu.make_async_copy(src, dst, in_sems.at[i])
        for i, (src, dst) in enumerate((
            (pos_ref, pos_in), (rad_ref, rad_in), (basis_ref, basis_in), (rhs_ref, rhs_in)
        ))
    ]
    for read in reads:
        read.start()
    for read in reads:
        read.wait()
    for half in range(2):
        lanes = slice(half * HALF, (half + 1) * HALF)
        geo[0:3, lanes] = pos_in[...]
        geo[3:4, lanes] = rad_in[...]
        for axis in range(3):
            wp[kh * axis:kh * (axis + 1), lanes] = basis_in[axis, kh * half:kh * (half + 1), :]

    lane1 = lax.broadcasted_iota(jnp.int32, (1, LANES), 1)
    lane4 = lax.broadcasted_iota(jnp.int32, (4, LANES), 1)
    lane8 = lax.broadcasted_iota(jnp.int32, (8, LANES), 1)
    lane_k = lax.broadcasted_iota(jnp.int32, (kh, LANES), 1)
    row_k = lax.broadcasted_iota(jnp.int32, (kh, LANES), 0)
    low1, low4, low_k = lane1 < HALF, lane4 < HALF, lane_k < HALF

    def swap(x):
        return pltpu.roll(x, HALF, 1)

    def to_row(src, dst, tag):
        def one(step, carry):
            peer = lax.rem(r + step, n)
            pltpu.make_async_remote_copy(
                src_ref=src(peer), dst_ref=dst.at[r], send_sem=send_sems.at[tag],
                recv_sem=recv_sems.at[tag], device_id=row_peer(peer), device_id_type=MESH,
            ).start()
            return carry
        lax.fori_loop(1, n, one, 0)

    def to_col(src, dst, tag):
        def one(step, carry):
            peer = lax.rem(c + step, n)
            pltpu.make_async_remote_copy(
                src_ref=src, dst_ref=dst.at[c], send_sem=send_sems.at[tag],
                recv_sem=recv_sems.at[tag], device_id=col_peer(peer), device_id_type=MESH,
            ).start()
            return carry
        lax.fori_loop(1, n, one, 0)

    chunks = n // 4
    order = sorted(range(chunks), key=lambda k: min(k, chunks - k))

    def to_col_chunks(src, dst, tag, which):
        def one(step, carry):
            peer = lax.rem(c + step, n)
            pltpu.make_async_remote_copy(
                src_ref=src, dst_ref=dst.at[c], send_sem=send_sems.at[tag],
                recv_sem=chunk_sems.at[which, lax.div(c, 4)], device_id=col_peer(peer),
                device_id_type=MESH,
            ).start()
            return carry
        lax.fori_loop(1, n, one, 0)

    def chunk_at(dst, which, step):
        chunk = lax.rem(lax.div(c, 4) + order[step], chunks)
        some = dst.at[pl.ds(0, 3 if step == 0 else 4)]
        pltpu.make_async_copy(some, some, chunk_sems.at[which, chunk]).wait()
        return chunk

    def arrived(dst, tag):
        all_but_one = dst.at[pl.ds(0, n - 1)]
        pltpu.make_async_copy(all_but_one, all_but_one, recv_sems.at[tag]).wait()

    def departed(dst, tag):
        all_but_one = dst.at[pl.ds(0, n - 1)]
        pltpu.make_async_copy(all_but_one, all_but_one, send_sems.at[tag]).wait()

    def total(ref):
        parts = [ref[i] for i in range(n)]
        while len(parts) > 1:
            parts = [parts[i] + parts[i + 1] for i in range(0, len(parts), 2)]
        return parts[0]

    pl.semaphore_wait(barrier, 2 * (n - 1))

    to_col_chunks(geo, gcol, 0, 3)
    to_row(lambda peer: geo, grow, 1)
    to_col_chunks(wp, wcol, 2, 0)
    to_row(lambda peer: wp, wrow, 14)
    gcol[c] = geo[...]
    grow[r] = geo[...]
    wcol[c] = wp[...]
    wrow[r] = wp[...]

    def spread(ref, pair, count, place):
        tile = jnp.where(low4, ref[2 * pair], ref[2 * pair + 1])
        turned = jnp.concatenate([tile, tile], axis=0).T
        for axis in range(count):
            src_b[axis, pl.ds(pl.multiple_of(place * LANES, LANES), LANES), :] = jnp.broadcast_to(
                turned[:, axis:axis + 1], (LANES, LANES)
            )

    for step in range(chunks):
        chunk = chunk_at(gcol, 3, step)
        for part in range(2):
            spread(gcol, 2 * chunk + part, 4, 2 * chunk + part)
    arrived(grow, 1)
    for q in range(tiles):
        tgt[:, q * LANES:(q + 1) * LANES] = jnp.where(low4, grow[2 * q], grow[2 * q + 1])

    def split(x):
        high = x.astype(BF16)
        return high, (x - high.astype(F32)).astype(BF16)

    def target_tile(q):
        lanes = pl.ds(pl.multiple_of(q * LANES, LANES), LANES)
        return lanes, [
            jnp.broadcast_to(tgt[axis:axis + 1, lanes], (8, LANES)) for axis in range(4)
        ]

    def form(rows, lanes, target, target_sq, patch):
        sx, sy, sz, s_rad = [src_b[axis, rows, :] for axis in range(4)]
        dx, dy, dz = target[0] - sx, target[1] - sy, target[2] - sz
        dist_sq = dx * dx + dy * dy + dz * dz
        if patch is not None:
            dist_sq = jnp.where(patch, 1.0, dist_sq)
        inv = lax.rsqrt(dist_sq)
        inv_sq = inv * inv
        scaled = far_scale * inv
        sized = scaled * ((target_sq + s_rad * s_rad) * inv_sq)
        iso = scaled + sized * (1.0 / 3.0)
        if patch is not None:
            iso = jnp.where(patch, self_scale / target[3], iso)
        along = (scaled - sized) * inv_sq
        ax, ay, az = along * dx, along * dy, along * dz
        mob[0, rows, lanes] = ax * dx + iso
        mob[1, rows, lanes] = ay * dy + iso
        mob[2, rows, lanes] = az * dz + iso
        mob[3, rows, lanes] = ax * dy
        mob[4, rows, lanes] = ay * dz
        mob[5, rows, lanes] = az * dx

    def form_tile(q, carry):
        lanes, target = target_tile(q)
        target_sq = target[3] * target[3]

        def form_row(i, inner):
            form(pl.ds(pl.multiple_of(i * 8, 8), 8), lanes, target, target_sq, None)
            return inner
        lax.fori_loop(0, span // 8, form_row, 0, unroll=8)
        return carry
    lax.fori_loop(0, tiles, form_tile, 0)

    lanes, target = target_tile(lax.div(r, 2))
    at_own = lane8 - lax.rem(r, 2) * HALF
    for i in range(HALF // 8):
        same = lax.broadcasted_iota(jnp.int32, (8, LANES), 0) + 8 * i == at_own
        form(
            pl.ds(pl.multiple_of(c * HALF + 8 * i, 8), 8), lanes, target,
            target[3] * target[3], same,
        )

    def unpack_pair(ref, p, axis):
        first = ref[2 * p, kh * axis:kh * (axis + 1), :]
        second = ref[2 * p + 1, kh * axis:kh * (axis + 1), :]
        return jnp.concatenate(
            [jnp.where(low_k, first, swap(second)), jnp.where(low_k, swap(first), second)], axis=0
        )

    arrived(wrow, 14)
    for p in range(tiles):
        cols = slice(p * LANES, (p + 1) * LANES)
        for axis in range(3):
            high, rest = split(unpack_pair(wrow, p, axis))
            w_tgt[axis, 0:vectors, cols] = high
            w_tgt[axis, vectors:2 * vectors, cols] = rest

    width = 4 * HALF
    for step in range(chunks):
        chunk = chunk_at(wcol, 0, step)
        for part in range(2):
            cols = pl.ds(pl.multiple_of(chunk * width + part * LANES, LANES), LANES)
            for axis in range(3):
                high, rest = split(unpack_pair(wcol, 2 * chunk + part, axis))
                for copy in (axis, axis + 3):
                    if copy < 4:
                        base = 2 * vectors * copy
                        fields[base:base + vectors, cols] = high
                        fields[base + vectors:base + 2 * vectors, cols] = rest

    def basis_chunk(t, carry):
        lanes = pl.ds(pl.multiple_of(t * width, width), width)
        sums = [None] * 3

        def add(axis, value):
            sums[axis] = value if sums[axis] is None else sums[axis] + value
        for slot, (a, b) in enumerate(PAIRS):
            first_row = 2 * vectors * a
            count = 2 * vectors if a == b else 4 * vectors
            by_high = by_rest = None
            for d in range(chunks):
                high, rest = split(mob[slot, d * width:(d + 1) * width, lanes])
                lhs = fields[first_row:first_row + count, d * width:(d + 1) * width]
                dot_high = jnp.dot(lhs, high, preferred_element_type=F32)
                dot_rest = jnp.dot(lhs, rest, preferred_element_type=F32)
                by_high = dot_high if by_high is None else by_high + dot_high
                by_rest = dot_rest if by_rest is None else by_rest + dot_rest
            for base, axis in ((0, b), (2 * vectors, a))[:count // (2 * vectors)]:
                add(axis, by_high[base:base + vectors])
                add(axis, by_high[base + vectors:base + 2 * vectors])
                add(axis, by_rest[base:base + vectors])
        for axis in range(3):
            p_tgt[axis, :, lanes] = sums[axis]
        return carry
    lax.fori_loop(0, span // width, basis_chunk, 0)

    rhs = [jnp.concatenate([rhs_in[axis:axis + 1, :]] * 2, axis=1) for axis in range(3)]
    row32 = lax.broadcasted_iota(jnp.int32, (vectors, LANES), 0)
    lane32 = lax.broadcasted_iota(jnp.int32, (vectors, LANES), 1)

    gram = None
    load = None
    for axis in range(3):
        high, rest = split(p_tgt[axis])
        along_lanes = (((1,), (1,)), ((), ()))
        by_high = lax.dot_general(w_tgt[axis], high, along_lanes, preferred_element_type=F32)
        by_rest = lax.dot_general(
            w_tgt[axis, 0:vectors, :], rest, along_lanes, preferred_element_type=F32
        )
        term = by_high[0:vectors] + by_high[vectors:2 * vectors] + by_rest
        block = wp[kh * axis:kh * (axis + 1), :]
        block = jnp.where(lane32 < HALF, jnp.concatenate([block, swap(block)], axis=0), 0.0)
        load_term = block * rhs[axis]
        gram = term if gram is None else gram + term
        load = load_term if load is None else load + load_term
    load = jnp.sum(load, axis=1, keepdims=True)
    wide = jnp.concatenate([gram, jnp.zeros((vectors, LANES - vectors), F32)], axis=1)
    groups = vectors // 8
    packed = wide[0:8]
    load_tile = jnp.where(lane8 == 0, load[0:8], 0.0)
    for g in range(1, groups):
        packed = packed + pltpu.roll(wide[8 * g:8 * g + 8], vectors * g, 1)
        load_tile = load_tile + jnp.where(lane8 == vectors * g, load[8 * g:8 * g + 8], 0.0)
    gram_a[0:8, :] = packed
    gram_a[8:16, :] = load_tile
    to_row(lambda peer: gram_a, gram_row, 4)
    gram_row[r] = gram_a[...]

    for q in range(tiles):
        for axis in range(3):
            piece = p_tgt[axis, :, q * LANES:(q + 1) * LANES]
            lower, upper = piece[:kh], piece[kh:]
            slot_rows = slice(kh * axis, kh * (axis + 1))
            aw_send[2 * q, slot_rows, :] = jnp.where(low_k, lower, swap(upper))
            aw_send[2 * q + 1, slot_rows, :] = jnp.where(low_k, swap(lower), upper)
    to_row(lambda peer: aw_send.at[peer], aw_recv, 3)
    aw_recv[r] = aw_send[r]
    arrived(gram_row, 4)
    gram_b[...] = total(gram_row)
    to_col(gram_b, gram_col, 5)
    gram_col[c] = gram_b[...]
    arrived(gram_col, 5)
    both = total(gram_col)
    packed, load_tile = both[0:8], both[8:16]
    pieces, load_pieces = [packed], [load_tile]
    for g in range(1, groups):
        pieces.append(pltpu.roll(packed, LANES - vectors * g, 1))
        load_pieces.append(pltpu.roll(load_tile, LANES - vectors * g, 1))
    gram = jnp.concatenate(pieces, axis=0)
    load = jnp.concatenate(load_pieces, axis=0)[:, 0:1]

    system = jnp.where(lane32 < vectors, gram, jnp.where(lane32 == row32 + vectors, 1.0, 0.0))
    system = jnp.where(lane32 == 2 * vectors, load, system)
    for j in range(vectors):
        pivot_row = system[j:j + 1, :]
        scaled_row = pivot_row / pivot_row[:, j:j + 1]
        column = system[:, j:j + 1]
        system = jnp.where(row32 == j, scaled_row, system - column * scaled_row)
    inverse = jnp.where(jnp.logical_and(lane32 >= vectors, lane32 < 2 * vectors), system, 0.0)
    coarse = system[:, 2 * vectors:2 * vectors + 1]

    def weights_of(column):
        return jnp.where(low_k, column[:kh], column[kh:])

    def combine(ref, weights):
        out = []
        for axis in range(3):
            s = jnp.sum(ref[kh * axis:kh * (axis + 1), :] * weights, axis=0, keepdims=True)
            out.append(s + swap(s))
        return out

    def solve(vector_row):
        return weights_of(jnp.sum(inverse * vector_row, axis=1, keepdims=True))

    def dots_row(field):
        s = None
        for axis in range(3):
            term = aw[kh * axis:kh * (axis + 1), :] * field[axis]
            s = term if s is None else s + term
        lower = jnp.sum(jnp.where(low_k, s, 0.0), axis=1, keepdims=True)
        upper = jnp.sum(jnp.where(low_k, 0.0, s), axis=1, keepdims=True)
        spots = jnp.where(lane_k == row_k + vectors, lower, 0.0)
        spots = spots + jnp.where(lane_k == row_k + vectors + kh, upper, 0.0)
        return jnp.sum(spots, axis=0, keepdims=True)

    def dot_local(x, y):
        s = x[0] * y[0] + x[1] * y[1] + x[2] * y[2]
        return jnp.sum(jnp.where(low1, s, 0.0), axis=1, keepdims=True)

    def stat(ref, row_value):
        ref[...] = row_value

    def at_lane(index, value):
        return jnp.where(lane1 == index, value, 0.0)

    def put(ref, field, last):
        for axis in range(3):
            ref[axis:axis + 1, :] = field[axis]
        ref[3:4, :] = last

    def product(vec_all, which, send, weigh, forward):
        zero = jnp.zeros((8, LANES), F32)
        sums = [zero] * (3 * tiles)
        half = 3 * tiles // 2
        for step in range(chunks):
            chunk = chunk_at(vec_all, which, step)
            for part in range(2):
                spread(vec_all, 2 * chunk + part, 3, 2 * step + part)
            for part in range(2):
                def one(i, carry, step=step, chunk=chunk, part=part):
                    rows = pl.ds(pl.multiple_of(chunk * width + i * 8, 8), 8)
                    at = pl.ds(pl.multiple_of(step * width + i * 8, 8), 8)
                    value = [src_b[axis, at, :] for axis in range(3)]
                    out = []
                    for q in range(tiles // 2):
                        base = (part * (tiles // 2) + q) * LANES
                        m = [mob[slot, rows, base:base + LANES] for slot in range(6)]
                        for axis in range(3):
                            out.append(
                                carry[3 * q + axis]
                                + (m[SLOT[axis, 0]] * value[0] + m[SLOT[axis, 1]] * value[1])
                                + m[SLOT[axis, 2]] * value[2]
                            )
                    return tuple(out)
                mine_sums = tuple(sums[part * half:(part + 1) * half])
                sums[part * half:(part + 1) * half] = lax.fori_loop(
                    0, width // 8, one, mine_sums, unroll=2
                )
        forward()
        dots = []
        for q in range(tiles):
            for axis in range(3):
                value = jnp.sum(sums[3 * q + axis], axis=0, keepdims=True)
                send[q, axis:axis + 1, :] = value
                if weigh is not None:
                    weight = jnp.where(
                        low1, weigh[2 * q, axis:axis + 1, :], weigh[2 * q + 1, axis:axis + 1, :]
                    )
                    dots.append(value * weight)
        last = jnp.zeros((1, LANES), F32)
        if weigh is not None:
            while len(dots) > 1:
                dots = [sum(dots[i:i + 2]) for i in range(0, len(dots), 2)]
            last = jnp.broadcast_to(jnp.sum(dots[0], axis=1, keepdims=True), (1, LANES))
        for q in range(tiles):
            send[q, 3:4, :] = last

    def mine(recv):
        tile = total(recv)
        odd = lax.rem(r, 2)
        keep = jnp.where(low1, 1 - odd, odd) == 1
        out = []
        for axis in range(3):
            half = jnp.where(keep, tile[axis:axis + 1, :], 0.0)
            out.append(half + swap(half))
        return out, tile[3:4, :]

    arrived(aw_recv, 3)
    aw[...] = total(aw_recv)
    weights = weights_of(coarse)
    x0 = combine(wp, weights)
    image0 = combine(aw, weights)
    r0 = [rhs[axis] - image0[axis] for axis in range(3)]

    put(vec_a, r0, jnp.zeros((1, LANES), F32))
    to_col_chunks(vec_a, vec_col_a, 6, 1)
    vec_col_a[c] = vec_a[...]
    stat(stat_a, dots_row(r0) + at_lane(0, dot_local(r0, r0)))
    to_row(lambda peer: stat_a, stat_row_a, 7)
    stat_row_a[r] = stat_a[...]

    def forward_a():
        arrived(stat_row_a, 7)
        stat_b[...] = total(stat_row_a)
        to_col(stat_b, stat_col_b, 9)
        stat_col_b[c] = stat_b[...]
    product(vec_col_a, 1, part_a, None, forward_a)
    to_row(lambda peer: part_a.at[lax.div(peer, 2)], part_row_a, 8)
    part_row_a[r] = part_a[lax.div(r, 2)]
    arrived(stat_col_b, 9)
    sums0 = total(stat_col_b)[0:1, :]
    norm0 = sums0[:, 0:1]
    weights = solve(sums0)
    shift = combine(wp, weights)
    d0 = [r0[axis] - shift[axis] for axis in range(3)]
    shift_image = combine(aw, weights)
    arrived(part_row_a, 8)
    z0, _ = mine(part_row_a)
    q0 = [z0[axis] - shift_image[axis] for axis in range(3)]

    put(vec_c, q0, jnp.zeros((1, LANES), F32))
    to_col_chunks(vec_c, vec_col_c, 10, 2)
    vec_col_c[c] = vec_c[...]
    put(
        vec_d, q0,
        dots_row(q0) + at_lane(0, dot_local(d0, q0)) + at_lane(1, dot_local(r0, q0))
        + at_lane(2, dot_local(q0, q0)),
    )
    to_row(lambda peer: vec_d, vec_row_c, 11)
    vec_row_c[r] = vec_d[...]

    def forward_c():
        arrived(vec_row_c, 11)
        stat_d[...] = total(vec_row_c)[3:4, :]
        to_col(stat_d, stat_col_d, 13)
        stat_col_d[c] = stat_d[...]
    product(vec_col_c, 2, part_c, vec_row_c, forward_c)
    to_row(lambda peer: part_c.at[lax.div(peer, 2)], part_row_c, 12)
    part_row_c[r] = part_c[lax.div(r, 2)]
    arrived(stat_col_d, 13)
    sums1 = total(stat_col_d)
    step0 = norm0 / sums1[:, 0:1]
    norm1 = norm0 - 2.0 * step0 * sums1[:, 1:2] + step0 * step0 * sums1[:, 2:3]
    beta = norm1 / norm0
    weights = solve(sums0 - step0 * sums1)
    shift = combine(wp, weights)
    shift_image = combine(aw, weights)
    x1 = [x0[axis] + step0 * d0[axis] for axis in range(3)]
    r1 = [r0[axis] - step0 * q0[axis] for axis in range(3)]
    d1 = [r1[axis] + beta * d0[axis] - shift[axis] for axis in range(3)]
    inner = jnp.sum(inverse * sums1, axis=1, keepdims=True)
    column = jnp.sum(jnp.where(lane32 == row32 + vectors, sums1, 0.0), axis=1, keepdims=True)
    removed = jnp.sum(inner * column, axis=0, keepdims=True)
    factor = 1.0 + beta
    fixed = factor * factor * sums1[:, 0:1] - 2.0 * factor * step0 * sums1[:, 2:3]
    arrived(part_row_c, 12)
    y0, block_sum = mine(part_row_c)
    stat_f[...] = block_sum
    to_col(stat_f, stat_col_f, 15)
    stat_col_f[c] = stat_f[...]
    q1 = [
        (z0[axis] - step0 * y0[axis]) + beta * q0[axis] - shift_image[axis] for axis in range(3)
    ]
    arrived(stat_col_f, 15)
    curvature = fixed + step0 * step0 * (total(stat_col_f)[:, 0:1] - removed)
    step1 = norm1 / curvature
    for axis in range(3):
        out_ref[axis:axis + 1, :] = x1[axis] + step1 * d1[axis]
        out_ref[4 + axis:5 + axis, :] = r1[axis] - step1 * q1[axis]

    for tag, dst in enumerate((
        gcol, grow, wcol, aw_recv, gram_row, gram_col, vec_col_a, stat_row_a, part_row_a,
        stat_col_b, vec_col_c, vec_row_c, part_row_c, stat_col_d, wrow, stat_col_f,
    )):
        departed(dst, tag)


def body(n, positions, radii, basis, rhs):
    vectors = basis.shape[0]
    kh = vectors // 2
    span = n * HALF
    row, rows = pltpu.VMEM((1, LANES), F32), pltpu.VMEM((n, 1, LANES), F32)
    tile, tile_slots = pltpu.VMEM((4, LANES), F32), pltpu.VMEM((n, 4, LANES), F32)
    parts = pltpu.VMEM((span // LANES, 4, LANES), F32)
    field, field_slots = pltpu.VMEM((3 * kh, LANES), F32), pltpu.VMEM((n, 3 * kh, LANES), F32)
    two, two_slots = pltpu.VMEM((16, LANES), F32), pltpu.VMEM((n, 16, LANES), F32)
    vmem = pl.BlockSpec(memory_space=pltpu.VMEM)
    anywhere = pl.BlockSpec(memory_space=pl.ANY)
    out = pl.pallas_call(
        functools.partial(kernel, n, vectors),
        out_shape=jax.ShapeDtypeStruct((8, LANES), F32),
        in_specs=[anywhere] * 4,
        out_specs=vmem,
        scratch_shapes=[
            pltpu.VMEM((3, HALF), F32), pltpu.VMEM((1, HALF), F32),
            pltpu.VMEM((3, vectors, HALF), F32), pltpu.VMEM((3, HALF), F32),
            tile, field,
            tile_slots, tile_slots, field_slots, field_slots,
            pltpu.VMEM((4, span, LANES), F32),
            pltpu.VMEM((4, span), F32),
            pltpu.VMEM((6, span, span), F32),
            pltpu.VMEM((8 * vectors, span), BF16),
            pltpu.VMEM((3, 2 * vectors, span), BF16), pltpu.VMEM((3, vectors, span), F32),
            field_slots, field_slots, field,
            two, two_slots, two, two_slots,
            tile, tile_slots, row, rows, parts, tile_slots, row, rows,
            tile, tile, tile_slots, tile_slots, parts, tile_slots, row, rows,
            row, rows,
            pltpu.SemaphoreType.DMA((4,)),
            pltpu.SemaphoreType.DMA((16,)),
            pltpu.SemaphoreType.DMA((16,)),
            pltpu.SemaphoreType.DMA((4, n // 4)),
        ],
        compiler_params=pltpu.CompilerParams(
            collective_id=0, has_side_effects=True, vmem_limit_bytes=60 << 20
        ),
    )(positions, radii[None], basis.transpose(1, 0, 2), rhs)
    return out[0:3, :HALF], out[4:7, :HALF]


def solution(mesh):
    return jax.shard_map(
        functools.partial(body, mesh.shape["row"]),
        mesh=mesh,
        in_specs=(
            P(None, ("row", "col")),
            P(("row", "col")),
            P(None, None, ("row", "col")),
            P(None, ("row", "col")),
        ),
        out_specs=(P(None, ("row", "col")), P(None, ("row", "col"))),
        check_vma=False,
    )
```

```python
import functools
import math

import jax
import jax.numpy as jnp
from jax import lax
from jax.experimental import pallas as pl
from jax.experimental.pallas import tpu as pltpu
from jax.sharding import PartitionSpec as P

MESH = pl.DeviceIdType.MESH
F32 = jnp.float32
BF16 = jnp.bfloat16

far_scale = 1.0 / (8.0 * math.pi)
self_scale = 1.0 / (6.0 * math.pi)

LANES = 128
HALF = 64
PAIRS = ((0, 0), (1, 1), (2, 2), (0, 1), (1, 2), (2, 0))
SLOT = {}
for _slot, (_a, _b) in enumerate(PAIRS):
    SLOT[_a, _b] = _slot
    SLOT[_b, _a] = _slot


def kernel(
    n, vectors,
    pos_ref, rad_ref, basis_ref, rhs_ref,
    out_ref,
    pos_in, rad_in, basis_in, rhs_in, geo, wp,
    grow, gcol, wcol, wrow, src_b, tgt, mob, fields, w_tgt, p_tgt, aw_send, aw_recv, aw,
    gram_a, gram_row, gram_b, gram_col,
    vec_a, vec_col_a, stat_a, stat_row_a, part_a, part_row_a, stat_b, stat_col_b,
    vec_c, vec_d, vec_col_c, vec_row_c, part_c, part_row_c, stat_d, stat_col_d,
    stat_f, stat_col_f,
    in_sems, send_sems, recv_sems, chunk_sems,
):
    at_row = lax.axis_index("row")
    at_col = lax.axis_index("col")
    core = lax.rem(at_row, 2)
    y_low = lax.rem(at_col, 2)
    r = lax.div(at_row, 2) * 2 + y_low
    c = lax.div(at_col, 2) * 2 + core

    def row_peer(index):
        return (lax.div(index, 2) * 2 + core, lax.div(at_col, 2) * 2 + lax.rem(index, 2))

    def col_peer(index):
        return (lax.div(at_row, 2) * 2 + lax.rem(index, 2), lax.div(index, 2) * 2 + y_low)

    kh = vectors // 2
    span = n * HALF
    tiles = span // LANES

    barrier = pltpu.get_barrier_semaphore()

    def greet(step, carry):
        pl.semaphore_signal(
            barrier, inc=1, device_id=row_peer(lax.rem(r + step, n)), device_id_type=MESH
        )
        pl.semaphore_signal(
            barrier, inc=1, device_id=col_peer(lax.rem(c + step, n)), device_id_type=MESH
        )
        return carry
    lax.fori_loop(1, n, greet, 0)

    reads = [
        pltpu.make_async_copy(src, dst, in_sems.at[i])
        for i, (src, dst) in enumerate((
            (pos_ref, pos_in), (rad_ref, rad_in), (basis_ref, basis_in), (rhs_ref, rhs_in)
        ))
    ]
    for read in reads:
        read.start()
    for read in reads:
        read.wait()
    for half in range(2):
        lanes = slice(half * HALF, (half + 1) * HALF)
        geo[0:3, lanes] = pos_in[...]
        geo[3:4, lanes] = rad_in[...]
        for axis in range(3):
            wp[kh * axis:kh * (axis + 1), lanes] = basis_in[axis, kh * half:kh * (half + 1), :]

    lane1 = lax.broadcasted_iota(jnp.int32, (1, LANES), 1)
    lane4 = lax.broadcasted_iota(jnp.int32, (4, LANES), 1)
    lane8 = lax.broadcasted_iota(jnp.int32, (8, LANES), 1)
    lane_k = lax.broadcasted_iota(jnp.int32, (kh, LANES), 1)
    row_k = lax.broadcasted_iota(jnp.int32, (kh, LANES), 0)
    low1, low4, low_k = lane1 < HALF, lane4 < HALF, lane_k < HALF

    def swap(x):
        return pltpu.roll(x, HALF, 1)

    def to_row(src, dst, tag):
        def one(step, carry):
            peer = lax.rem(r + step, n)
            pltpu.make_async_remote_copy(
                src_ref=src(peer), dst_ref=dst.at[r], send_sem=send_sems.at[tag],
                recv_sem=recv_sems.at[tag], device_id=row_peer(peer), device_id_type=MESH,
            ).start()
            return carry
        lax.fori_loop(1, n, one, 0)

    def to_col(src, dst, tag):
        def one(step, carry):
            peer = lax.rem(c + step, n)
            pltpu.make_async_remote_copy(
                src_ref=src, dst_ref=dst.at[c], send_sem=send_sems.at[tag],
                recv_sem=recv_sems.at[tag], device_id=col_peer(peer), device_id_type=MESH,
            ).start()
            return carry
        lax.fori_loop(1, n, one, 0)

    chunks = n // 4
    order = sorted(range(chunks), key=lambda k: min(k, chunks - k))

    def to_col_chunks(src, dst, tag, which):
        def one(step, carry):
            peer = lax.rem(c + step, n)
            pltpu.make_async_remote_copy(
                src_ref=src, dst_ref=dst.at[c], send_sem=send_sems.at[tag],
                recv_sem=chunk_sems.at[which, lax.div(c, 4)], device_id=col_peer(peer),
                device_id_type=MESH,
            ).start()
            return carry
        lax.fori_loop(1, n, one, 0)

    def chunk_at(dst, which, step):
        chunk = lax.rem(lax.div(c, 4) + order[step], chunks)
        some = dst.at[pl.ds(0, 3 if step == 0 else 4)]
        pltpu.make_async_copy(some, some, chunk_sems.at[which, chunk]).wait()
        return chunk

    def arrived(dst, tag):
        all_but_one = dst.at[pl.ds(0, n - 1)]
        pltpu.make_async_copy(all_but_one, all_but_one, recv_sems.at[tag]).wait()

    def departed(dst, tag):
        all_but_one = dst.at[pl.ds(0, n - 1)]
        pltpu.make_async_copy(all_but_one, all_but_one, send_sems.at[tag]).wait()

    def total(ref):
        parts = [ref[i] for i in range(n)]
        while len(parts) > 1:
            parts = [parts[i] + parts[i + 1] for i in range(0, len(parts), 2)]
        return parts[0]

    pl.semaphore_wait(barrier, 2 * (n - 1))

    to_col_chunks(geo, gcol, 0, 3)
    to_row(lambda peer: geo, grow, 1)
    to_col_chunks(wp, wcol, 2, 0)
    to_row(lambda peer: wp, wrow, 14)
    gcol[c] = geo[...]
    grow[r] = geo[...]
    wcol[c] = wp[...]
    wrow[r] = wp[...]

    def spread(ref, pair, count, place):
        tile = jnp.where(low4, ref[2 * pair], ref[2 * pair + 1])
        turned = jnp.concatenate([tile, tile], axis=0).T
        for axis in range(count):
            src_b[axis, pl.ds(pl.multiple_of(place * LANES, LANES), LANES), :] = jnp.broadcast_to(
                turned[:, axis:axis + 1], (LANES, LANES)
            )

    for step in range(chunks):
        chunk = chunk_at(gcol, 3, step)
        for part in range(2):
            spread(gcol, 2 * chunk + part, 4, 2 * chunk + part)
    arrived(grow, 1)
    for q in range(tiles):
        tgt[:, q * LANES:(q + 1) * LANES] = jnp.where(low4, grow[2 * q], grow[2 * q + 1])

    def split(x):
        high = x.astype(BF16)
        return high, (x - high.astype(F32)).astype(BF16)

    def target_tile(q):
        lanes = pl.ds(pl.multiple_of(q * LANES, LANES), LANES)
        return lanes, [
            jnp.broadcast_to(tgt[axis:axis + 1, lanes], (8, LANES)) for axis in range(4)
        ]

    def form(rows, lanes, target, target_sq, patch):
        sx, sy, sz, s_rad = [src_b[axis, rows, :] for axis in range(4)]
        dx, dy, dz = target[0] - sx, target[1] - sy, target[2] - sz
        dist_sq = dx * dx + dy * dy + dz * dz
        if patch is not None:
            dist_sq = jnp.where(patch, 1.0, dist_sq)
        inv = lax.rsqrt(dist_sq)
        inv_sq = inv * inv
        scaled = far_scale * inv
        sized = scaled * ((target_sq + s_rad * s_rad) * inv_sq)
        iso = scaled + sized * (1.0 / 3.0)
        if patch is not None:
            iso = jnp.where(patch, self_scale / target[3], iso)
        along = (scaled - sized) * inv_sq
        ax, ay, az = along * dx, along * dy, along * dz
        mob[0, rows, lanes] = ax * dx + iso
        mob[1, rows, lanes] = ay * dy + iso
        mob[2, rows, lanes] = az * dz + iso
        mob[3, rows, lanes] = ax * dy
        mob[4, rows, lanes] = ay * dz
        mob[5, rows, lanes] = az * dx

    def form_tile(q, carry):
        lanes, target = target_tile(q)
        target_sq = target[3] * target[3]

        def form_row(i, inner):
            form(pl.ds(pl.multiple_of(i * 8, 8), 8), lanes, target, target_sq, None)
            return inner
        lax.fori_loop(0, span // 8, form_row, 0, unroll=8)
        return carry
    lax.fori_loop(0, tiles, form_tile, 0)

    lanes, target = target_tile(lax.div(r, 2))
    at_own = lane8 - lax.rem(r, 2) * HALF
    for i in range(HALF // 8):
        same = lax.broadcasted_iota(jnp.int32, (8, LANES), 0) + 8 * i == at_own
        form(
            pl.ds(pl.multiple_of(c * HALF + 8 * i, 8), 8), lanes, target,
            target[3] * target[3], same,
        )

    def unpack_pair(ref, p, axis):
        first = ref[2 * p, kh * axis:kh * (axis + 1), :]
        second = ref[2 * p + 1, kh * axis:kh * (axis + 1), :]
        return jnp.concatenate(
            [jnp.where(low_k, first, swap(second)), jnp.where(low_k, swap(first), second)], axis=0
        )

    arrived(wrow, 14)
    for p in range(tiles):
        cols = slice(p * LANES, (p + 1) * LANES)
        for axis in range(3):
            high, rest = split(unpack_pair(wrow, p, axis))
            w_tgt[axis, 0:vectors, cols] = high
            w_tgt[axis, vectors:2 * vectors, cols] = rest

    width = 4 * HALF
    for step in range(chunks):
        chunk = chunk_at(wcol, 0, step)
        for part in range(2):
            cols = pl.ds(pl.multiple_of(chunk * width + part * LANES, LANES), LANES)
            for axis in range(3):
                high, rest = split(unpack_pair(wcol, 2 * chunk + part, axis))
                for copy in (axis, axis + 3):
                    if copy < 4:
                        base = vectors * copy
                        fields[base:base + vectors, cols] = high
                        fields[4 * vectors + base:4 * vectors + base + vectors, cols] = rest

    def basis_chunk(t, carry):
        lanes = pl.ds(pl.multiple_of(t * width, width), width)
        sums = [None] * 3

        def add(axis, value):
            sums[axis] = value if sums[axis] is None else sums[axis] + value
        for slot, (a, b) in enumerate(PAIRS):
            first = vectors * a
            count = vectors if a == b else 2 * vectors
            by_high = by_rest = None
            for d in range(chunks):
                high, rest = split(mob[slot, d * width:(d + 1) * width, lanes])
                cols = slice(d * width, (d + 1) * width)
                lhs_high = fields[first:first + count, cols]
                lhs_rest = fields[4 * vectors + first:4 * vectors + first + count, cols]
                both = jnp.concatenate([lhs_high, lhs_rest], axis=0)
                dot_high = jnp.dot(both, high, preferred_element_type=F32)
                dot_rest = jnp.dot(lhs_high, rest, preferred_element_type=F32)
                by_high = dot_high if by_high is None else by_high + dot_high
                by_rest = dot_rest if by_rest is None else by_rest + dot_rest
            value = by_high[0:count] + by_high[count:2 * count] + by_rest
            add(b, value[0:vectors])
            if a != b:
                add(a, value[vectors:2 * vectors])
        for axis in range(3):
            p_tgt[axis, :, lanes] = sums[axis]
        return carry
    lax.fori_loop(0, span // width, basis_chunk, 0)

    rhs = [jnp.concatenate([rhs_in[axis:axis + 1, :]] * 2, axis=1) for axis in range(3)]
    row32 = lax.broadcasted_iota(jnp.int32, (vectors, LANES), 0)
    lane32 = lax.broadcasted_iota(jnp.int32, (vectors, LANES), 1)

    gram = None
    load = None
    for axis in range(3):
        high, rest = split(p_tgt[axis])
        along_lanes = (((1,), (1,)), ((), ()))
        by_high = lax.dot_general(w_tgt[axis], high, along_lanes, preferred_element_type=F32)
        by_rest = lax.dot_general(
            w_tgt[axis, 0:vectors, :], rest, along_lanes, preferred_element_type=F32
        )
        term = by_high[0:vectors] + by_high[vectors:2 * vectors] + by_rest
        block = wp[kh * axis:kh * (axis + 1), :]
        block = jnp.where(lane32 < HALF, jnp.concatenate([block, swap(block)], axis=0), 0.0)
        load_term = block * rhs[axis]
        gram = term if gram is None else gram + term
        load = load_term if load is None else load + load_term
    load = jnp.sum(load, axis=1, keepdims=True)
    wide = jnp.concatenate([gram, jnp.zeros((vectors, LANES - vectors), F32)], axis=1)
    groups = vectors // 8
    packed = wide[0:8]
    for g in range(1, groups):
        packed = packed + pltpu.roll(wide[8 * g:8 * g + 8], vectors * g, 1)
    gram_a[0:8, :] = packed
    gram_a[8:9, :] = jnp.sum(jnp.where(lane32 == row32, load, 0.0), axis=0, keepdims=True)
    to_row(lambda peer: gram_a, gram_row, 4)
    gram_row[r] = gram_a[...]

    for q in range(tiles):
        for axis in range(3):
            piece = p_tgt[axis, :, q * LANES:(q + 1) * LANES]
            lower, upper = piece[:kh], piece[kh:]
            slot_rows = slice(kh * axis, kh * (axis + 1))
            aw_send[2 * q, slot_rows, :] = jnp.where(low_k, lower, swap(upper))
            aw_send[2 * q + 1, slot_rows, :] = jnp.where(low_k, swap(lower), upper)
    to_row(lambda peer: aw_send.at[peer], aw_recv, 3)
    aw_recv[r] = aw_send[r]
    arrived(gram_row, 4)
    gram_b[...] = total(gram_row)
    to_col(gram_b, gram_col, 5)
    gram_col[c] = gram_b[...]
    arrived(gram_col, 5)
    both = total(gram_col)
    packed, load_row = both[0:8], both[8:9]
    pieces = [packed]
    for g in range(1, groups):
        pieces.append(pltpu.roll(packed, LANES - vectors * g, 1))
    gram = jnp.concatenate(pieces, axis=0)
    load = jnp.sum(jnp.where(lane32 == row32, load_row, 0.0), axis=1, keepdims=True)

    system = jnp.where(lane32 < vectors, gram, jnp.where(lane32 == row32 + vectors, 1.0, 0.0))
    system = jnp.where(lane32 == 2 * vectors, load, system)
    for j in range(vectors):
        pivot_row = system[j:j + 1, :]
        scaled_row = pivot_row / pivot_row[:, j:j + 1]
        column = system[:, j:j + 1]
        system = jnp.where(row32 == j, scaled_row, system - column * scaled_row)
    inverse = jnp.where(jnp.logical_and(lane32 >= vectors, lane32 < 2 * vectors), system, 0.0)
    coarse = system[:, 2 * vectors:2 * vectors + 1]

    def weights_of(column):
        return jnp.where(low_k, column[:kh], column[kh:])

    def combine(ref, weights):
        out = []
        for axis in range(3):
            s = jnp.sum(ref[kh * axis:kh * (axis + 1), :] * weights, axis=0, keepdims=True)
            out.append(s + swap(s))
        return out

    def solve(vector_row):
        return weights_of(jnp.sum(inverse * vector_row, axis=1, keepdims=True))

    def dots_row(field):
        s = None
        for axis in range(3):
            term = aw[kh * axis:kh * (axis + 1), :] * field[axis]
            s = term if s is None else s + term
        lower = jnp.sum(jnp.where(low_k, s, 0.0), axis=1, keepdims=True)
        upper = jnp.sum(jnp.where(low_k, 0.0, s), axis=1, keepdims=True)
        spots = jnp.where(lane_k == row_k + vectors, lower, 0.0)
        spots = spots + jnp.where(lane_k == row_k + vectors + kh, upper, 0.0)
        return jnp.sum(spots, axis=0, keepdims=True)

    def dot_local(x, y):
        s = x[0] * y[0] + x[1] * y[1] + x[2] * y[2]
        return jnp.sum(jnp.where(low1, s, 0.0), axis=1, keepdims=True)

    def stat(ref, row_value):
        ref[...] = row_value

    def at_lane(index, value):
        return jnp.where(lane1 == index, value, 0.0)

    def put(ref, field, last):
        for axis in range(3):
            ref[axis:axis + 1, :] = field[axis]
        ref[3:4, :] = last

    def product(vec_all, which, send, weigh, forward):
        zero = jnp.zeros((8, LANES), F32)
        sums = [zero] * (3 * tiles)
        half = 3 * tiles // 2
        for step in range(chunks):
            chunk = chunk_at(vec_all, which, step)
            for part in range(2):
                spread(vec_all, 2 * chunk + part, 3, 2 * step + part)
            for part in range(2):
                def one(i, carry, step=step, chunk=chunk, part=part):
                    rows = pl.ds(pl.multiple_of(chunk * width + i * 8, 8), 8)
                    at = pl.ds(pl.multiple_of(step * width + i * 8, 8), 8)
                    value = [src_b[axis, at, :] for axis in range(3)]
                    out = []
                    for q in range(tiles // 2):
                        base = (part * (tiles // 2) + q) * LANES
                        m = [mob[slot, rows, base:base + LANES] for slot in range(6)]
                        for axis in range(3):
                            out.append(
                                carry[3 * q + axis]
                                + (m[SLOT[axis, 0]] * value[0] + m[SLOT[axis, 1]] * value[1])
                                + m[SLOT[axis, 2]] * value[2]
                            )
                    return tuple(out)
                mine_sums = tuple(sums[part * half:(part + 1) * half])
                sums[part * half:(part + 1) * half] = lax.fori_loop(
                    0, width // 8, one, mine_sums, unroll=4
                )
        forward()
        dots = []
        for q in range(tiles):
            for axis in range(3):
                value = jnp.sum(sums[3 * q + axis], axis=0, keepdims=True)
                send[q, axis:axis + 1, :] = value
                if weigh is not None:
                    weight = jnp.where(
                        low1, weigh[2 * q, axis:axis + 1, :], weigh[2 * q + 1, axis:axis + 1, :]
                    )
                    dots.append(value * weight)
        last = jnp.zeros((1, LANES), F32)
        if weigh is not None:
            while len(dots) > 1:
                dots = [sum(dots[i:i + 2]) for i in range(0, len(dots), 2)]
            last = jnp.broadcast_to(jnp.sum(dots[0], axis=1, keepdims=True), (1, LANES))
        for q in range(tiles):
            send[q, 3:4, :] = last

    def mine(recv):
        tile = total(recv)
        odd = lax.rem(r, 2)
        keep = jnp.where(low1, 1 - odd, odd) == 1
        out = []
        for axis in range(3):
            half = jnp.where(keep, tile[axis:axis + 1, :], 0.0)
            out.append(half + swap(half))
        return out, tile[3:4, :]

    arrived(aw_recv, 3)
    aw[...] = total(aw_recv)
    weights = weights_of(coarse)
    x0 = combine(wp, weights)
    image0 = combine(aw, weights)
    r0 = [rhs[axis] - image0[axis] for axis in range(3)]

    put(vec_a, r0, jnp.zeros((1, LANES), F32))
    to_col_chunks(vec_a, vec_col_a, 6, 1)
    vec_col_a[c] = vec_a[...]
    stat(stat_a, dots_row(r0) + at_lane(0, dot_local(r0, r0)))
    to_row(lambda peer: stat_a, stat_row_a, 7)
    stat_row_a[r] = stat_a[...]

    def forward_a():
        arrived(stat_row_a, 7)
        stat_b[...] = total(stat_row_a)
        to_col(stat_b, stat_col_b, 9)
        stat_col_b[c] = stat_b[...]
    product(vec_col_a, 1, part_a, None, forward_a)
    to_row(lambda peer: part_a.at[lax.div(peer, 2)], part_row_a, 8)
    part_row_a[r] = part_a[lax.div(r, 2)]
    arrived(stat_col_b, 9)
    sums0 = total(stat_col_b)[0:1, :]
    norm0 = sums0[:, 0:1]
    weights = solve(sums0)
    shift = combine(wp, weights)
    d0 = [r0[axis] - shift[axis] for axis in range(3)]
    shift_image = combine(aw, weights)
    arrived(part_row_a, 8)
    z0, _ = mine(part_row_a)
    q0 = [z0[axis] - shift_image[axis] for axis in range(3)]

    put(vec_c, q0, jnp.zeros((1, LANES), F32))
    to_col_chunks(vec_c, vec_col_c, 10, 2)
    vec_col_c[c] = vec_c[...]
    put(
        vec_d, q0,
        dots_row(q0) + at_lane(0, dot_local(d0, q0)) + at_lane(1, dot_local(r0, q0))
        + at_lane(2, dot_local(q0, q0)),
    )
    to_row(lambda peer: vec_d, vec_row_c, 11)
    vec_row_c[r] = vec_d[...]

    def forward_c():
        arrived(vec_row_c, 11)
        stat_d[...] = total(vec_row_c)[3:4, :]
        to_col(stat_d, stat_col_d, 13)
        stat_col_d[c] = stat_d[...]
    product(vec_col_c, 2, part_c, vec_row_c, forward_c)
    to_row(lambda peer: part_c.at[lax.div(peer, 2)], part_row_c, 12)
    part_row_c[r] = part_c[lax.div(r, 2)]
    arrived(stat_col_d, 13)
    sums1 = total(stat_col_d)
    step0 = norm0 / sums1[:, 0:1]
    norm1 = norm0 - 2.0 * step0 * sums1[:, 1:2] + step0 * step0 * sums1[:, 2:3]
    beta = norm1 / norm0
    weights = solve(sums0 - step0 * sums1)
    shift = combine(wp, weights)
    shift_image = combine(aw, weights)
    x1 = [x0[axis] + step0 * d0[axis] for axis in range(3)]
    r1 = [r0[axis] - step0 * q0[axis] for axis in range(3)]
    d1 = [r1[axis] + beta * d0[axis] - shift[axis] for axis in range(3)]
    inner = jnp.sum(inverse * sums1, axis=1, keepdims=True)
    column = jnp.sum(jnp.where(lane32 == row32 + vectors, sums1, 0.0), axis=1, keepdims=True)
    removed = jnp.sum(inner * column, axis=0, keepdims=True)
    factor = 1.0 + beta
    fixed = factor * factor * sums1[:, 0:1] - 2.0 * factor * step0 * sums1[:, 2:3]
    arrived(part_row_c, 12)
    y0, block_sum = mine(part_row_c)
    stat_f[...] = block_sum
    to_col(stat_f, stat_col_f, 15)
    stat_col_f[c] = stat_f[...]
    q1 = [
        (z0[axis] - step0 * y0[axis]) + beta * q0[axis] - shift_image[axis] for axis in range(3)
    ]
    arrived(stat_col_f, 15)
    curvature = fixed + step0 * step0 * (total(stat_col_f)[:, 0:1] - removed)
    step1 = norm1 / curvature
    for axis in range(3):
        out_ref[axis:axis + 1, :] = x1[axis] + step1 * d1[axis]
        out_ref[4 + axis:5 + axis, :] = r1[axis] - step1 * q1[axis]

    for tag, dst in enumerate((
        gcol, grow, wcol, aw_recv, gram_row, gram_col, vec_col_a, stat_row_a, part_row_a,
        stat_col_b, vec_col_c, vec_row_c, part_row_c, stat_col_d, wrow, stat_col_f,
    )):
        departed(dst, tag)


def body(n, positions, radii, basis, rhs):
    vectors = basis.shape[0]
    kh = vectors // 2
    span = n * HALF
    row, rows = pltpu.VMEM((1, LANES), F32), pltpu.VMEM((n, 1, LANES), F32)
    tile, tile_slots = pltpu.VMEM((4, LANES), F32), pltpu.VMEM((n, 4, LANES), F32)
    parts = pltpu.VMEM((span // LANES, 4, LANES), F32)
    field, field_slots = pltpu.VMEM((3 * kh, LANES), F32), pltpu.VMEM((n, 3 * kh, LANES), F32)
    two, two_slots = pltpu.VMEM((9, LANES), F32), pltpu.VMEM((n, 9, LANES), F32)
    vmem = pl.BlockSpec(memory_space=pltpu.VMEM)
    anywhere = pl.BlockSpec(memory_space=pl.ANY)
    out = pl.pallas_call(
        functools.partial(kernel, n, vectors),
        out_shape=jax.ShapeDtypeStruct((8, LANES), F32),
        in_specs=[anywhere] * 4,
        out_specs=vmem,
        scratch_shapes=[
            pltpu.VMEM((3, HALF), F32), pltpu.VMEM((1, HALF), F32),
            pltpu.VMEM((3, vectors, HALF), F32), pltpu.VMEM((3, HALF), F32),
            tile, field,
            tile_slots, tile_slots, field_slots, field_slots,
            pltpu.VMEM((4, span, LANES), F32),
            pltpu.VMEM((4, span), F32),
            pltpu.VMEM((6, span, span), F32),
            pltpu.VMEM((8 * vectors, span), BF16),
            pltpu.VMEM((3, 2 * vectors, span), BF16), pltpu.VMEM((3, vectors, span), F32),
            field_slots, field_slots, field,
            two, two_slots, two, two_slots,
            tile, tile_slots, row, rows, parts, tile_slots, row, rows,
            tile, tile, tile_slots, tile_slots, parts, tile_slots, row, rows,
            row, rows,
            pltpu.SemaphoreType.DMA((4,)),
            pltpu.SemaphoreType.DMA((16,)),
            pltpu.SemaphoreType.DMA((16,)),
            pltpu.SemaphoreType.DMA((4, n // 4)),
        ],
        compiler_params=pltpu.CompilerParams(
            collective_id=0, has_side_effects=True, vmem_limit_bytes=60 << 20
        ),
    )(positions, radii[None], basis.transpose(1, 0, 2), rhs)
    return out[0:3, :HALF], out[4:7, :HALF]


def solution(mesh):
    return jax.shard_map(
        functools.partial(body, mesh.shape["row"]),
        mesh=mesh,
        in_specs=(
            P(None, ("row", "col")),
            P(("row", "col")),
            P(None, None, ("row", "col")),
            P(None, ("row", "col")),
        ),
        out_specs=(P(None, ("row", "col")), P(None, ("row", "col"))),
        check_vma=False,
    )
```

```python
import functools
import math

import jax
import jax.numpy as jnp
from jax import lax
from jax.experimental import pallas as pl
from jax.experimental.pallas import tpu as pltpu
from jax.sharding import PartitionSpec as P

MESH = pl.DeviceIdType.MESH
F32 = jnp.float32
BF16 = jnp.bfloat16

far_scale = 1.0 / (8.0 * math.pi)
self_scale = 1.0 / (6.0 * math.pi)

LANES = 128
HALF = 64
PAIRS = ((0, 0), (1, 1), (2, 2), (0, 1), (1, 2), (2, 0))
SLOT = {}
for _slot, (_a, _b) in enumerate(PAIRS):
    SLOT[_a, _b] = _slot
    SLOT[_b, _a] = _slot


def kernel(
    n, vectors,
    pos_ref, rad_ref, basis_ref, rhs_ref,
    out_ref,
    pos_in, rad_in, basis_in, rhs_in, geo, wp,
    grow, gcol, wcol, wrow, src_b, tgt, mob, fields, w_tgt, p_tgt, aw_send, aw_recv, aw,
    gram_a, gram_row, gram_b, gram_col,
    vec_a, vec_col_a, stat_a, stat_row_a, part_a, part_row_a, stat_b, stat_col_b,
    vec_c, vec_d, vec_col_c, vec_row_c, part_c, part_row_c, stat_d, stat_col_d,
    stat_f, stat_col_f,
    in_sems, send_sems, recv_sems, chunk_sems,
):
    at_row = lax.axis_index("row")
    at_col = lax.axis_index("col")
    core = lax.rem(at_row, 2)
    y_low = lax.rem(at_col, 2)
    r = lax.div(at_row, 2) * 2 + y_low
    c = lax.div(at_col, 2) * 2 + core

    def row_peer(index):
        return (lax.div(index, 2) * 2 + core, lax.div(at_col, 2) * 2 + lax.rem(index, 2))

    def col_peer(index):
        return (lax.div(at_row, 2) * 2 + lax.rem(index, 2), lax.div(index, 2) * 2 + y_low)

    kh = vectors // 2
    span = n * HALF
    tiles = span // LANES

    barrier = pltpu.get_barrier_semaphore()

    def greet(step, carry):
        pl.semaphore_signal(
            barrier, inc=1, device_id=row_peer(lax.rem(r + step, n)), device_id_type=MESH
        )
        pl.semaphore_signal(
            barrier, inc=1, device_id=col_peer(lax.rem(c + step, n)), device_id_type=MESH
        )
        return carry
    lax.fori_loop(1, n, greet, 0)

    reads = [
        pltpu.make_async_copy(src, dst, in_sems.at[i])
        for i, (src, dst) in enumerate((
            (pos_ref, pos_in), (rad_ref, rad_in), (basis_ref, basis_in), (rhs_ref, rhs_in)
        ))
    ]
    for read in reads:
        read.start()
    for read in reads:
        read.wait()
    for half in range(2):
        lanes = slice(half * HALF, (half + 1) * HALF)
        geo[0:3, lanes] = pos_in[...]
        geo[3:4, lanes] = rad_in[...]
        for axis in range(3):
            wp[kh * axis:kh * (axis + 1), lanes] = basis_in[axis, kh * half:kh * (half + 1), :]

    lane1 = lax.broadcasted_iota(jnp.int32, (1, LANES), 1)
    lane4 = lax.broadcasted_iota(jnp.int32, (4, LANES), 1)
    lane8 = lax.broadcasted_iota(jnp.int32, (8, LANES), 1)
    lane_k = lax.broadcasted_iota(jnp.int32, (kh, LANES), 1)
    row_k = lax.broadcasted_iota(jnp.int32, (kh, LANES), 0)
    low1, low4, low_k = lane1 < HALF, lane4 < HALF, lane_k < HALF

    def swap(x):
        return pltpu.roll(x, HALF, 1)

    def to_row(src, dst, tag):
        def one(step, carry):
            peer = lax.rem(r + step, n)
            pltpu.make_async_remote_copy(
                src_ref=src(peer), dst_ref=dst.at[r], send_sem=send_sems.at[tag],
                recv_sem=recv_sems.at[tag], device_id=row_peer(peer), device_id_type=MESH,
            ).start()
            return carry
        lax.fori_loop(1, n, one, 0)

    def to_col(src, dst, tag):
        def one(step, carry):
            peer = lax.rem(c + step, n)
            pltpu.make_async_remote_copy(
                src_ref=src, dst_ref=dst.at[c], send_sem=send_sems.at[tag],
                recv_sem=recv_sems.at[tag], device_id=col_peer(peer), device_id_type=MESH,
            ).start()
            return carry
        lax.fori_loop(1, n, one, 0)

    chunks = n // 4
    order = sorted(range(chunks), key=lambda k: min(k, chunks - k))

    def to_col_chunks(src, dst, tag, which):
        def one(step, carry):
            peer = lax.rem(c + step, n)
            pltpu.make_async_remote_copy(
                src_ref=src, dst_ref=dst.at[c], send_sem=send_sems.at[tag],
                recv_sem=chunk_sems.at[which, lax.div(c, 4)], device_id=col_peer(peer),
                device_id_type=MESH,
            ).start()
            return carry
        lax.fori_loop(1, n, one, 0)

    def chunk_at(dst, which, step):
        chunk = lax.rem(lax.div(c, 4) + order[step], chunks)
        some = dst.at[pl.ds(0, 3 if step == 0 else 4)]
        pltpu.make_async_copy(some, some, chunk_sems.at[which, chunk]).wait()
        return chunk

    def arrived(dst, tag):
        all_but_one = dst.at[pl.ds(0, n - 1)]
        pltpu.make_async_copy(all_but_one, all_but_one, recv_sems.at[tag]).wait()

    def departed(dst, tag):
        all_but_one = dst.at[pl.ds(0, n - 1)]
        pltpu.make_async_copy(all_but_one, all_but_one, send_sems.at[tag]).wait()

    def total(ref):
        parts = [ref[i] for i in range(n)]
        while len(parts) > 1:
            parts = [parts[i] + parts[i + 1] for i in range(0, len(parts), 2)]
        return parts[0]

    pl.semaphore_wait(barrier, 2 * (n - 1))

    to_col_chunks(geo, gcol, 0, 3)
    to_row(lambda peer: geo, grow, 1)
    to_col_chunks(wp, wcol, 2, 0)
    to_row(lambda peer: wp, wrow, 14)
    gcol[c] = geo[...]
    grow[r] = geo[...]
    wcol[c] = wp[...]
    wrow[r] = wp[...]

    def spread(ref, pair, count, place):
        tile = jnp.where(low4, ref[2 * pair], ref[2 * pair + 1])
        turned = jnp.concatenate([tile, tile], axis=0).T
        for axis in range(count):
            src_b[axis, pl.ds(pl.multiple_of(place * LANES, LANES), LANES), :] = jnp.broadcast_to(
                turned[:, axis:axis + 1], (LANES, LANES)
            )

    for step in range(chunks):
        chunk = chunk_at(gcol, 3, step)
        for part in range(2):
            spread(gcol, 2 * chunk + part, 4, 2 * chunk + part)
    arrived(grow, 1)
    for q in range(tiles):
        tgt[:, q * LANES:(q + 1) * LANES] = jnp.where(low4, grow[2 * q], grow[2 * q + 1])

    def split(x):
        high = x.astype(BF16)
        return high, (x - high.astype(F32)).astype(BF16)

    def target_tile(q):
        lanes = pl.ds(pl.multiple_of(q * LANES, LANES), LANES)
        return lanes, [
            jnp.broadcast_to(tgt[axis:axis + 1, lanes], (8, LANES)) for axis in range(4)
        ]

    def form(rows, lanes, target, target_sq, patch):
        sx, sy, sz, s_rad = [src_b[axis, rows, :] for axis in range(4)]
        dx, dy, dz = target[0] - sx, target[1] - sy, target[2] - sz
        dist_sq = dx * dx + dy * dy + dz * dz
        if patch is not None:
            dist_sq = jnp.where(patch, 1.0, dist_sq)
        inv = lax.rsqrt(dist_sq)
        inv_sq = inv * inv
        scaled = far_scale * inv
        sized = scaled * ((target_sq + s_rad * s_rad) * inv_sq)
        iso = scaled + sized * (1.0 / 3.0)
        if patch is not None:
            iso = jnp.where(patch, self_scale / target[3], iso)
        along = (scaled - sized) * inv_sq
        ax, ay, az = along * dx, along * dy, along * dz
        mob[0, rows, lanes] = ax * dx + iso
        mob[1, rows, lanes] = ay * dy + iso
        mob[2, rows, lanes] = az * dz + iso
        mob[3, rows, lanes] = ax * dy
        mob[4, rows, lanes] = ay * dz
        mob[5, rows, lanes] = az * dx

    def form_tile(q, carry):
        lanes, target = target_tile(q)
        target_sq = target[3] * target[3]

        def form_row(i, inner):
            form(pl.ds(pl.multiple_of(i * 8, 8), 8), lanes, target, target_sq, None)
            return inner
        lax.fori_loop(0, span // 8, form_row, 0, unroll=8)
        return carry
    lax.fori_loop(0, tiles, form_tile, 0)

    lanes, target = target_tile(lax.div(r, 2))
    at_own = lane8 - lax.rem(r, 2) * HALF
    for i in range(HALF // 8):
        same = lax.broadcasted_iota(jnp.int32, (8, LANES), 0) + 8 * i == at_own
        form(
            pl.ds(pl.multiple_of(c * HALF + 8 * i, 8), 8), lanes, target,
            target[3] * target[3], same,
        )

    def unpack_pair(ref, p, axis):
        first = ref[2 * p, kh * axis:kh * (axis + 1), :]
        second = ref[2 * p + 1, kh * axis:kh * (axis + 1), :]
        return jnp.concatenate(
            [jnp.where(low_k, first, swap(second)), jnp.where(low_k, swap(first), second)], axis=0
        )

    arrived(wrow, 14)
    for p in range(tiles):
        cols = slice(p * LANES, (p + 1) * LANES)
        for axis in range(3):
            high, rest = split(unpack_pair(wrow, p, axis))
            w_tgt[axis, 0:vectors, cols] = high
            w_tgt[axis, vectors:2 * vectors, cols] = rest

    width = 4 * HALF
    for step in range(chunks):
        chunk = chunk_at(wcol, 0, step)
        for part in range(2):
            cols = pl.ds(pl.multiple_of(chunk * width + part * LANES, LANES), LANES)
            for axis in range(3):
                high, rest = split(unpack_pair(wcol, 2 * chunk + part, axis))
                for copy in (axis, axis + 3):
                    if copy < 4:
                        base = vectors * copy
                        fields[base:base + vectors, cols] = high
                        fields[4 * vectors + base:4 * vectors + base + vectors, cols] = rest

    def basis_chunk(t, carry):
        lanes = pl.ds(pl.multiple_of(t * width, width), width)
        sums = [None] * 3

        def add(axis, value):
            sums[axis] = value if sums[axis] is None else sums[axis] + value
        for slot, (a, b) in enumerate(PAIRS):
            first = vectors * a
            count = vectors if a == b else 2 * vectors
            by_high = by_rest = None
            for d in range(chunks):
                high, rest = split(mob[slot, d * width:(d + 1) * width, lanes])
                cols = slice(d * width, (d + 1) * width)
                lhs_high = fields[first:first + count, cols]
                lhs_rest = fields[4 * vectors + first:4 * vectors + first + count, cols]
                both = jnp.concatenate([lhs_high, lhs_rest], axis=0)
                dot_high = jnp.dot(both, high, preferred_element_type=F32)
                dot_rest = jnp.dot(lhs_high, rest, preferred_element_type=F32)
                by_high = dot_high if by_high is None else by_high + dot_high
                by_rest = dot_rest if by_rest is None else by_rest + dot_rest
            value = by_high[0:count] + by_high[count:2 * count] + by_rest
            add(b, value[0:vectors])
            if a != b:
                add(a, value[vectors:2 * vectors])
        for axis in range(3):
            p_tgt[axis, :, lanes] = sums[axis]
        return carry
    lax.fori_loop(0, span // width, basis_chunk, 0)

    rhs = [jnp.concatenate([rhs_in[axis:axis + 1, :]] * 2, axis=1) for axis in range(3)]
    row32 = lax.broadcasted_iota(jnp.int32, (vectors, LANES), 0)
    lane32 = lax.broadcasted_iota(jnp.int32, (vectors, LANES), 1)

    gram = None
    load = None
    for axis in range(3):
        high, rest = split(p_tgt[axis])
        along_lanes = (((1,), (1,)), ((), ()))
        by_high = lax.dot_general(w_tgt[axis], high, along_lanes, preferred_element_type=F32)
        by_rest = lax.dot_general(
            w_tgt[axis, 0:vectors, :], rest, along_lanes, preferred_element_type=F32
        )
        term = by_high[0:vectors] + by_high[vectors:2 * vectors] + by_rest
        block = wp[kh * axis:kh * (axis + 1), :]
        block = jnp.where(lane32 < HALF, jnp.concatenate([block, swap(block)], axis=0), 0.0)
        load_term = block * rhs[axis]
        gram = term if gram is None else gram + term
        load = load_term if load is None else load + load_term
    load = jnp.sum(load, axis=1, keepdims=True)
    wide = jnp.concatenate([gram, jnp.zeros((vectors, LANES - vectors), F32)], axis=1)
    groups = vectors // 8
    packed = wide[0:8]
    for g in range(1, groups):
        packed = packed + pltpu.roll(wide[8 * g:8 * g + 8], vectors * g, 1)
    gram_a[0:8, :] = packed
    gram_a[8:9, :] = jnp.sum(jnp.where(lane32 == row32, load, 0.0), axis=0, keepdims=True)
    to_row(lambda peer: gram_a, gram_row, 4)
    gram_row[r] = gram_a[...]

    for q in range(tiles):
        for axis in range(3):
            piece = p_tgt[axis, :, q * LANES:(q + 1) * LANES]
            lower, upper = piece[:kh], piece[kh:]
            slot_rows = slice(kh * axis, kh * (axis + 1))
            aw_send[2 * q, slot_rows, :] = jnp.where(low_k, lower, swap(upper))
            aw_send[2 * q + 1, slot_rows, :] = jnp.where(low_k, swap(lower), upper)
    to_row(lambda peer: aw_send.at[peer], aw_recv, 3)
    aw_recv[r] = aw_send[r]
    arrived(gram_row, 4)
    gram_b[...] = total(gram_row)
    to_col(gram_b, gram_col, 5)
    gram_col[c] = gram_b[...]
    arrived(gram_col, 5)
    arrived(aw_recv, 3)
    aw[...] = total(aw_recv)
    both = total(gram_col)
    packed, load_row = both[0:8], both[8:9]
    pieces = [packed]
    for g in range(1, groups):
        pieces.append(pltpu.roll(packed, LANES - vectors * g, 1))
    gram = jnp.concatenate(pieces, axis=0)
    load = jnp.sum(jnp.where(lane32 == row32, load_row, 0.0), axis=1, keepdims=True)

    system = jnp.where(lane32 < vectors, gram, jnp.where(lane32 == row32 + vectors, 1.0, 0.0))
    system = jnp.where(lane32 == 2 * vectors, load, system)
    for j in range(vectors):
        column = jnp.broadcast_to(system[:, j:j + 1], (vectors, LANES))
        scaled_row = system[j:j + 1, :] * (1.0 / column[j:j + 1, :])
        system = jnp.where(row32 == j, scaled_row, system - column * scaled_row)
    inverse = jnp.where(jnp.logical_and(lane32 >= vectors, lane32 < 2 * vectors), system, 0.0)
    coarse = system[:, 2 * vectors:2 * vectors + 1]

    def weights_of(column):
        return jnp.where(low_k, column[:kh], column[kh:])

    def combine(ref, weights):
        out = []
        for axis in range(3):
            s = jnp.sum(ref[kh * axis:kh * (axis + 1), :] * weights, axis=0, keepdims=True)
            out.append(s + swap(s))
        return out

    def solve(vector_row):
        return weights_of(jnp.sum(inverse * vector_row, axis=1, keepdims=True))

    def dots_row(field):
        s = None
        for axis in range(3):
            term = aw[kh * axis:kh * (axis + 1), :] * field[axis]
            s = term if s is None else s + term
        lower = jnp.sum(jnp.where(low_k, s, 0.0), axis=1, keepdims=True)
        upper = jnp.sum(jnp.where(low_k, 0.0, s), axis=1, keepdims=True)
        spots = jnp.where(lane_k == row_k + vectors, lower, 0.0)
        spots = spots + jnp.where(lane_k == row_k + vectors + kh, upper, 0.0)
        return jnp.sum(spots, axis=0, keepdims=True)

    def dot_local(x, y):
        s = x[0] * y[0] + x[1] * y[1] + x[2] * y[2]
        return jnp.sum(jnp.where(low1, s, 0.0), axis=1, keepdims=True)

    def stat(ref, row_value):
        ref[...] = row_value

    def at_lane(index, value):
        return jnp.where(lane1 == index, value, 0.0)

    def put(ref, field, last):
        for axis in range(3):
            ref[axis:axis + 1, :] = field[axis]
        ref[3:4, :] = last

    def product(vec_all, which, send, weigh, forward):
        zero = jnp.zeros((8, LANES), F32)
        sums = [zero] * (3 * tiles)
        half = 3 * tiles // 2
        for step in range(chunks):
            chunk = chunk_at(vec_all, which, step)
            for part in range(2):
                spread(vec_all, 2 * chunk + part, 3, 2 * step + part)
            for part in range(2):
                def one(i, carry, step=step, chunk=chunk, part=part):
                    rows = pl.ds(pl.multiple_of(chunk * width + i * 8, 8), 8)
                    at = pl.ds(pl.multiple_of(step * width + i * 8, 8), 8)
                    value = [src_b[axis, at, :] for axis in range(3)]
                    out = []
                    for q in range(tiles // 2):
                        base = (part * (tiles // 2) + q) * LANES
                        m = [mob[slot, rows, base:base + LANES] for slot in range(6)]
                        for axis in range(3):
                            out.append(
                                carry[3 * q + axis]
                                + (m[SLOT[axis, 0]] * value[0] + m[SLOT[axis, 1]] * value[1])
                                + m[SLOT[axis, 2]] * value[2]
                            )
                    return tuple(out)
                mine_sums = tuple(sums[part * half:(part + 1) * half])
                sums[part * half:(part + 1) * half] = lax.fori_loop(
                    0, width // 8, one, mine_sums, unroll=4
                )
        forward()
        dots = []
        for q in range(tiles):
            for axis in range(3):
                value = jnp.sum(sums[3 * q + axis], axis=0, keepdims=True)
                send[q, axis:axis + 1, :] = value
                if weigh is not None:
                    weight = jnp.where(
                        low1, weigh[2 * q, axis:axis + 1, :], weigh[2 * q + 1, axis:axis + 1, :]
                    )
                    dots.append(value * weight)
        last = jnp.zeros((1, LANES), F32)
        if weigh is not None:
            while len(dots) > 1:
                dots = [sum(dots[i:i + 2]) for i in range(0, len(dots), 2)]
            last = jnp.broadcast_to(jnp.sum(dots[0], axis=1, keepdims=True), (1, LANES))
        for q in range(tiles):
            send[q, 3:4, :] = last

    def mine(recv):
        tile = total(recv)
        odd = lax.rem(r, 2)
        keep = jnp.where(low1, 1 - odd, odd) == 1
        out = []
        for axis in range(3):
            half = jnp.where(keep, tile[axis:axis + 1, :], 0.0)
            out.append(half + swap(half))
        return out, tile[3:4, :]

    weights = weights_of(coarse)
    image0 = combine(aw, weights)
    r0 = [rhs[axis] - image0[axis] for axis in range(3)]

    put(vec_a, r0, jnp.zeros((1, LANES), F32))
    to_col_chunks(vec_a, vec_col_a, 6, 1)
    vec_col_a[c] = vec_a[...]
    stat(stat_a, dots_row(r0) + at_lane(0, dot_local(r0, r0)))
    to_row(lambda peer: stat_a, stat_row_a, 7)
    stat_row_a[r] = stat_a[...]
    x0 = combine(wp, weights)

    def forward_a():
        arrived(stat_row_a, 7)
        stat_b[...] = total(stat_row_a)
        to_col(stat_b, stat_col_b, 9)
        stat_col_b[c] = stat_b[...]
    product(vec_col_a, 1, part_a, None, forward_a)
    to_row(lambda peer: part_a.at[lax.div(peer, 2)], part_row_a, 8)
    part_row_a[r] = part_a[lax.div(r, 2)]
    arrived(stat_col_b, 9)
    sums0 = total(stat_col_b)[0:1, :]
    norm0 = sums0[:, 0:1]
    weights = solve(sums0)
    shift_image = combine(aw, weights)
    arrived(part_row_a, 8)
    z0, _ = mine(part_row_a)
    q0 = [z0[axis] - shift_image[axis] for axis in range(3)]

    put(vec_c, q0, jnp.zeros((1, LANES), F32))
    to_col_chunks(vec_c, vec_col_c, 10, 2)
    vec_col_c[c] = vec_c[...]
    shift = combine(wp, weights)
    d0 = [r0[axis] - shift[axis] for axis in range(3)]
    put(
        vec_d, q0,
        dots_row(q0) + at_lane(0, dot_local(d0, q0)) + at_lane(1, dot_local(r0, q0))
        + at_lane(2, dot_local(q0, q0)),
    )
    to_row(lambda peer: vec_d, vec_row_c, 11)
    vec_row_c[r] = vec_d[...]

    def forward_c():
        arrived(vec_row_c, 11)
        stat_d[...] = total(vec_row_c)[3:4, :]
        to_col(stat_d, stat_col_d, 13)
        stat_col_d[c] = stat_d[...]
    product(vec_col_c, 2, part_c, vec_row_c, forward_c)
    to_row(lambda peer: part_c.at[lax.div(peer, 2)], part_row_c, 12)
    part_row_c[r] = part_c[lax.div(r, 2)]
    arrived(stat_col_d, 13)
    sums1 = total(stat_col_d)
    step0 = norm0 / sums1[:, 0:1]
    norm1 = norm0 - 2.0 * step0 * sums1[:, 1:2] + step0 * step0 * sums1[:, 2:3]
    beta = norm1 / norm0
    weights = solve(sums0 - step0 * sums1)
    shift = combine(wp, weights)
    shift_image = combine(aw, weights)
    x1 = [x0[axis] + step0 * d0[axis] for axis in range(3)]
    r1 = [r0[axis] - step0 * q0[axis] for axis in range(3)]
    d1 = [r1[axis] + beta * d0[axis] - shift[axis] for axis in range(3)]
    inner = jnp.sum(inverse * sums1, axis=1, keepdims=True)
    column = jnp.sum(jnp.where(lane32 == row32 + vectors, sums1, 0.0), axis=1, keepdims=True)
    removed = jnp.sum(inner * column, axis=0, keepdims=True)
    factor = 1.0 + beta
    fixed = factor * factor * sums1[:, 0:1] - 2.0 * factor * step0 * sums1[:, 2:3]
    arrived(part_row_c, 12)
    y0, block_sum = mine(part_row_c)
    stat_f[...] = block_sum
    to_col(stat_f, stat_col_f, 15)
    stat_col_f[c] = stat_f[...]
    q1 = [
        (z0[axis] - step0 * y0[axis]) + beta * q0[axis] - shift_image[axis] for axis in range(3)
    ]
    arrived(stat_col_f, 15)
    curvature = fixed + step0 * step0 * (total(stat_col_f)[:, 0:1] - removed)
    step1 = norm1 / curvature
    for axis in range(3):
        out_ref[axis:axis + 1, :] = x1[axis] + step1 * d1[axis]
        out_ref[4 + axis:5 + axis, :] = r1[axis] - step1 * q1[axis]

    for tag, dst in enumerate((
        gcol, grow, wcol, aw_recv, gram_row, gram_col, vec_col_a, stat_row_a, part_row_a,
        stat_col_b, vec_col_c, vec_row_c, part_row_c, stat_col_d, wrow, stat_col_f,
    )):
        departed(dst, tag)


def body(n, positions, radii, basis, rhs):
    vectors = basis.shape[0]
    kh = vectors // 2
    span = n * HALF
    row, rows = pltpu.VMEM((1, LANES), F32), pltpu.VMEM((n, 1, LANES), F32)
    tile, tile_slots = pltpu.VMEM((4, LANES), F32), pltpu.VMEM((n, 4, LANES), F32)
    parts = pltpu.VMEM((span // LANES, 4, LANES), F32)
    field, field_slots = pltpu.VMEM((3 * kh, LANES), F32), pltpu.VMEM((n, 3 * kh, LANES), F32)
    two, two_slots = pltpu.VMEM((9, LANES), F32), pltpu.VMEM((n, 9, LANES), F32)
    vmem = pl.BlockSpec(memory_space=pltpu.VMEM)
    anywhere = pl.BlockSpec(memory_space=pl.ANY)
    out = pl.pallas_call(
        functools.partial(kernel, n, vectors),
        out_shape=jax.ShapeDtypeStruct((8, LANES), F32),
        in_specs=[anywhere] * 4,
        out_specs=vmem,
        scratch_shapes=[
            pltpu.VMEM((3, HALF), F32), pltpu.VMEM((1, HALF), F32),
            pltpu.VMEM((3, vectors, HALF), F32), pltpu.VMEM((3, HALF), F32),
            tile, field,
            tile_slots, tile_slots, field_slots, field_slots,
            pltpu.VMEM((4, span, LANES), F32),
            pltpu.VMEM((4, span), F32),
            pltpu.VMEM((6, span, span), F32),
            pltpu.VMEM((8 * vectors, span), BF16),
            pltpu.VMEM((3, 2 * vectors, span), BF16), pltpu.VMEM((3, vectors, span), F32),
            field_slots, field_slots, field,
            two, two_slots, two, two_slots,
            tile, tile_slots, row, rows, parts, tile_slots, row, rows,
            tile, tile, tile_slots, tile_slots, parts, tile_slots, row, rows,
            row, rows,
            pltpu.SemaphoreType.DMA((4,)),
            pltpu.SemaphoreType.DMA((16,)),
            pltpu.SemaphoreType.DMA((16,)),
            pltpu.SemaphoreType.DMA((4, n // 4)),
        ],
        compiler_params=pltpu.CompilerParams(
            collective_id=0, has_side_effects=True, vmem_limit_bytes=60 << 20
        ),
    )(positions, radii[None], basis.transpose(1, 0, 2), rhs)
    return out[0:3, :HALF], out[4:7, :HALF]


def solution(mesh):
    return jax.shard_map(
        functools.partial(body, mesh.shape["row"]),
        mesh=mesh,
        in_specs=(
            P(None, ("row", "col")),
            P(("row", "col")),
            P(None, None, ("row", "col")),
            P(None, ("row", "col")),
        ),
        out_specs=(P(None, ("row", "col")), P(None, ("row", "col"))),
        check_vma=False,
    )
```

```python
import functools
import math

import jax
import jax.numpy as jnp
from jax import lax
from jax.experimental import pallas as pl
from jax.experimental.pallas import tpu as pltpu
from jax.sharding import PartitionSpec as P

MESH = pl.DeviceIdType.MESH
F32 = jnp.float32
BF16 = jnp.bfloat16

far_scale = 1.0 / (8.0 * math.pi)
self_scale = 1.0 / (6.0 * math.pi)

LANES = 128
HALF = 64
PAIRS = ((0, 0), (1, 1), (2, 2), (0, 1), (1, 2), (2, 0))
SLOT = {}
for _slot, (_a, _b) in enumerate(PAIRS):
    SLOT[_a, _b] = _slot
    SLOT[_b, _a] = _slot


def kernel(
    n, vectors,
    pos_ref, rad_ref, basis_ref, rhs_ref,
    out_ref,
    pos_in, rad_in, basis_in, rhs_in, geo, wp,
    grow, gcol, wcol, wrow, src_b, tgt, mob, fields, w_tgt, p_tgt, aw_send, aw_recv, aw,
    gram_a, gram_row, gram_b, gram_col,
    vec_a, vec_col_a, stat_a, stat_row_a, part_a, part_row_a, stat_b, stat_col_b,
    vec_c, vec_d, vec_col_c, vec_row_c, part_c, part_row_c, stat_d, stat_col_d,
    stat_f, stat_col_f,
    in_sems, send_sems, recv_sems, chunk_sems,
):
    at_row = lax.axis_index("row")
    at_col = lax.axis_index("col")
    core = lax.rem(at_row, 2)
    y_low = lax.rem(at_col, 2)
    r = lax.div(at_row, 2) * 2 + y_low
    c = lax.div(at_col, 2) * 2 + core

    def row_peer(index):
        return (lax.div(index, 2) * 2 + core, lax.div(at_col, 2) * 2 + lax.rem(index, 2))

    def col_peer(index):
        return (lax.div(at_row, 2) * 2 + lax.rem(index, 2), lax.div(index, 2) * 2 + y_low)

    kh = vectors // 2
    span = n * HALF
    tiles = span // LANES

    barrier = pltpu.get_barrier_semaphore()

    def greet(step, carry):
        pl.semaphore_signal(
            barrier, inc=1, device_id=row_peer(lax.rem(r + step, n)), device_id_type=MESH
        )
        pl.semaphore_signal(
            barrier, inc=1, device_id=col_peer(lax.rem(c + step, n)), device_id_type=MESH
        )
        return carry
    lax.fori_loop(1, n, greet, 0)

    reads = [
        pltpu.make_async_copy(src, dst, in_sems.at[i])
        for i, (src, dst) in enumerate((
            (pos_ref, pos_in), (rad_ref, rad_in), (basis_ref, basis_in), (rhs_ref, rhs_in)
        ))
    ]
    for read in reads:
        read.start()
    for read in reads:
        read.wait()
    for half in range(2):
        lanes = slice(half * HALF, (half + 1) * HALF)
        geo[0:3, lanes] = pos_in[...]
        geo[3:4, lanes] = rad_in[...]
        for axis in range(3):
            wp[kh * axis:kh * (axis + 1), lanes] = basis_in[axis, kh * half:kh * (half + 1), :]

    lane1 = lax.broadcasted_iota(jnp.int32, (1, LANES), 1)
    lane4 = lax.broadcasted_iota(jnp.int32, (4, LANES), 1)
    lane8 = lax.broadcasted_iota(jnp.int32, (8, LANES), 1)
    lane_k = lax.broadcasted_iota(jnp.int32, (kh, LANES), 1)
    row_k = lax.broadcasted_iota(jnp.int32, (kh, LANES), 0)
    low1, low4, low_k = lane1 < HALF, lane4 < HALF, lane_k < HALF

    def swap(x):
        return pltpu.roll(x, HALF, 1)

    def to_row(src, dst, tag):
        def one(step, carry):
            peer = lax.rem(r + step, n)
            pltpu.make_async_remote_copy(
                src_ref=src(peer), dst_ref=dst.at[r], send_sem=send_sems.at[tag],
                recv_sem=recv_sems.at[tag], device_id=row_peer(peer), device_id_type=MESH,
            ).start()
            return carry
        lax.fori_loop(1, n, one, 0)

    def to_col(src, dst, tag):
        def one(step, carry):
            peer = lax.rem(c + step, n)
            pltpu.make_async_remote_copy(
                src_ref=src, dst_ref=dst.at[c], send_sem=send_sems.at[tag],
                recv_sem=recv_sems.at[tag], device_id=col_peer(peer), device_id_type=MESH,
            ).start()
            return carry
        lax.fori_loop(1, n, one, 0)

    chunks = n // 4
    order = sorted(range(chunks), key=lambda k: min(k, chunks - k))

    def to_col_chunks(src, dst, tag, which):
        def one(step, carry):
            peer = lax.rem(c + step, n)
            pltpu.make_async_remote_copy(
                src_ref=src, dst_ref=dst.at[c], send_sem=send_sems.at[tag],
                recv_sem=chunk_sems.at[which, lax.div(c, 4)], device_id=col_peer(peer),
                device_id_type=MESH,
            ).start()
            return carry
        lax.fori_loop(1, n, one, 0)

    def chunk_at(dst, which, step):
        chunk = lax.rem(lax.div(c, 4) + order[step], chunks)
        some = dst.at[pl.ds(0, 3 if step == 0 else 4)]
        pltpu.make_async_copy(some, some, chunk_sems.at[which, chunk]).wait()
        return chunk

    def arrived(dst, tag):
        all_but_one = dst.at[pl.ds(0, n - 1)]
        pltpu.make_async_copy(all_but_one, all_but_one, recv_sems.at[tag]).wait()

    def departed(dst, tag):
        all_but_one = dst.at[pl.ds(0, n - 1)]
        pltpu.make_async_copy(all_but_one, all_but_one, send_sems.at[tag]).wait()

    def total(ref):
        parts = [ref[i] for i in range(n)]
        while len(parts) > 1:
            parts = [parts[i] + parts[i + 1] for i in range(0, len(parts), 2)]
        return parts[0]

    pl.semaphore_wait(barrier, 2 * (n - 1))

    to_col_chunks(geo, gcol, 0, 3)
    to_row(lambda peer: geo, grow, 1)
    to_col_chunks(wp, wcol, 2, 0)
    to_row(lambda peer: wp, wrow, 14)
    gcol[c] = geo[...]
    grow[r] = geo[...]
    wcol[c] = wp[...]
    wrow[r] = wp[...]

    def spread(ref, pair, count, place):
        tile = jnp.where(low4, ref[2 * pair], ref[2 * pair + 1])
        turned = jnp.concatenate([tile, tile], axis=0).T
        for axis in range(count):
            src_b[axis, pl.ds(pl.multiple_of(place * LANES, LANES), LANES), :] = jnp.broadcast_to(
                turned[:, axis:axis + 1], (LANES, LANES)
            )

    for step in range(chunks):
        chunk = chunk_at(gcol, 3, step)
        for part in range(2):
            spread(gcol, 2 * chunk + part, 4, 2 * chunk + part)
    arrived(grow, 1)
    for q in range(tiles):
        tgt[:, q * LANES:(q + 1) * LANES] = jnp.where(low4, grow[2 * q], grow[2 * q + 1])

    def split(x):
        high = x.astype(BF16)
        return high, (x - high.astype(F32)).astype(BF16)

    def target_tile(q):
        lanes = pl.ds(pl.multiple_of(q * LANES, LANES), LANES)
        return lanes, [
            jnp.broadcast_to(tgt[axis:axis + 1, lanes], (8, LANES)) for axis in range(4)
        ]

    def form(rows, lanes, target, target_sq, patch):
        sx, sy, sz, s_rad = [src_b[axis, rows, :] for axis in range(4)]
        dx, dy, dz = target[0] - sx, target[1] - sy, target[2] - sz
        dist_sq = dx * dx + dy * dy + dz * dz
        if patch is not None:
            dist_sq = jnp.where(patch, 1.0, dist_sq)
        inv = lax.rsqrt(dist_sq)
        inv_sq = inv * inv
        scaled = far_scale * inv
        sized = scaled * ((target_sq + s_rad * s_rad) * inv_sq)
        iso = scaled + sized * (1.0 / 3.0)
        if patch is not None:
            iso = jnp.where(patch, self_scale / target[3], iso)
        along = (scaled - sized) * inv_sq
        ax, ay, az = along * dx, along * dy, along * dz
        mob[0, rows, lanes] = ax * dx + iso
        mob[1, rows, lanes] = ay * dy + iso
        mob[2, rows, lanes] = az * dz + iso
        mob[3, rows, lanes] = ax * dy
        mob[4, rows, lanes] = ay * dz
        mob[5, rows, lanes] = az * dx

    def form_tile(q, carry):
        lanes, target = target_tile(q)
        target_sq = target[3] * target[3]

        def form_row(i, inner):
            form(pl.ds(pl.multiple_of(i * 8, 8), 8), lanes, target, target_sq, None)
            return inner
        lax.fori_loop(0, span // 8, form_row, 0, unroll=8)
        return carry
    lax.fori_loop(0, tiles, form_tile, 0)

    lanes, target = target_tile(lax.div(r, 2))
    at_own = lane8 - lax.rem(r, 2) * HALF
    for i in range(HALF // 8):
        same = lax.broadcasted_iota(jnp.int32, (8, LANES), 0) + 8 * i == at_own
        form(
            pl.ds(pl.multiple_of(c * HALF + 8 * i, 8), 8), lanes, target,
            target[3] * target[3], same,
        )

    def unpack_pair(ref, p, axis):
        first = ref[2 * p, kh * axis:kh * (axis + 1), :]
        second = ref[2 * p + 1, kh * axis:kh * (axis + 1), :]
        return jnp.concatenate(
            [jnp.where(low_k, first, swap(second)), jnp.where(low_k, swap(first), second)], axis=0
        )

    arrived(wrow, 14)
    for p in range(tiles):
        cols = slice(p * LANES, (p + 1) * LANES)
        for axis in range(3):
            high, rest = split(unpack_pair(wrow, p, axis))
            w_tgt[axis, 0:vectors, cols] = high
            w_tgt[axis, vectors:2 * vectors, cols] = rest

    width = 4 * HALF
    for step in range(chunks):
        chunk = chunk_at(wcol, 0, step)
        for part in range(2):
            cols = pl.ds(pl.multiple_of(chunk * width + part * LANES, LANES), LANES)
            for axis in range(3):
                high, rest = split(unpack_pair(wcol, 2 * chunk + part, axis))
                for copy in (axis, axis + 3):
                    if copy < 4:
                        base = vectors * copy
                        fields[base:base + vectors, cols] = high
                        fields[4 * vectors + base:4 * vectors + base + vectors, cols] = rest

    def basis_chunk(t, carry):
        lanes = pl.ds(pl.multiple_of(t * width, width), width)
        sums = [None] * 3

        def add(axis, value):
            sums[axis] = value if sums[axis] is None else sums[axis] + value
        for slot, (a, b) in enumerate(PAIRS):
            first = vectors * a
            count = vectors if a == b else 2 * vectors
            by_high = by_rest = None
            for d in range(chunks):
                high, rest = split(mob[slot, d * width:(d + 1) * width, lanes])
                cols = slice(d * width, (d + 1) * width)
                lhs_high = fields[first:first + count, cols]
                lhs_rest = fields[4 * vectors + first:4 * vectors + first + count, cols]
                both = jnp.concatenate([lhs_high, lhs_rest], axis=0)
                dot_high = jnp.dot(both, high, preferred_element_type=F32)
                dot_rest = jnp.dot(lhs_high, rest, preferred_element_type=F32)
                by_high = dot_high if by_high is None else by_high + dot_high
                by_rest = dot_rest if by_rest is None else by_rest + dot_rest
            value = by_high[0:count] + by_high[count:2 * count] + by_rest
            add(b, value[0:vectors])
            if a != b:
                add(a, value[vectors:2 * vectors])
        for axis in range(3):
            p_tgt[axis, :, lanes] = sums[axis]
        return carry
    lax.fori_loop(0, span // width, basis_chunk, 0)

    rhs = [jnp.concatenate([rhs_in[axis:axis + 1, :]] * 2, axis=1) for axis in range(3)]
    row32 = lax.broadcasted_iota(jnp.int32, (vectors, LANES), 0)
    lane32 = lax.broadcasted_iota(jnp.int32, (vectors, LANES), 1)

    gram = None
    load = None
    for axis in range(3):
        high, rest = split(p_tgt[axis])
        along_lanes = (((1,), (1,)), ((), ()))
        by_high = lax.dot_general(w_tgt[axis], high, along_lanes, preferred_element_type=F32)
        by_rest = lax.dot_general(
            w_tgt[axis, 0:vectors, :], rest, along_lanes, preferred_element_type=F32
        )
        term = by_high[0:vectors] + by_high[vectors:2 * vectors] + by_rest
        block = wp[kh * axis:kh * (axis + 1), :]
        block = jnp.where(lane32 < HALF, jnp.concatenate([block, swap(block)], axis=0), 0.0)
        load_term = block * rhs[axis]
        gram = term if gram is None else gram + term
        load = load_term if load is None else load + load_term
    load = jnp.sum(load, axis=1, keepdims=True)
    wide = jnp.concatenate([gram, jnp.zeros((vectors, LANES - vectors), F32)], axis=1)
    groups = vectors // 8
    packed = wide[0:8]
    for g in range(1, groups):
        packed = packed + pltpu.roll(wide[8 * g:8 * g + 8], vectors * g, 1)
    gram_a[0:8, :] = packed
    gram_a[8:9, :] = jnp.sum(jnp.where(lane32 == row32, load, 0.0), axis=0, keepdims=True)
    to_row(lambda peer: gram_a, gram_row, 4)
    gram_row[r] = gram_a[...]

    for q in range(tiles):
        for axis in range(3):
            piece = p_tgt[axis, :, q * LANES:(q + 1) * LANES]
            lower, upper = piece[:kh], piece[kh:]
            slot_rows = slice(kh * axis, kh * (axis + 1))
            aw_send[2 * q, slot_rows, :] = jnp.where(low_k, lower, swap(upper))
            aw_send[2 * q + 1, slot_rows, :] = jnp.where(low_k, swap(lower), upper)
    to_row(lambda peer: aw_send.at[peer], aw_recv, 3)
    aw_recv[r] = aw_send[r]
    arrived(gram_row, 4)
    gram_b[...] = total(gram_row)
    to_col(gram_b, gram_col, 5)
    gram_col[c] = gram_b[...]
    arrived(gram_col, 5)
    both = total(gram_col)
    packed, load_row = both[0:8], both[8:9]
    pieces = [packed]
    for g in range(1, groups):
        pieces.append(pltpu.roll(packed, LANES - vectors * g, 1))
    gram = jnp.concatenate(pieces, axis=0)
    load = jnp.sum(jnp.where(lane32 == row32, load_row, 0.0), axis=1, keepdims=True)

    system = jnp.where(lane32 < vectors, gram, jnp.where(lane32 == row32 + vectors, 1.0, 0.0))
    system = jnp.where(lane32 == 2 * vectors, load, system)
    for j in range(vectors):
        column = jnp.broadcast_to(system[:, j:j + 1], (vectors, LANES))
        scaled_row = system[j:j + 1, :] * (1.0 / column[j:j + 1, :])
        system = jnp.where(row32 == j, scaled_row, system - column * scaled_row)
    inverse = jnp.where(jnp.logical_and(lane32 >= vectors, lane32 < 2 * vectors), system, 0.0)
    coarse = system[:, 2 * vectors:2 * vectors + 1]

    def weights_of(column):
        return jnp.where(low_k, column[:kh], column[kh:])

    def combine(ref, weights):
        out = []
        for axis in range(3):
            s = jnp.sum(ref[kh * axis:kh * (axis + 1), :] * weights, axis=0, keepdims=True)
            out.append(s + swap(s))
        return out

    def solve(vector_row):
        return weights_of(jnp.sum(inverse * vector_row, axis=1, keepdims=True))

    def dots_row(field):
        s = None
        for axis in range(3):
            term = aw[kh * axis:kh * (axis + 1), :] * field[axis]
            s = term if s is None else s + term
        lower = jnp.sum(jnp.where(low_k, s, 0.0), axis=1, keepdims=True)
        upper = jnp.sum(jnp.where(low_k, 0.0, s), axis=1, keepdims=True)
        spots = jnp.where(lane_k == row_k + vectors, lower, 0.0)
        spots = spots + jnp.where(lane_k == row_k + vectors + kh, upper, 0.0)
        return jnp.sum(spots, axis=0, keepdims=True)

    def dot_local(x, y):
        s = x[0] * y[0] + x[1] * y[1] + x[2] * y[2]
        return jnp.sum(jnp.where(low1, s, 0.0), axis=1, keepdims=True)

    def stat(ref, row_value):
        ref[...] = row_value

    def at_lane(index, value):
        return jnp.where(lane1 == index, value, 0.0)

    def put(ref, field, last):
        for axis in range(3):
            ref[axis:axis + 1, :] = field[axis]
        ref[3:4, :] = last

    def product(vec_all, which, send, weigh, forward):
        zero = jnp.zeros((8, LANES), F32)
        sums = [zero] * (3 * tiles)
        half = 3 * tiles // 2
        for step in range(chunks):
            chunk = chunk_at(vec_all, which, step)
            for part in range(2):
                spread(vec_all, 2 * chunk + part, 3, 2 * step + part)
            for part in range(2):
                def one(i, carry, step=step, chunk=chunk, part=part):
                    rows = pl.ds(pl.multiple_of(chunk * width + i * 8, 8), 8)
                    at = pl.ds(pl.multiple_of(step * width + i * 8, 8), 8)
                    value = [src_b[axis, at, :] for axis in range(3)]
                    out = []
                    for q in range(tiles // 2):
                        base = (part * (tiles // 2) + q) * LANES
                        m = [mob[slot, rows, base:base + LANES] for slot in range(6)]
                        for axis in range(3):
                            out.append(
                                carry[3 * q + axis]
                                + (m[SLOT[axis, 0]] * value[0] + m[SLOT[axis, 1]] * value[1])
                                + m[SLOT[axis, 2]] * value[2]
                            )
                    return tuple(out)
                mine_sums = tuple(sums[part * half:(part + 1) * half])
                sums[part * half:(part + 1) * half] = lax.fori_loop(
                    0, width // 8, one, mine_sums, unroll=8
                )
        forward()
        dots = []
        for q in range(tiles):
            for axis in range(3):
                value = jnp.sum(sums[3 * q + axis], axis=0, keepdims=True)
                send[q, axis:axis + 1, :] = value
                if weigh is not None:
                    weight = jnp.where(
                        low1, weigh[2 * q, axis:axis + 1, :], weigh[2 * q + 1, axis:axis + 1, :]
                    )
                    dots.append(value * weight)
        last = jnp.zeros((1, LANES), F32)
        if weigh is not None:
            while len(dots) > 1:
                dots = [sum(dots[i:i + 2]) for i in range(0, len(dots), 2)]
            last = jnp.broadcast_to(jnp.sum(dots[0], axis=1, keepdims=True), (1, LANES))
        for q in range(tiles):
            send[q, 3:4, :] = last

    def mine(recv):
        tile = total(recv)
        odd = lax.rem(r, 2)
        keep = jnp.where(low1, 1 - odd, odd) == 1
        out = []
        for axis in range(3):
            half = jnp.where(keep, tile[axis:axis + 1, :], 0.0)
            out.append(half + swap(half))
        return out, tile[3:4, :]

    arrived(aw_recv, 3)
    aw[...] = total(aw_recv)
    weights = weights_of(coarse)
    image0 = combine(aw, weights)
    r0 = [rhs[axis] - image0[axis] for axis in range(3)]

    put(vec_a, r0, jnp.zeros((1, LANES), F32))
    to_col_chunks(vec_a, vec_col_a, 6, 1)
    vec_col_a[c] = vec_a[...]
    stat(stat_a, dots_row(r0) + at_lane(0, dot_local(r0, r0)))
    to_row(lambda peer: stat_a, stat_row_a, 7)
    stat_row_a[r] = stat_a[...]
    x0 = combine(wp, weights)

    def forward_a():
        arrived(stat_row_a, 7)
        stat_b[...] = total(stat_row_a)
        to_col(stat_b, stat_col_b, 9)
        stat_col_b[c] = stat_b[...]
    product(vec_col_a, 1, part_a, None, forward_a)
    to_row(lambda peer: part_a.at[lax.div(peer, 2)], part_row_a, 8)
    part_row_a[r] = part_a[lax.div(r, 2)]
    arrived(stat_col_b, 9)
    sums0 = total(stat_col_b)[0:1, :]
    norm0 = sums0[:, 0:1]
    weights = solve(sums0)
    shift_image = combine(aw, weights)
    arrived(part_row_a, 8)
    z0, _ = mine(part_row_a)
    q0 = [z0[axis] - shift_image[axis] for axis in range(3)]

    put(vec_c, q0, jnp.zeros((1, LANES), F32))
    to_col_chunks(vec_c, vec_col_c, 10, 2)
    vec_col_c[c] = vec_c[...]
    shift = combine(wp, weights)
    d0 = [r0[axis] - shift[axis] for axis in range(3)]
    put(
        vec_d, q0,
        dots_row(q0) + at_lane(0, dot_local(d0, q0)) + at_lane(1, dot_local(r0, q0))
        + at_lane(2, dot_local(q0, q0)),
    )
    to_row(lambda peer: vec_d, vec_row_c, 11)
    vec_row_c[r] = vec_d[...]

    def forward_c():
        arrived(vec_row_c, 11)
        stat_d[...] = total(vec_row_c)[3:4, :]
        to_col(stat_d, stat_col_d, 13)
        stat_col_d[c] = stat_d[...]
    product(vec_col_c, 2, part_c, vec_row_c, forward_c)
    to_row(lambda peer: part_c.at[lax.div(peer, 2)], part_row_c, 12)
    part_row_c[r] = part_c[lax.div(r, 2)]
    arrived(stat_col_d, 13)
    sums1 = total(stat_col_d)
    step0 = norm0 / sums1[:, 0:1]
    norm1 = norm0 - 2.0 * step0 * sums1[:, 1:2] + step0 * step0 * sums1[:, 2:3]
    beta = norm1 / norm0
    weights = solve(sums0 - step0 * sums1)
    shift = combine(wp, weights)
    shift_image = combine(aw, weights)
    x1 = [x0[axis] + step0 * d0[axis] for axis in range(3)]
    r1 = [r0[axis] - step0 * q0[axis] for axis in range(3)]
    d1 = [r1[axis] + beta * d0[axis] - shift[axis] for axis in range(3)]
    inner = jnp.sum(inverse * sums1, axis=1, keepdims=True)
    column = jnp.sum(jnp.where(lane32 == row32 + vectors, sums1, 0.0), axis=1, keepdims=True)
    removed = jnp.sum(inner * column, axis=0, keepdims=True)
    factor = 1.0 + beta
    fixed = factor * factor * sums1[:, 0:1] - 2.0 * factor * step0 * sums1[:, 2:3]
    arrived(part_row_c, 12)
    y0, block_sum = mine(part_row_c)
    stat_f[...] = block_sum
    to_col(stat_f, stat_col_f, 15)
    stat_col_f[c] = stat_f[...]
    q1 = [
        (z0[axis] - step0 * y0[axis]) + beta * q0[axis] - shift_image[axis] for axis in range(3)
    ]
    arrived(stat_col_f, 15)
    curvature = fixed + step0 * step0 * (total(stat_col_f)[:, 0:1] - removed)
    step1 = norm1 / curvature
    for axis in range(3):
        out_ref[axis:axis + 1, :] = x1[axis] + step1 * d1[axis]
        out_ref[4 + axis:5 + axis, :] = r1[axis] - step1 * q1[axis]

    for tag, dst in enumerate((
        gcol, grow, wcol, aw_recv, gram_row, gram_col, vec_col_a, stat_row_a, part_row_a,
        stat_col_b, vec_col_c, vec_row_c, part_row_c, stat_col_d, wrow, stat_col_f,
    )):
        departed(dst, tag)


def body(n, positions, radii, basis, rhs):
    vectors = basis.shape[0]
    kh = vectors // 2
    span = n * HALF
    row, rows = pltpu.VMEM((1, LANES), F32), pltpu.VMEM((n, 1, LANES), F32)
    tile, tile_slots = pltpu.VMEM((4, LANES), F32), pltpu.VMEM((n, 4, LANES), F32)
    parts = pltpu.VMEM((span // LANES, 4, LANES), F32)
    field, field_slots = pltpu.VMEM((3 * kh, LANES), F32), pltpu.VMEM((n, 3 * kh, LANES), F32)
    two, two_slots = pltpu.VMEM((9, LANES), F32), pltpu.VMEM((n, 9, LANES), F32)
    vmem = pl.BlockSpec(memory_space=pltpu.VMEM)
    anywhere = pl.BlockSpec(memory_space=pl.ANY)
    out = pl.pallas_call(
        functools.partial(kernel, n, vectors),
        out_shape=jax.ShapeDtypeStruct((8, LANES), F32),
        in_specs=[anywhere] * 4,
        out_specs=vmem,
        scratch_shapes=[
            pltpu.VMEM((3, HALF), F32), pltpu.VMEM((1, HALF), F32),
            pltpu.VMEM((3, vectors, HALF), F32), pltpu.VMEM((3, HALF), F32),
            tile, field,
            tile_slots, tile_slots, field_slots, field_slots,
            pltpu.VMEM((4, span, LANES), F32),
            pltpu.VMEM((4, span), F32),
            pltpu.VMEM((6, span, span), F32),
            pltpu.VMEM((8 * vectors, span), BF16),
            pltpu.VMEM((3, 2 * vectors, span), BF16), pltpu.VMEM((3, vectors, span), F32),
            field_slots, field_slots, field,
            two, two_slots, two, two_slots,
            tile, tile_slots, row, rows, parts, tile_slots, row, rows,
            tile, tile, tile_slots, tile_slots, parts, tile_slots, row, rows,
            row, rows,
            pltpu.SemaphoreType.DMA((4,)),
            pltpu.SemaphoreType.DMA((16,)),
            pltpu.SemaphoreType.DMA((16,)),
            pltpu.SemaphoreType.DMA((4, n // 4)),
        ],
        compiler_params=pltpu.CompilerParams(
            collective_id=0, has_side_effects=True, vmem_limit_bytes=60 << 20
        ),
    )(positions, radii[None], basis.transpose(1, 0, 2), rhs)
    return out[0:3, :HALF], out[4:7, :HALF]


def solution(mesh):
    return jax.shard_map(
        functools.partial(body, mesh.shape["row"]),
        mesh=mesh,
        in_specs=(
            P(None, ("row", "col")),
            P(("row", "col")),
            P(None, None, ("row", "col")),
            P(None, ("row", "col")),
        ),
        out_specs=(P(None, ("row", "col")), P(None, ("row", "col"))),
        check_vma=False,
    )
```

```python
import functools
import math

import jax
import jax.numpy as jnp
from jax import lax
from jax.experimental import pallas as pl
from jax.experimental.pallas import tpu as pltpu
from jax.sharding import PartitionSpec as P

MESH = pl.DeviceIdType.MESH
F32 = jnp.float32
BF16 = jnp.bfloat16

far_scale = 1.0 / (8.0 * math.pi)
self_scale = 1.0 / (6.0 * math.pi)

LANES = 128
HALF = 64
PAIRS = ((0, 0), (1, 1), (2, 2), (0, 1), (1, 2), (2, 0))
SLOT = {}
for _slot, (_a, _b) in enumerate(PAIRS):
    SLOT[_a, _b] = _slot
    SLOT[_b, _a] = _slot


def kernel(
    n, vectors,
    pos_ref, rad_ref, basis_ref, rhs_ref,
    out_ref,
    pos_in, rad_in, basis_in, rhs_in, geo, wp,
    grow, gcol, wcol, wrow, src_b, tgt, mob, fields, w_tgt, p_tgt, aw_send, aw_recv, aw,
    gram_a, gram_row, gram_b, gram_col,
    vec_a, vec_col_a, stat_a, stat_row_a, part_a, part_row_a, stat_b, stat_col_b,
    vec_c, vec_d, vec_col_c, vec_row_c, part_c, part_row_c, stat_d, stat_col_d,
    stat_f, stat_col_f,
    in_sems, send_sems, recv_sems, chunk_sems,
):
    at_row = lax.axis_index("row")
    at_col = lax.axis_index("col")
    core = lax.rem(at_row, 2)
    y_low = lax.rem(at_col, 2)
    r = lax.div(at_row, 2) * 2 + y_low
    c = lax.div(at_col, 2) * 2 + core

    def row_peer(index):
        return (lax.div(index, 2) * 2 + core, lax.div(at_col, 2) * 2 + lax.rem(index, 2))

    def col_peer(index):
        return (lax.div(at_row, 2) * 2 + lax.rem(index, 2), lax.div(index, 2) * 2 + y_low)

    kh = vectors // 2
    span = n * HALF
    tiles = span // LANES

    barrier = pltpu.get_barrier_semaphore()

    def greet(step, carry):
        pl.semaphore_signal(
            barrier, inc=1, device_id=row_peer(lax.rem(r + step, n)), device_id_type=MESH
        )
        pl.semaphore_signal(
            barrier, inc=1, device_id=col_peer(lax.rem(c + step, n)), device_id_type=MESH
        )
        return carry
    lax.fori_loop(1, n, greet, 0)

    reads = [
        pltpu.make_async_copy(src, dst, in_sems.at[i])
        for i, (src, dst) in enumerate((
            (pos_ref, pos_in), (rad_ref, rad_in), (basis_ref, basis_in), (rhs_ref, rhs_in)
        ))
    ]
    for read in reads:
        read.start()
    for read in reads:
        read.wait()
    for half in range(2):
        lanes = slice(half * HALF, (half + 1) * HALF)
        geo[0:3, lanes] = pos_in[...]
        geo[3:4, lanes] = rad_in[...]
        for axis in range(3):
            wp[kh * axis:kh * (axis + 1), lanes] = basis_in[axis, kh * half:kh * (half + 1), :]

    lane1 = lax.broadcasted_iota(jnp.int32, (1, LANES), 1)
    lane4 = lax.broadcasted_iota(jnp.int32, (4, LANES), 1)
    lane8 = lax.broadcasted_iota(jnp.int32, (8, LANES), 1)
    lane_k = lax.broadcasted_iota(jnp.int32, (kh, LANES), 1)
    row_k = lax.broadcasted_iota(jnp.int32, (kh, LANES), 0)
    low1, low4, low_k = lane1 < HALF, lane4 < HALF, lane_k < HALF

    def swap(x):
        return pltpu.roll(x, HALF, 1)

    def to_row(src, dst, tag):
        def one(step, carry):
            peer = lax.rem(r + step, n)
            pltpu.make_async_remote_copy(
                src_ref=src(peer), dst_ref=dst.at[r], send_sem=send_sems.at[tag],
                recv_sem=recv_sems.at[tag], device_id=row_peer(peer), device_id_type=MESH,
            ).start()
            return carry
        lax.fori_loop(1, n, one, 0)

    def to_col(src, dst, tag):
        def one(step, carry):
            peer = lax.rem(c + step, n)
            pltpu.make_async_remote_copy(
                src_ref=src, dst_ref=dst.at[c], send_sem=send_sems.at[tag],
                recv_sem=recv_sems.at[tag], device_id=col_peer(peer), device_id_type=MESH,
            ).start()
            return carry
        lax.fori_loop(1, n, one, 0)

    chunks = n // 4
    order = sorted(range(chunks), key=lambda k: min(k, chunks - k))

    def to_col_chunks(src, dst, tag, which):
        def one(step, carry):
            peer = lax.rem(c + step, n)
            pltpu.make_async_remote_copy(
                src_ref=src, dst_ref=dst.at[c], send_sem=send_sems.at[tag],
                recv_sem=chunk_sems.at[which, lax.div(c, 4)], device_id=col_peer(peer),
                device_id_type=MESH,
            ).start()
            return carry
        lax.fori_loop(1, n, one, 0)

    def chunk_at(dst, which, step):
        chunk = lax.rem(lax.div(c, 4) + order[step], chunks)
        some = dst.at[pl.ds(0, 3 if step == 0 else 4)]
        pltpu.make_async_copy(some, some, chunk_sems.at[which, chunk]).wait()
        return chunk

    def arrived(dst, tag):
        all_but_one = dst.at[pl.ds(0, n - 1)]
        pltpu.make_async_copy(all_but_one, all_but_one, recv_sems.at[tag]).wait()

    def departed(dst, tag):
        all_but_one = dst.at[pl.ds(0, n - 1)]
        pltpu.make_async_copy(all_but_one, all_but_one, send_sems.at[tag]).wait()

    def total(ref):
        parts = [ref[i] for i in range(n)]
        while len(parts) > 1:
            parts = [parts[i] + parts[i + 1] for i in range(0, len(parts), 2)]
        return parts[0]

    pl.semaphore_wait(barrier, 2 * (n - 1))

    to_col_chunks(geo, gcol, 0, 3)
    to_row(lambda peer: geo, grow, 1)
    to_col_chunks(wp, wcol, 2, 0)
    to_row(lambda peer: wp, wrow, 14)
    gcol[c] = geo[...]
    grow[r] = geo[...]
    wcol[c] = wp[...]
    wrow[r] = wp[...]

    def spread(ref, pair, count, place):
        tile = jnp.where(low4, ref[2 * pair], ref[2 * pair + 1])
        turned = jnp.concatenate([tile, tile], axis=0).T
        for axis in range(count):
            src_b[axis, pl.ds(pl.multiple_of(place * LANES, LANES), LANES), :] = jnp.broadcast_to(
                turned[:, axis:axis + 1], (LANES, LANES)
            )

    for step in range(chunks):
        chunk = chunk_at(gcol, 3, step)
        for part in range(2):
            spread(gcol, 2 * chunk + part, 4, 2 * chunk + part)
    arrived(grow, 1)
    for q in range(tiles):
        tgt[:, q * LANES:(q + 1) * LANES] = jnp.where(low4, grow[2 * q], grow[2 * q + 1])

    def split(x):
        high = x.astype(BF16)
        return high, (x - high.astype(F32)).astype(BF16)

    def target_tile(q):
        lanes = pl.ds(pl.multiple_of(q * LANES, LANES), LANES)
        return lanes, [
            jnp.broadcast_to(tgt[axis:axis + 1, lanes], (8, LANES)) for axis in range(4)
        ]

    def form(rows, lanes, target, target_sq, patch):
        sx, sy, sz, s_rad = [src_b[axis, rows, :] for axis in range(4)]
        dx, dy, dz = target[0] - sx, target[1] - sy, target[2] - sz
        dist_sq = dx * dx + dy * dy + dz * dz
        if patch is not None:
            dist_sq = jnp.where(patch, 1.0, dist_sq)
        inv = lax.rsqrt(dist_sq)
        inv_sq = inv * inv
        scaled = far_scale * inv
        sized = scaled * ((target_sq + s_rad * s_rad) * inv_sq)
        iso = scaled + sized * (1.0 / 3.0)
        if patch is not None:
            iso = jnp.where(patch, self_scale / target[3], iso)
        along = (scaled - sized) * inv_sq
        ax, ay, az = along * dx, along * dy, along * dz
        mob[0, rows, lanes] = ax * dx + iso
        mob[1, rows, lanes] = ay * dy + iso
        mob[2, rows, lanes] = az * dz + iso
        mob[3, rows, lanes] = ax * dy
        mob[4, rows, lanes] = ay * dz
        mob[5, rows, lanes] = az * dx

    def form_tile(q, carry):
        lanes, target = target_tile(q)
        target_sq = target[3] * target[3]

        def form_row(i, inner):
            form(pl.ds(pl.multiple_of(i * 8, 8), 8), lanes, target, target_sq, None)
            return inner
        lax.fori_loop(0, span // 8, form_row, 0, unroll=16)
        return carry
    lax.fori_loop(0, tiles, form_tile, 0)

    lanes, target = target_tile(lax.div(r, 2))
    at_own = lane8 - lax.rem(r, 2) * HALF
    for i in range(HALF // 8):
        same = lax.broadcasted_iota(jnp.int32, (8, LANES), 0) + 8 * i == at_own
        form(
            pl.ds(pl.multiple_of(c * HALF + 8 * i, 8), 8), lanes, target,
            target[3] * target[3], same,
        )

    def unpack_pair(ref, p, axis):
        first = ref[2 * p, kh * axis:kh * (axis + 1), :]
        second = ref[2 * p + 1, kh * axis:kh * (axis + 1), :]
        return jnp.concatenate(
            [jnp.where(low_k, first, swap(second)), jnp.where(low_k, swap(first), second)], axis=0
        )

    arrived(wrow, 14)
    for p in range(tiles):
        cols = slice(p * LANES, (p + 1) * LANES)
        for axis in range(3):
            high, rest = split(unpack_pair(wrow, p, axis))
            w_tgt[axis, 0:vectors, cols] = high
            w_tgt[axis, vectors:2 * vectors, cols] = rest

    width = 4 * HALF
    for step in range(chunks):
        chunk = chunk_at(wcol, 0, step)
        for part in range(2):
            cols = pl.ds(pl.multiple_of(chunk * width + part * LANES, LANES), LANES)
            for axis in range(3):
                high, rest = split(unpack_pair(wcol, 2 * chunk + part, axis))
                for copy in (axis, axis + 3):
                    if copy < 4:
                        base = vectors * copy
                        fields[base:base + vectors, cols] = high
                        fields[4 * vectors + base:4 * vectors + base + vectors, cols] = rest

    def basis_chunk(t, carry):
        lanes = pl.ds(pl.multiple_of(t * width, width), width)
        sums = [None] * 3

        def add(axis, value):
            sums[axis] = value if sums[axis] is None else sums[axis] + value
        for slot, (a, b) in enumerate(PAIRS):
            first = vectors * a
            count = vectors if a == b else 2 * vectors
            by_high = by_rest = None
            for d in range(chunks):
                high, rest = split(mob[slot, d * width:(d + 1) * width, lanes])
                cols = slice(d * width, (d + 1) * width)
                lhs_high = fields[first:first + count, cols]
                lhs_rest = fields[4 * vectors + first:4 * vectors + first + count, cols]
                both = jnp.concatenate([lhs_high, lhs_rest], axis=0)
                dot_high = jnp.dot(both, high, preferred_element_type=F32)
                dot_rest = jnp.dot(lhs_high, rest, preferred_element_type=F32)
                by_high = dot_high if by_high is None else by_high + dot_high
                by_rest = dot_rest if by_rest is None else by_rest + dot_rest
            value = by_high[0:count] + by_high[count:2 * count] + by_rest
            add(b, value[0:vectors])
            if a != b:
                add(a, value[vectors:2 * vectors])
        for axis in range(3):
            p_tgt[axis, :, lanes] = sums[axis]
        return carry
    lax.fori_loop(0, span // width, basis_chunk, 0)

    rhs = [jnp.concatenate([rhs_in[axis:axis + 1, :]] * 2, axis=1) for axis in range(3)]
    row32 = lax.broadcasted_iota(jnp.int32, (vectors, LANES), 0)
    lane32 = lax.broadcasted_iota(jnp.int32, (vectors, LANES), 1)

    gram = None
    load = None
    for axis in range(3):
        high, rest = split(p_tgt[axis])
        along_lanes = (((1,), (1,)), ((), ()))
        by_high = lax.dot_general(w_tgt[axis], high, along_lanes, preferred_element_type=F32)
        by_rest = lax.dot_general(
            w_tgt[axis, 0:vectors, :], rest, along_lanes, preferred_element_type=F32
        )
        term = by_high[0:vectors] + by_high[vectors:2 * vectors] + by_rest
        block = wp[kh * axis:kh * (axis + 1), :]
        block = jnp.where(lane32 < HALF, jnp.concatenate([block, swap(block)], axis=0), 0.0)
        load_term = block * rhs[axis]
        gram = term if gram is None else gram + term
        load = load_term if load is None else load + load_term
    load = jnp.sum(load, axis=1, keepdims=True)
    wide = jnp.concatenate([gram, jnp.zeros((vectors, LANES - vectors), F32)], axis=1)
    groups = vectors // 8
    packed = wide[0:8]
    for g in range(1, groups):
        packed = packed + pltpu.roll(wide[8 * g:8 * g + 8], vectors * g, 1)
    gram_a[0:8, :] = packed
    gram_a[8:9, :] = jnp.sum(jnp.where(lane32 == row32, load, 0.0), axis=0, keepdims=True)
    to_row(lambda peer: gram_a, gram_row, 4)
    gram_row[r] = gram_a[...]

    for q in range(tiles):
        for axis in range(3):
            piece = p_tgt[axis, :, q * LANES:(q + 1) * LANES]
            lower, upper = piece[:kh], piece[kh:]
            slot_rows = slice(kh * axis, kh * (axis + 1))
            aw_send[2 * q, slot_rows, :] = jnp.where(low_k, lower, swap(upper))
            aw_send[2 * q + 1, slot_rows, :] = jnp.where(low_k, swap(lower), upper)
    to_row(lambda peer: aw_send.at[peer], aw_recv, 3)
    aw_recv[r] = aw_send[r]
    arrived(gram_row, 4)
    gram_b[...] = total(gram_row)
    to_col(gram_b, gram_col, 5)
    gram_col[c] = gram_b[...]
    arrived(gram_col, 5)
    both = total(gram_col)
    packed, load_row = both[0:8], both[8:9]
    pieces = [packed]
    for g in range(1, groups):
        pieces.append(pltpu.roll(packed, LANES - vectors * g, 1))
    gram = jnp.concatenate(pieces, axis=0)
    load = jnp.sum(jnp.where(lane32 == row32, load_row, 0.0), axis=1, keepdims=True)

    system = jnp.where(lane32 < vectors, gram, jnp.where(lane32 == row32 + vectors, 1.0, 0.0))
    system = jnp.where(lane32 == 2 * vectors, load, system)
    for j in range(vectors):
        column = jnp.broadcast_to(system[:, j:j + 1], (vectors, LANES))
        scaled_row = system[j:j + 1, :] * (1.0 / column[j:j + 1, :])
        system = jnp.where(row32 == j, scaled_row, system - column * scaled_row)
    inverse = jnp.where(jnp.logical_and(lane32 >= vectors, lane32 < 2 * vectors), system, 0.0)
    coarse = system[:, 2 * vectors:2 * vectors + 1]

    def weights_of(column):
        return jnp.where(low_k, column[:kh], column[kh:])

    def combine(ref, weights):
        out = []
        for axis in range(3):
            s = jnp.sum(ref[kh * axis:kh * (axis + 1), :] * weights, axis=0, keepdims=True)
            out.append(s + swap(s))
        return out

    def solve(vector_row):
        return weights_of(jnp.sum(inverse * vector_row, axis=1, keepdims=True))

    def dots_row(field):
        s = None
        for axis in range(3):
            term = aw[kh * axis:kh * (axis + 1), :] * field[axis]
            s = term if s is None else s + term
        lower = jnp.sum(jnp.where(low_k, s, 0.0), axis=1, keepdims=True)
        upper = jnp.sum(jnp.where(low_k, 0.0, s), axis=1, keepdims=True)
        spots = jnp.where(lane_k == row_k + vectors, lower, 0.0)
        spots = spots + jnp.where(lane_k == row_k + vectors + kh, upper, 0.0)
        return jnp.sum(spots, axis=0, keepdims=True)

    def dot_local(x, y):
        s = x[0] * y[0] + x[1] * y[1] + x[2] * y[2]
        return jnp.sum(jnp.where(low1, s, 0.0), axis=1, keepdims=True)

    def stat(ref, row_value):
        ref[...] = row_value

    def at_lane(index, value):
        return jnp.where(lane1 == index, value, 0.0)

    def put(ref, field, last):
        for axis in range(3):
            ref[axis:axis + 1, :] = field[axis]
        ref[3:4, :] = last

    def product(vec_all, which, send, weigh, forward):
        zero = jnp.zeros((8, LANES), F32)
        sums = [zero] * (3 * tiles)
        half = 3 * tiles // 2
        for step in range(chunks):
            chunk = chunk_at(vec_all, which, step)
            for part in range(2):
                spread(vec_all, 2 * chunk + part, 3, 2 * step + part)
            for part in range(2):
                def one(i, carry, step=step, chunk=chunk, part=part):
                    rows = pl.ds(pl.multiple_of(chunk * width + i * 8, 8), 8)
                    at = pl.ds(pl.multiple_of(step * width + i * 8, 8), 8)
                    value = [src_b[axis, at, :] for axis in range(3)]
                    out = []
                    for q in range(tiles // 2):
                        base = (part * (tiles // 2) + q) * LANES
                        m = [mob[slot, rows, base:base + LANES] for slot in range(6)]
                        for axis in range(3):
                            out.append(
                                carry[3 * q + axis]
                                + (m[SLOT[axis, 0]] * value[0] + m[SLOT[axis, 1]] * value[1])
                                + m[SLOT[axis, 2]] * value[2]
                            )
                    return tuple(out)
                mine_sums = tuple(sums[part * half:(part + 1) * half])
                sums[part * half:(part + 1) * half] = lax.fori_loop(
                    0, width // 8, one, mine_sums, unroll=8
                )
        forward()
        dots = []
        for q in range(tiles):
            for axis in range(3):
                value = jnp.sum(sums[3 * q + axis], axis=0, keepdims=True)
                send[q, axis:axis + 1, :] = value
                if weigh is not None:
                    weight = jnp.where(
                        low1, weigh[2 * q, axis:axis + 1, :], weigh[2 * q + 1, axis:axis + 1, :]
                    )
                    dots.append(value * weight)
        last = jnp.zeros((1, LANES), F32)
        if weigh is not None:
            while len(dots) > 1:
                dots = [sum(dots[i:i + 2]) for i in range(0, len(dots), 2)]
            last = jnp.broadcast_to(jnp.sum(dots[0], axis=1, keepdims=True), (1, LANES))
        for q in range(tiles):
            send[q, 3:4, :] = last

    def mine(recv):
        tile = total(recv)
        odd = lax.rem(r, 2)
        keep = jnp.where(low1, 1 - odd, odd) == 1
        out = []
        for axis in range(3):
            half = jnp.where(keep, tile[axis:axis + 1, :], 0.0)
            out.append(half + swap(half))
        return out, tile[3:4, :]

    arrived(aw_recv, 3)
    aw[...] = total(aw_recv)
    weights = weights_of(coarse)
    image0 = combine(aw, weights)
    r0 = [rhs[axis] - image0[axis] for axis in range(3)]

    put(vec_a, r0, jnp.zeros((1, LANES), F32))
    to_col_chunks(vec_a, vec_col_a, 6, 1)
    vec_col_a[c] = vec_a[...]
    stat(stat_a, dots_row(r0) + at_lane(0, dot_local(r0, r0)))
    to_row(lambda peer: stat_a, stat_row_a, 7)
    stat_row_a[r] = stat_a[...]
    x0 = combine(wp, weights)

    def forward_a():
        arrived(stat_row_a, 7)
        stat_b[...] = total(stat_row_a)
        to_col(stat_b, stat_col_b, 9)
        stat_col_b[c] = stat_b[...]
    product(vec_col_a, 1, part_a, None, forward_a)
    to_row(lambda peer: part_a.at[lax.div(peer, 2)], part_row_a, 8)
    part_row_a[r] = part_a[lax.div(r, 2)]
    arrived(stat_col_b, 9)
    sums0 = total(stat_col_b)[0:1, :]
    norm0 = sums0[:, 0:1]
    weights = solve(sums0)
    shift_image = combine(aw, weights)
    arrived(part_row_a, 8)
    z0, _ = mine(part_row_a)
    q0 = [z0[axis] - shift_image[axis] for axis in range(3)]

    put(vec_c, q0, jnp.zeros((1, LANES), F32))
    to_col_chunks(vec_c, vec_col_c, 10, 2)
    vec_col_c[c] = vec_c[...]
    shift = combine(wp, weights)
    d0 = [r0[axis] - shift[axis] for axis in range(3)]
    put(
        vec_d, q0,
        dots_row(q0) + at_lane(0, dot_local(d0, q0)) + at_lane(1, dot_local(r0, q0))
        + at_lane(2, dot_local(q0, q0)),
    )
    to_row(lambda peer: vec_d, vec_row_c, 11)
    vec_row_c[r] = vec_d[...]

    def forward_c():
        arrived(vec_row_c, 11)
        stat_d[...] = total(vec_row_c)[3:4, :]
        to_col(stat_d, stat_col_d, 13)
        stat_col_d[c] = stat_d[...]
    product(vec_col_c, 2, part_c, vec_row_c, forward_c)
    to_row(lambda peer: part_c.at[lax.div(peer, 2)], part_row_c, 12)
    part_row_c[r] = part_c[lax.div(r, 2)]
    arrived(stat_col_d, 13)
    sums1 = total(stat_col_d)
    step0 = norm0 / sums1[:, 0:1]
    norm1 = norm0 - 2.0 * step0 * sums1[:, 1:2] + step0 * step0 * sums1[:, 2:3]
    beta = norm1 / norm0
    weights = solve(sums0 - step0 * sums1)
    shift = combine(wp, weights)
    shift_image = combine(aw, weights)
    x1 = [x0[axis] + step0 * d0[axis] for axis in range(3)]
    r1 = [r0[axis] - step0 * q0[axis] for axis in range(3)]
    d1 = [r1[axis] + beta * d0[axis] - shift[axis] for axis in range(3)]
    inner = jnp.sum(inverse * sums1, axis=1, keepdims=True)
    column = jnp.sum(jnp.where(lane32 == row32 + vectors, sums1, 0.0), axis=1, keepdims=True)
    removed = jnp.sum(inner * column, axis=0, keepdims=True)
    factor = 1.0 + beta
    fixed = factor * factor * sums1[:, 0:1] - 2.0 * factor * step0 * sums1[:, 2:3]
    arrived(part_row_c, 12)
    y0, block_sum = mine(part_row_c)
    stat_f[...] = block_sum
    to_col(stat_f, stat_col_f, 15)
    stat_col_f[c] = stat_f[...]
    q1 = [
        (z0[axis] - step0 * y0[axis]) + beta * q0[axis] - shift_image[axis] for axis in range(3)
    ]
    arrived(stat_col_f, 15)
    curvature = fixed + step0 * step0 * (total(stat_col_f)[:, 0:1] - removed)
    step1 = norm1 / curvature
    for axis in range(3):
        out_ref[axis:axis + 1, :] = x1[axis] + step1 * d1[axis]
        out_ref[4 + axis:5 + axis, :] = r1[axis] - step1 * q1[axis]

    for tag, dst in enumerate((
        gcol, grow, wcol, aw_recv, gram_row, gram_col, vec_col_a, stat_row_a, part_row_a,
        stat_col_b, vec_col_c, vec_row_c, part_row_c, stat_col_d, wrow, stat_col_f,
    )):
        departed(dst, tag)


def body(n, positions, radii, basis, rhs):
    vectors = basis.shape[0]
    kh = vectors // 2
    span = n * HALF
    row, rows = pltpu.VMEM((1, LANES), F32), pltpu.VMEM((n, 1, LANES), F32)
    tile, tile_slots = pltpu.VMEM((4, LANES), F32), pltpu.VMEM((n, 4, LANES), F32)
    parts = pltpu.VMEM((span // LANES, 4, LANES), F32)
    field, field_slots = pltpu.VMEM((3 * kh, LANES), F32), pltpu.VMEM((n, 3 * kh, LANES), F32)
    two, two_slots = pltpu.VMEM((9, LANES), F32), pltpu.VMEM((n, 9, LANES), F32)
    vmem = pl.BlockSpec(memory_space=pltpu.VMEM)
    anywhere = pl.BlockSpec(memory_space=pl.ANY)
    out = pl.pallas_call(
        functools.partial(kernel, n, vectors),
        out_shape=jax.ShapeDtypeStruct((8, LANES), F32),
        in_specs=[anywhere] * 4,
        out_specs=vmem,
        scratch_shapes=[
            pltpu.VMEM((3, HALF), F32), pltpu.VMEM((1, HALF), F32),
            pltpu.VMEM((3, vectors, HALF), F32), pltpu.VMEM((3, HALF), F32),
            tile, field,
            tile_slots, tile_slots, field_slots, field_slots,
            pltpu.VMEM((4, span, LANES), F32),
            pltpu.VMEM((4, span), F32),
            pltpu.VMEM((6, span, span), F32),
            pltpu.VMEM((8 * vectors, span), BF16),
            pltpu.VMEM((3, 2 * vectors, span), BF16), pltpu.VMEM((3, vectors, span), F32),
            field_slots, field_slots, field,
            two, two_slots, two, two_slots,
            tile, tile_slots, row, rows, parts, tile_slots, row, rows,
            tile, tile, tile_slots, tile_slots, parts, tile_slots, row, rows,
            row, rows,
            pltpu.SemaphoreType.DMA((4,)),
            pltpu.SemaphoreType.DMA((16,)),
            pltpu.SemaphoreType.DMA((16,)),
            pltpu.SemaphoreType.DMA((4, n // 4)),
        ],
        compiler_params=pltpu.CompilerParams(
            collective_id=0, has_side_effects=True, vmem_limit_bytes=60 << 20
        ),
    )(positions, radii[None], basis.transpose(1, 0, 2), rhs)
    return out[0:3, :HALF], out[4:7, :HALF]


def solution(mesh):
    return jax.shard_map(
        functools.partial(body, mesh.shape["row"]),
        mesh=mesh,
        in_specs=(
            P(None, ("row", "col")),
            P(("row", "col")),
            P(None, None, ("row", "col")),
            P(None, ("row", "col")),
        ),
        out_specs=(P(None, ("row", "col")), P(None, ("row", "col"))),
        check_vma=False,
    )
```
